32 devices in a mesh: dp: 16 (over z, y, core), fsdp: 2 (over x).
Axes of the slice: x: 2, y: 2, z: 4, core: 2. Of those that a mesh axis runs over, the one named last changes fastest.
Arguments:
- tokens: bfloat16 [16384, 2048], P(('dp', 'fsdp')), may hold values from -6 to 6
- cotangent: bfloat16 [16384, 2048], P(('dp', 'fsdp')), may hold values from -6 to 6
- lengths: int32 [32], P(('dp', 'fsdp')), may hold values from 128 to 512, as said below
- widths: int32 [32], replicated, may hold values from 1 to 8
- norm_gain: float32 [2048], replicated, may hold values from 0.1 to 1.9
- w_zx: bfloat16 [2048, 2, 4096], P('dp', None, 'fsdp'), may hold values from -0.125 to 0.125
- w_bc: bfloat16 [2048, 256], P('dp'), may hold values from -0.125 to 0.125
- w_dt: bfloat16 [2048, 64], P('dp', 'fsdp'), may hold values from -0.125 to 0.125
- w_out: bfloat16 [4096, 2048], P('fsdp', 'dp'), may hold values from -0.125 to 0.125
- conv_w: float32 [4, 4352], replicated, may hold values from -3 to 3
- conv_b: float32 [4352], replicated, may hold values from -1.5 to 1.5
- dt_bias: float32 [64], replicated, may hold values from -4 to -2
- a_log: float32 [64], replicated, may hold values from -3 to 0.5
- d_skip: float32 [64], replicated, may hold values from 0.5 to 2
- gate_gain: float32 [4096], replicated, may hold values from 0.1 to 1.9
Outputs:
- output: bfloat16 [16384, 2048], P(('dp', 'fsdp'))
- input_grad: bfloat16 [16384, 2048], P(('dp', 'fsdp'))
- g_norm_gain: float32 [2048], replicated
- g_w_zx: float32 [2048, 2, 4096], P('dp', None, 'fsdp')
- g_w_bc: float32 [2048, 256], P('dp')
- g_w_dt: float32 [2048, 64], P('dp', 'fsdp')
- g_w_out: float32 [4096, 2048], P('fsdp', 'dp')
- g_conv_w: float32 [4, 4352], replicated
- g_conv_b: float32 [4352], replicated
- g_dt_bias: float32 [64], replicated
- g_a_log: float32 [64], replicated
- g_d_skip: float32 [64], replicated
- g_gate_gain: float32 [4096], replicated
The draws below stay inside these ranges and needn't reach their ends.
Inputs may be any that keep to these rules, and one draw needn't show every extreme that they name: `lengths`: some sequence fills its whole slot of 512 positions, and some holds exactly 128.
All inputs are finite; a program needn't handle non-finite values.
Results may differ from the reference program's by a relative error of at most 0.018.
Values may be sent and summed in bfloat16 or wider, within the bound.
No kernel may reach another device: no remote copies, remote signals or barrier semaphores. Data moves between devices by JAX's collectives and lax.ppermute only.
A program may use at most 384 MiB of HBM per device.

```python
import jax
import jax.numpy as jnp
from jax import lax

D = 2048
HEADS = 64
HEAD_DIM = 64
STATE = 128
CONV = 4
STRETCH = 256
SLOT = 512
INNER = 4096
SEQS = 32
TOKENS = 16384


def draw_lengths(key, part):
    drawn = jax.random.randint(key, (SEQS,), SLOT // 4, SLOT + 1)
    place = jax.random.randint(jax.random.fold_in(key, 7), (), 0, SEQS)
    other = (place + 1 + jax.random.randint(jax.random.fold_in(key, 11), (), 0, SEQS - 1)) % SEQS
    drawn = drawn.at[other].set(SLOT // 4)
    return drawn.at[place].set(SLOT).astype(jnp.int32)


def plant(array, stream_key, least, top_value):
    longest = array.shape.index(max(array.shape))
    spots = []
    for shift in (0, 1):
        where = [jax.random.randint(jax.random.fold_in(stream_key, axis), (), 0, length) for axis, length in enumerate(array.shape)]
        where[longest] = (where[longest] + shift) % array.shape[longest]
        spots.append(tuple(where))
    return array.at[spots[0]].set(least).at[spots[1]].set(top_value)


def levels(stream_key, shape, pieces, least, top_value):
    loudness, own = 1.0, jax.random.fold_in(stream_key, 6)
    for dim, parts in pieces:
        heights = jnp.exp(jax.random.uniform(jax.random.fold_in(own, dim), (parts,), jnp.float32, least / len(pieces), top_value / len(pieces)))
        loudness = loudness * jnp.repeat(heights, shape[dim] // parts).reshape([-1 if axis == dim else 1 for axis in range(len(shape))])
    return loudness


def centred(own_key, extent, deviation, reach, split=(), held_as=jnp.bfloat16):
    entries = deviation * jax.random.normal(own_key, extent, jnp.float32)
    if split:
        entries = entries * levels(own_key, extent, split, -0.22, 0.18)
    return jnp.clip(entries, -reach, reach).astype(held_as)


def setup_inputs(seed: int = 0) -> dict:
    streams_of = jax.random.split(jax.random.key(seed), 16)
    return {
        "tokens": centred(streams_of[0], (TOKENS, D), 1.0, 6.0, ((0, 32),)),
        "cotangent": centred(streams_of[1], (TOKENS, D), 1.0, 6.0, ((0, 32),)),
        "lengths": draw_lengths(jax.random.fold_in(streams_of[15], 71), 0),
        "widths": plant(jax.random.randint(streams_of[3], (SEQS,), 1, 9), jax.random.fold_in(streams_of[3], 1), 1, 8).astype(jnp.int32),
        "norm_gain": jnp.clip(1.0 + 0.18 * jax.random.normal(streams_of[4], (D,), jnp.float32), 0.1, 1.9),
        "w_zx": centred(streams_of[5], (D, 2, INNER), D ** -0.5, 0.125, ((0, 16), (2, 2))),
        "w_bc": centred(streams_of[6], (D, 2 * STATE), D ** -0.5, 0.125, ((0, 16),)),
        "w_dt": centred(streams_of[7], (D, HEADS), D ** -0.5, 0.125, ((0, 16), (1, 2))),
        "w_out": centred(streams_of[8], (INNER, D), (INNER // 2) ** -0.5, 0.125, ((0, 2), (1, 16))),
        "conv_w": centred(streams_of[9], (CONV, INNER + 2 * STATE), CONV ** -0.5, 3.0, (), jnp.float32),
        "conv_b": centred(streams_of[10], (INNER + 2 * STATE,), 0.3, 1.5, (), jnp.float32),
        "dt_bias": jnp.clip(jax.random.uniform(streams_of[11], (HEADS,), jnp.float32, -4.0, -2.0), -4.0, -2.0),
        "a_log": jnp.clip(jax.random.uniform(streams_of[12], (HEADS,), jnp.float32, -3.0, 0.5), -3.0, 0.5),
        "d_skip": jnp.clip(jax.random.uniform(streams_of[13], (HEADS,), jnp.float32, 0.5, 2.0), 0.5, 2.0),
        "gate_gain": jnp.clip(1.0 + 0.18 * jax.random.normal(streams_of[14], (INNER,), jnp.float32), 0.1, 1.9),
    }


@jax.custom_vjp
def low(v):
    return lax.optimization_barrier(v.astype(jnp.bfloat16)).astype(jnp.float32)

@jax.custom_vjp
def low_back(v):
    return v

def low_keep(v):
    return (low(v), None)

def low_pass(kept, grad):
    return (grad,)

def back_keep(v):
    return (v, None)

def back_low(kept, grad):
    return (low(grad),)
low.defvjp(low_keep, low_pass)
low_back.defvjp(back_keep, back_low)

def matmul(left, right):
    return jnp.dot(left, right, precision=lax.Precision.HIGHEST, preferred_element_type=jnp.float32)

def normed_rows(values, gain):
    return values * lax.rsqrt(lax.optimization_barrier(jnp.mean(values * values, axis=-1, keepdims=True)) + 1e-05) * gain

def block_step(carry, packed):
    state_now, decay_rate = carry
    x_heads, b_mat, c_mat, steps_here = packed
    size = steps_here.shape[0]
    running = jnp.cumsum(-steps_here * decay_rate, axis=0)
    lower = jnp.arange(size)[:, None] >= jnp.arange(size)[None, :]
    spans = running.T[:, :, None] - running.T[:, None, :]
    decay = jnp.exp(jnp.where(lower[None], spans, 0.0)) * lower[None].astype(jnp.float32)
    gram = jnp.dot(c_mat, b_mat.T, precision=lax.Precision.HIGHEST, preferred_element_type=jnp.float32)
    mixing = low(gram[None] * decay * steps_here.T[:, None, :])
    intra = jnp.einsum('hts,hsp->htp', mixing, x_heads, precision=lax.Precision.HIGHEST)
    prior = low(state_now)
    inter = jnp.exp(running.T)[:, :, None] * jnp.einsum('tn,hpn->htp', c_mat, prior, precision=lax.Precision.HIGHEST)
    tail = running[-1]
    factor = jnp.exp(tail[None, :] - running) * steps_here
    weighted = low(x_heads * factor.T[:, :, None])
    new_state = jnp.exp(tail)[:, None, None] * state_now + jnp.einsum('hsp,sn->hpn', weighted, b_mat, precision=lax.Precision.HIGHEST)
    return ((new_state, decay_rate), intra + inter)

def core(z, xr, bc, dtr, params, limit, channel_base, head_base):
    conv_w, conv_b, dt_bias, a_log, d_skip = params
    slot = z.shape[0]
    inner = z.shape[1]
    heads = dtr.shape[1]
    head_dim = inner // heads
    state = bc.shape[1] // 2
    taps = conv_w.shape[0]
    total = conv_w.shape[1]
    tap_w = jnp.concatenate([lax.dynamic_slice_in_dim(conv_w, channel_base, inner, 1), conv_w[:, total - 2 * state:]], axis=1)
    tap_b = jnp.concatenate([lax.dynamic_slice_in_dim(conv_b, channel_base, inner, 0), conv_b[total - 2 * state:]])
    joined = jnp.concatenate([xr, bc], axis=1)
    padded = jnp.pad(joined, ((taps - 1, 0), (0, 0)))
    conv = tap_b + sum((tap_w[k] * padded[k:k + slot] for k in range(taps)))
    act = jax.nn.silu(conv)
    channel = channel_base + jnp.arange(inner).astype(jnp.int32)
    used_mask = (channel < limit).astype(jnp.float32)
    x_used = low(act[:, :inner] * used_mask)
    b_all = low(act[:, inner:inner + state])
    c_all = low(act[:, inner + state:])
    steps = jax.nn.softplus(dtr + lax.dynamic_slice_in_dim(dt_bias, head_base, heads, 0))
    decay_rate = jnp.exp(lax.dynamic_slice_in_dim(a_log, head_base, heads, 0))
    skip = lax.dynamic_slice_in_dim(d_skip, head_base, heads, 0)
    blocks = slot // STRETCH
    x_blocks = x_used.reshape(blocks, STRETCH, heads, head_dim).transpose(0, 2, 1, 3)
    start = (jnp.zeros((heads, head_dim, state), jnp.float32), decay_rate)
    carried, y_blocks = lax.scan(jax.checkpoint(block_step), start, (x_blocks, b_all.reshape(blocks, STRETCH, state), c_all.reshape(blocks, STRETCH, state), steps.reshape(blocks, STRETCH, heads)))
    y = y_blocks.transpose(0, 2, 1, 3).reshape(slot, inner) + x_used * jnp.repeat(skip, head_dim)
    y = low_back(y)
    return y * jax.nn.silu(z)

def layer(u, norm_gain, w_zx, w_bc, w_dt, w_out, conv_w, conv_b, dt_bias, a_log, d_skip, gate_gain, lengths, widths):
    seq_count = lengths.shape[0]
    slot = u.shape[0] // seq_count
    inner = w_out.shape[0]
    width_d = u.shape[1]
    params = (conv_w, conv_b, dt_bias, a_log, d_skip)

    def one(packed):
        useq, width, length = packed
        normed = low(normed_rows(useq, norm_gain))
        zx = low_back(matmul(normed, w_zx.reshape(width_d, 2 * inner)))
        bc = low_back(matmul(normed, w_bc))
        dtr = low_back(matmul(normed, w_dt))
        limit = width * (HEADS // 8) * HEAD_DIM
        gated = core(zx[:, :inner], zx[:, inner:], bc, dtr, params, limit, 0, 0)
        count = limit.astype(jnp.float32)
        gnorm = gated * lax.rsqrt(lax.optimization_barrier(jnp.sum(gated * gated, axis=-1, keepdims=True)) / count + 1e-05) * gate_gain
        branch = matmul(low(gnorm), w_out)
        valid = (jnp.arange(slot) < length).astype(jnp.float32)
        return useq + valid[:, None] * branch
    result = lax.map(jax.checkpoint(one), (u.reshape(seq_count, slot, width_d), widths, lengths))
    return result.reshape(u.shape)

def reference(tokens, cotangent, lengths, widths, norm_gain, w_zx, w_bc, w_dt, w_out, conv_w, conv_b, dt_bias, a_log, d_skip, gate_gain):
    floats = [tokens.astype(jnp.float32), norm_gain, w_zx.astype(jnp.float32), w_bc.astype(jnp.float32), w_dt.astype(jnp.float32), w_out.astype(jnp.float32), conv_w, conv_b, dt_bias, a_log, d_skip, gate_gain]

    def forward(*values):
        return layer(*values, lengths, widths)
    result, pull = jax.vjp(forward, *floats)
    grads = pull(cotangent.astype(jnp.float32))
    return (result.astype(jnp.bfloat16), grads[0].astype(jnp.bfloat16), grads[1], grads[2], grads[3], grads[4], grads[5], grads[6], grads[7], grads[8], grads[9], grads[10], grads[11])
```

```python
import functools

import jax
import jax.numpy as jnp
from jax import lax
from jax.experimental import pallas as pl
from jax.experimental.pallas import tpu as pltpu
from jax.sharding import PartitionSpec as P

HEADS = 64
HEAD_DIM = 64
STRETCH = 256
LANES = 128
F32 = jnp.float32
BF16 = jnp.bfloat16
NEG = -1e30
HIGH = lax.Precision.HIGHEST


def dot_nn(a, b):
    return lax.dot_general(a, b, (((1,), (0,)), ((), ())), preferred_element_type=F32)


def dot_nt(a, b):
    return lax.dot_general(a, b, (((1,), (1,)), ((), ())), preferred_element_type=F32)


def dot_tn(a, b):
    return lax.dot_general(a, b, (((0,), (0,)), ((), ())), preferred_element_type=F32)


class Grid:
    def __init__(self):
        self.dp = lax.axis_size("dp")
        self.n = lax.axis_size("fsdp")
        chips = self.dp // 2
        self.zs = 4 if chips % 4 == 0 else 1
        self.ys = chips // self.zs
        index = lax.axis_index("dp")
        self.core = index % 2
        self.chip = index // 2
        self.z = self.chip // self.ys
        self.y = self.chip % self.ys
        self.j = lax.axis_index("fsdp")
        self.slots = self.zs * self.ys

    def _dp(self, value, move):
        pairs = []
        for i in range(self.dp):
            z, y, c = i // (2 * self.ys), (i // 2) % self.ys, i % 2
            z, y, c = move(z, y, c)
            pairs.append((i, (z * self.ys + y) * 2 + c))
        return lax.ppermute(value, "dp", pairs)

    def swap_core(self, value):
        return self._dp(value, lambda z, y, c: (z, y, 1 - c))

    def send_z(self, value, s):
        return self._dp(value, lambda z, y, c: ((z + s) % self.zs, y, c))

    def send_y(self, value, f):
        return self._dp(value, lambda z, y, c: (z, (y + f) % self.ys, c))

    def send_x(self, value, g):
        pairs = [(i, (i + g) % self.n) for i in range(self.n)]
        return lax.ppermute(value, "fsdp", pairs)

    def slot_chip(self, k):
        f, s = k // self.zs, k % self.zs
        return ((self.z - s) % self.zs) * self.ys + (self.y - f) % self.ys

    def chip_slot(self, b):
        return ((self.y - b % self.ys) % self.ys) * self.zs + (self.z - b // self.ys) % self.zs

    def gather(self, block):
        column = [block] + [self.send_z(block, s) for s in range(1, self.zs)]
        pieces = list(column)
        for f in range(1, self.ys):
            pieces += [self.send_y(piece, f) for piece in column]
        return pieces

    def scatter(self, pieces):
        total = None
        for s in list(range(1, self.zs)) + [0]:
            part = pieces[s].astype(F32)
            for f in range(1, self.ys):
                part = part + self.send_y(pieces[f * self.zs + s], -f).astype(F32)
            if s:
                part = self.send_z(part.astype(BF16), -s).astype(F32)
            total = part if total is None else total + part
        return total


def to_slots(grid, value, axis):
    size = value.shape[axis] // grid.slots
    return jnp.concatenate(
        [
            lax.dynamic_slice_in_dim(value, grid.slot_chip(k) * size, size, axis)
            for k in range(grid.slots)
        ],
        axis=axis,
    )


def from_slots(grid, value, axis):
    size = value.shape[axis] // grid.slots
    return jnp.concatenate(
        [
            lax.dynamic_slice_in_dim(value, grid.chip_slot(b) * size, size, axis)
            for b in range(grid.slots)
        ],
        axis=axis,
    )


def shift_down(value, by):
    if by == 0:
        return value
    rows = lax.broadcasted_iota(jnp.int32, value.shape, 0)
    return jnp.where(rows < by, 0.0, pltpu.roll(value, by, 0))


def shift_up(value, by):
    if by == 0:
        return value
    size = value.shape[0]
    rows = lax.broadcasted_iota(jnp.int32, value.shape, 0)
    return jnp.where(rows >= size - by, 0.0, pltpu.roll(value, size - by, 0))


def convolve(joined, taps, lanes):
    shifted = [shift_down(joined, 3 - k) for k in range(4)]
    total = taps[4:5, lanes]
    for k in range(4):
        total = total + taps[k : k + 1, lanes] * shifted[k]
    return shifted, total


def head_tables(dtr, heads):
    x = dtr + heads[0:1, :]
    dt = jnp.maximum(x, 0.0) + jnp.log1p(jnp.exp(-jnp.abs(x)))
    small = x < -30.0
    log_dt = jnp.where(small, x, jnp.log(dt))
    ratio = jnp.where(small, 1.0, jax.nn.sigmoid(x) / dt)
    rate = -dt * jnp.exp(heads[1:2, :])
    return log_dt, rate, ratio


def triangle(upper):
    rows = lax.broadcasted_iota(jnp.int32, (STRETCH, STRETCH), 0)
    cols = lax.broadcasted_iota(jnp.int32, (STRETCH, STRETCH), 1)
    return jnp.where(cols >= rows if upper else cols <= rows, 1.0, 0.0).astype(F32)


def dot_high(a, b):
    return jnp.dot(a, b, precision=HIGH, preferred_element_type=F32)


def pair_lanes(low, high, width=LANES):
    lane = lax.broadcasted_iota(jnp.int32, (low.shape[0], width), 1)
    return jnp.where(lane < HEAD_DIM, low, high)


def only(value, e):
    lane = lax.broadcasted_iota(jnp.int32, value.shape, 1)
    keep = (lane < HEAD_DIM) if e == 0 else (lane >= HEAD_DIM)
    return jnp.where(keep, value, jnp.zeros_like(value))


def fwd_kernel(limit_ref, xb_ref, taps_ref, heads_ref, skip_ref, y_ref, s1_ref, cm_ref):
    inner = y_ref.shape[1]
    q = pl.program_id(0)
    limit = limit_ref[q]
    half = STRETCH // 2
    lo, hi = slice(0, STRETCH), slice(STRETCH, 2 * STRETCH)
    bc = slice(inner, inner + 2 * LANES)
    _, conv = convolve(xb_ref[:, bc], taps_ref, bc)
    act = jax.nn.silu(conv).astype(BF16)
    bm, cm = act[:, :LANES], act[:, LANES:]
    log_dt, rate, _ = head_tables(xb_ref[:, inner + 2 * LANES :], heads_ref)
    tri = triangle(False)
    cum = jnp.concatenate([dot_high(tri, rate[lo]), dot_high(tri, rate[hi])], 0)
    late = cum - log_dt
    late_t = late.T
    tail = jnp.exp(cum[STRETCH - 1 : STRETCH] - late[lo])
    ecum = jnp.exp(cum[hi])
    grams = [dot_nt(cm[b], bm[b]) for b in (lo, hi)]
    mask = lax.broadcasted_iota(jnp.int32, (half, half), 0) >= lax.broadcasted_iota(
        jnp.int32, (half, half), 1
    )
    for p in range(inner // LANES):
        lanes = slice(p * LANES, (p + 1) * LANES)
        _, conv = convolve(xb_ref[:, lanes], taps_ref, lanes)
        channel = lax.broadcasted_iota(jnp.int32, (1, LANES), 1) + p * LANES
        xs = (jax.nn.silu(conv) * (channel < limit).astype(F32)).astype(BF16)
        h = 2 * p
        weights = pair_lanes(tail[:, h : h + 1], tail[:, h + 1 : h + 2])
        weighted = (xs[lo].astype(F32) * weights).astype(BF16)
        state = dot_tn(weighted, bm[lo]).astype(BF16)
        s1_ref[lanes, :] = state
        for b, gram in zip((lo, hi), grams):
            tops, lows = [], []
            xe = [only(xs[b], e) for e in (0, 1)]
            base = b.start
            for e in (0, 1):
                col = cum[b, h + e : h + e + 1]
                row = late_t[h + e : h + e + 1, b]
                top = jnp.exp(jnp.where(mask, col[:half] - row[:, :half], NEG))
                low0 = jnp.exp(col[half:] - row[:, :half])
                low1 = jnp.exp(jnp.where(mask, col[half:] - row[:, half:], NEG))
                tops.append((gram[:half, :half] * top).astype(BF16))
                lows.append((gram[half:, :half] * low0).astype(BF16))
                lows.append((gram[half:, half:] * low1).astype(BF16))
            y0 = dot_nn(
                jnp.concatenate(tops, 1), jnp.concatenate([xe[0][:half], xe[1][:half]], 0)
            )
            y1 = dot_nn(jnp.concatenate(lows, 1), jnp.concatenate(xe, 0))
            if base:
                inter = dot_nt(cm[b], state)
                inter = inter * pair_lanes(ecum[:, h : h + 1], ecum[:, h + 1 : h + 2])
                y0, y1 = y0 + inter[:half], y1 + inter[half:]
            skip = skip_ref[0:1, lanes] * xs[b].astype(F32)
            y_ref[pl.ds(base, half), lanes] = y0 + skip[:half]
            y_ref[pl.ds(base + half, half), lanes] = y1 + skip[half:]


def lane_sum(value, e):
    return jnp.sum(only(value, e), axis=1, keepdims=True)


def bwd_kernel(
    limit_ref,
    xb_ref,
    y_ref,
    dy_ref,
    s1_ref,
    taps_ref,
    heads_ref,
    skip_ref,
    dxb_ref,
    gch_ref,
    gh_ref,
    dg_ref,
    rs_ref,
):
    inner = y_ref.shape[1]
    q = pl.program_id(0)
    limit = limit_ref[q]
    half = STRETCH // 2
    lo, hi = slice(0, STRETCH), slice(STRETCH, 2 * STRETCH)
    bc = slice(inner, inner + 2 * LANES)

    @pl.when(q == 0)
    def _():
        gch_ref[...] = jnp.zeros_like(gch_ref)
        gh_ref[...] = jnp.zeros_like(gh_ref)

    dg_ref[...] = jnp.zeros_like(dg_ref)
    rs_ref[...] = jnp.zeros_like(rs_ref)
    shifted_bc, conv_bc = convolve(xb_ref[:, bc], taps_ref, bc)
    sig_bc = jax.nn.sigmoid(conv_bc)
    act = (conv_bc * sig_bc).astype(BF16)
    bm, cm = act[:, :LANES], act[:, LANES:]
    log_dt, rate, ratio = head_tables(xb_ref[:, inner + 2 * LANES :], heads_ref)
    tri = triangle(False)
    cum = jnp.concatenate([dot_high(tri, rate[lo]), dot_high(tri, rate[hi])], 0)
    late = cum - log_dt
    cum_t = cum.T
    tail = jnp.exp(cum[STRETCH - 1 : STRETCH] - late[lo])
    ecum = jnp.exp(cum[hi])
    grams = [dot_nt(bm[b], cm[b]) for b in (lo, hi)]
    mask = lax.broadcasted_iota(jnp.int32, (half, half), 1) >= lax.broadcasted_iota(
        jnp.int32, (half, half), 0
    )
    d_bm0 = jnp.zeros((STRETCH, LANES), F32)
    d_cm1 = jnp.zeros((STRETCH, LANES), F32)
    d_tail = jnp.zeros((1, LANES), F32)
    lane_of = lax.broadcasted_iota(jnp.int32, (1, LANES), 1)

    def conv_back(d_act, conv, sig, shifted, lanes):
        d_conv = d_act * (sig * (1.0 + conv * (1.0 - sig)))
        rows = [jnp.sum(d_conv * part, axis=0, keepdims=True) for part in shifted]
        rows.append(jnp.sum(d_conv, axis=0, keepdims=True))
        total = None
        for k in range(4):
            part = taps_ref[k : k + 1, lanes] * shift_up(d_conv, 3 - k)
            total = part if total is None else total + part
        dxb_ref[:, lanes] = total.astype(BF16)
        return rows

    for p in range(inner // LANES):
        lanes = slice(p * LANES, (p + 1) * LANES)
        h = 2 * p
        shifted, conv = convolve(xb_ref[:, lanes], taps_ref, lanes)
        sig = jax.nn.sigmoid(conv)
        channel = lane_of + p * LANES
        used = (channel < limit).astype(F32)
        xs = (conv * sig * used).astype(BF16)
        xf = xs.astype(F32)
        dy = dy_ref[:, lanes]
        dyf = dy.astype(F32)
        skip = skip_ref[0:1, lanes]
        d_prior = (dyf[hi] * pair_lanes(ecum[:, h : h + 1], ecum[:, h + 1 : h + 2])).astype(BF16)
        d_state = dot_tn(d_prior, cm[hi]).astype(BF16)
        weights = pair_lanes(tail[:, h : h + 1], tail[:, h + 1 : h + 2])
        weighted = (xf[lo] * weights).astype(BF16)
        d_from_state = dot_nt(bm[lo], d_state) * weights
        d_bm0 = d_bm0 + dot_nn(weighted, d_state)
        d_cm1 = d_cm1 + dot_nn(d_prior, s1_ref[lanes, :])
        columns = []
        for i, (b, gram) in enumerate(zip((lo, hi), grams)):
            tops, lows = [], []
            dye = [only(dy[b], e) for e in (0, 1)]
            for e in (0, 1):
                col = late[b, h + e : h + e + 1]
                row = cum_t[h + e : h + e + 1, b]
                top0 = jnp.exp(jnp.where(mask, row[:, :half] - col[:half], NEG))
                top1 = jnp.exp(row[:, half:] - col[:half])
                low = jnp.exp(jnp.where(mask, row[:, half:] - col[half:], NEG))
                xe = only(xs[b], e)
                d_top = dot_nt(xe[:half], dy[b])
                d_low = dot_nt(xe[half:], dy[b][half:])
                tops.append((gram[:half, :half] * top0).astype(BF16))
                tops.append((gram[:half, half:] * top1).astype(BF16))
                lows.append((gram[half:, half:] * low).astype(BF16))
                dg_ref[i, :half, :half] += d_top[:, :half] * top0
                dg_ref[i, :half, half:] += d_top[:, half:] * top1
                dg_ref[i, half:, half:] += d_low * low
            d0 = dot_nn(jnp.concatenate(tops, 1), jnp.concatenate(dye, 0))
            d1 = dot_nn(
                jnp.concatenate(lows, 1), jnp.concatenate([dye[0][half:], dye[1][half:]], 0)
            )
            columns += [d0, d1]
        d_x = jnp.concatenate(columns, 0)
        d_x = jnp.concatenate([d_x[lo] + d_from_state, d_x[hi]], 0)
        from_x = xf * d_x
        from_y = dyf * (y_ref[:, lanes] - skip * xf)
        state_sum = jnp.sum(xf[lo] * d_from_state, axis=0, keepdims=True)
        for e in (0, 1):
            here = lane_of == h + e
            rs_ref[0] = jnp.where(here, lane_sum(from_x, e), rs_ref[0])
            rs_ref[1] = jnp.where(here, lane_sum(from_y, e), rs_ref[1])
            d_tail = jnp.where(here, lane_sum(state_sum, e), d_tail)
        d_act = (d_x + skip * dyf) * used
        rows = conv_back(d_act, conv, sig, shifted, lanes)
        rows.append(jnp.sum(dyf * xf, axis=0, keepdims=True))
        for r, row in enumerate(rows):
            gch_ref[r : r + 1, lanes] += row

    d_bm, d_cm = [], []
    for i, b in enumerate((lo, hi)):
        d_gram = dg_ref[i].astype(BF16)
        d_bm.append(dot_nn(d_gram, cm[b]))
        d_cm.append(dot_tn(d_gram, bm[b]))
    d_bm[0] = d_bm[0] + d_bm0
    d_cm[1] = d_cm[1] + d_cm1
    d_act = jnp.concatenate([jnp.concatenate(d_bm, 0), jnp.concatenate(d_cm, 0)], 1)
    rows = conv_back(d_act, conv_bc, sig_bc, shifted_bc, bc)
    for r, row in enumerate(rows):
        gch_ref[r : r + 1, bc] += row

    from_x, from_y = rs_ref[0], rs_ref[1]
    d_cum = from_y - from_x
    row_of = lax.broadcasted_iota(jnp.int32, (STRETCH, 1), 0)
    first = d_cum[lo] + jnp.where(row_of == STRETCH - 1, d_tail, 0.0)
    tri_t = triangle(True)
    d_rate = jnp.concatenate([dot_high(tri_t, first), dot_high(tri_t, d_cum[hi])], 0)
    flow = rate * d_rate
    d_dt = (from_x + flow) * ratio
    dxb_ref[:, inner + 2 * LANES :] = d_dt.astype(BF16)
    gh_ref[0:1, :] += jnp.sum(d_dt, axis=0, keepdims=True)
    gh_ref[1:2, :] += jnp.sum(flow, axis=0, keepdims=True)


def run_fwd(limits, xb, taps, heads, skip, slot):
    rows, cols = xb.shape
    inner = cols - 3 * LANES
    seqs = rows // slot
    whole = lambda shape: pl.BlockSpec(shape, lambda q, *_: (0,) * len(shape))
    per = lambda width: pl.BlockSpec((slot, width), lambda q, *_: (q, 0))
    return pl.pallas_call(
        fwd_kernel,
        grid_spec=pltpu.PrefetchScalarGridSpec(
            num_scalar_prefetch=1,
            grid=(seqs,),
            in_specs=[per(cols), whole(taps.shape), whole(heads.shape), whole(skip.shape)],
            out_specs=[
                per(inner),
                pl.BlockSpec((inner, LANES), lambda q, *_: (q, 0)),
            ],
            scratch_shapes=[pltpu.VMEM((8, LANES), F32)],
        ),
        out_shape=[
            jax.ShapeDtypeStruct((rows, inner), F32),
            jax.ShapeDtypeStruct((seqs * inner, LANES), BF16),
        ],
        name="scan_forward",
    )(limits, xb, taps, heads, skip)


def run_bwd(limits, xb, y, dy, s1, taps, heads, skip, slot):
    rows, cols = xb.shape
    inner = cols - 3 * LANES
    seqs = rows // slot
    whole = lambda shape: pl.BlockSpec(shape, lambda q, *_: (0,) * len(shape))
    per = lambda width: pl.BlockSpec((slot, width), lambda q, *_: (q, 0))
    return pl.pallas_call(
        bwd_kernel,
        grid_spec=pltpu.PrefetchScalarGridSpec(
            num_scalar_prefetch=1,
            grid=(seqs,),
            in_specs=[
                per(cols),
                per(inner),
                per(inner),
                pl.BlockSpec((inner, LANES), lambda q, *_: (q, 0)),
                whole(taps.shape),
                whole(heads.shape),
                whole(skip.shape),
            ],
            out_specs=[per(cols), whole((8, cols)), whole((8, LANES))],
            scratch_shapes=[
                pltpu.VMEM((2, STRETCH, STRETCH), F32),
                pltpu.VMEM((2, 2 * STRETCH, LANES), F32),
            ],
        ),
        out_shape=[
            jax.ShapeDtypeStruct((rows, cols), BF16),
            jax.ShapeDtypeStruct((8, cols), F32),
            jax.ShapeDtypeStruct((8, LANES), F32),
        ],
        name="scan_backward",
    )(limits, xb, y, dy, s1, taps, heads, skip)


def per_device(
    tokens,
    cotangent,
    lengths,
    widths,
    norm_gain,
    w_zx,
    w_bc,
    w_dt,
    w_out,
    conv_w,
    conv_b,
    dt_bias,
    a_log,
    d_skip,
    gate_gain,
):
    grid = Grid()
    core, j, n = grid.core, grid.j, grid.n
    slot, width = tokens.shape
    assert lengths.shape[0] == 1 and slot == 2 * STRETCH
    rows_d = w_zx.shape[0]
    inner = w_zx.shape[2] // 2
    heads = w_dt.shape[1] // 2
    state2 = w_bc.shape[1]
    total = conv_w.shape[1]
    all_inner = total - state2
    part = j * 2 + core
    channel_base = part * inner
    head_base = part * heads
    cols = inner + 3 * LANES
    sent = inner + state2 + heads

    def halves(value, axis):
        size = value.shape[axis] // 2
        mine = lax.dynamic_slice_in_dim(value, core * size, size, axis)
        other = lax.dynamic_slice_in_dim(value, (1 - core) * size, size, axis)
        return mine, other

    def by_core(mine, other, axis):
        first = jnp.where(core == 0, mine, other)
        second = jnp.where(core == 0, other, mine)
        return jnp.concatenate([first, second], axis=axis)

    z_mine, z_other = halves(w_zx[:, 0], 1)
    x_mine, x_other = halves(w_zx[:, 1], 1)
    t_mine, t_other = halves(w_dt, 1)
    o_mine, o_other = halves(w_out.T, 1)
    x_mine = jnp.concatenate([x_mine, w_bc, t_mine], axis=1)
    x_other = jnp.concatenate([x_other, w_bc, t_other], axis=1)
    block_o = by_core(o_mine, grid.swap_core(o_other), 0)
    block_x = by_core(x_mine, grid.swap_core(x_other), 0)
    block_z = by_core(z_mine, grid.swap_core(z_other), 0)
    w_o = jnp.concatenate(grid.gather(block_o), axis=0)
    w_x = jnp.concatenate(grid.gather(block_x), axis=0)
    w_z = jnp.concatenate(grid.gather(block_z), axis=0)
    w_x = jnp.pad(w_x, ((0, 0), (0, cols - sent)))

    u = to_slots(grid, tokens, 1).astype(F32)
    cot = to_slots(grid, cotangent, 1)
    gain = to_slots(grid, norm_gain, 0)
    rstd = lax.rsqrt(jnp.mean(u * u, axis=-1, keepdims=True) + 1e-05)
    normed_own = (u * rstd * gain).astype(BF16)
    valid = (jnp.arange(slot) < lengths[0])[:, None]
    d_branch_own = jnp.where(valid, cot, jnp.zeros_like(cot))

    def share(value):
        near = [value] + [grid.send_x(value, g) for g in range(1, n)]
        pieces = []
        for piece in near:
            pieces += [piece, grid.swap_core(piece)]
        return jnp.concatenate(pieces, axis=0)

    def collect(value):
        value = value.reshape(n, 2, slot, width)
        here = value[:, 0].astype(F32) + grid.swap_core(value[:, 1]).astype(F32)
        out = here[0]
        for g in range(1, n):
            out = out + grid.send_x(here[g].astype(BF16), -g).astype(F32)
        return out

    normed = share(normed_own)
    d_branch = share(d_branch_own)
    index = lax.axis_index("dp")
    owners = []
    for g in range(n):
        for e in (0, 1):
            owners.append((index + e * (1 - 2 * core)) * n + (j - g) % n)
    seqs = len(owners)
    seq_width = jnp.stack([widths[o] for o in owners])
    used = seq_width * ((HEADS // 8) * HEAD_DIM)
    counts = jnp.repeat(used.astype(F32), slot)
    limits = jnp.clip(used - channel_base, 0, inner).astype(jnp.int32)

    taps = jnp.concatenate(
        [
            lax.dynamic_slice_in_dim(conv_w, channel_base, inner, 1),
            conv_w[:, all_inner:],
        ],
        axis=1,
    )
    bias = jnp.concatenate(
        [lax.dynamic_slice_in_dim(conv_b, channel_base, inner, 0), conv_b[all_inner:]]
    )
    taps = jnp.pad(jnp.concatenate([taps, bias[None]], 0), ((0, 3), (0, LANES)))
    own_heads = lambda v: lax.dynamic_slice_in_dim(v, head_base, heads, 0)
    head_rows = jnp.pad(
        jnp.stack([own_heads(dt_bias), own_heads(a_log)]), ((0, 6), (0, LANES - heads))
    )
    skip = jnp.broadcast_to(jnp.repeat(own_heads(d_skip), HEAD_DIM)[None], (8, inner))
    own_gain = lax.dynamic_slice_in_dim(gate_gain, channel_base, inner, 0)

    d_gnorm = dot_nn(d_branch, w_o)
    xb = dot_nn(normed, w_x)
    y, s1 = run_fwd(limits, xb, taps, head_rows, skip, slot)
    z = dot_nn(normed, w_z)
    sig = jax.nn.sigmoid(z)
    gated = y * (z * sig)
    weighted = d_gnorm * own_gain
    stats = jnp.stack([jnp.sum(gated * gated, axis=1), jnp.sum(weighted * gated, axis=1)])
    stats = stats.reshape(2, n, 2, slot)
    stats = stats + grid.swap_core(stats)[:, :, ::-1]
    whole = stats
    for g in range(1, n):
        whole = whole + jnp.roll(grid.send_x(stats, g), g, axis=1)
    stats = whole.reshape(2, seqs * slot)
    scale = lax.rsqrt(stats[0] / counts + 1e-05)
    pull = scale * scale * scale / counts * stats[1]
    gnorm = (gated * scale[:, None] * own_gain).astype(BF16)
    d_gated = weighted * scale[:, None] - gated * pull[:, None]
    g_gate = jnp.sum(d_gnorm * gated * scale[:, None], axis=0)
    silu = z * sig
    d_y = (d_gated * silu).astype(BF16)
    d_z = (d_gated * y * (sig * (1.0 + z * (1.0 - sig)))).astype(BF16)

    def reduce(grad):
        return grid.scatter(jnp.split(grad.astype(BF16), grid.slots, axis=0))

    g_o = reduce(dot_tn(d_branch, gnorm))
    g_z = reduce(dot_tn(normed, d_z))
    branch = collect(dot_nt(gnorm, w_o).astype(BF16))
    d_xb, g_channels, g_heads = run_bwd(limits, xb, y, d_y, s1, taps, head_rows, skip, slot)
    g_x = reduce(dot_tn(normed, d_xb)[:, :sent])
    d_normed_part = dot_nt(d_z, w_z) + dot_nt(d_xb, w_x)
    g_norm_part = jnp.sum(d_normed_part * normed.astype(F32), axis=0) / gain
    d_normed = collect(d_normed_part.astype(BF16))

    output = (u + jnp.where(valid, branch, 0.0)).astype(BF16)
    d_scaled = d_normed * gain
    back = jnp.mean(d_scaled * u, axis=-1, keepdims=True)
    d_u = d_scaled * rstd - u * (rstd * rstd * rstd * back)
    input_grad = (cot.astype(F32) + d_u).astype(BF16)
    output = from_slots(grid, output, 1)
    input_grad = from_slots(grid, input_grad, 1)

    def to_rows(value):
        mine = lax.dynamic_slice_in_dim(value, core * rows_d, rows_d, 0)
        other = lax.dynamic_slice_in_dim(value, (1 - core) * rows_d, rows_d, 0)
        return mine, grid.swap_core(other)

    z_rows = by_core(*to_rows(g_z), 1)
    o_rows = by_core(*to_rows(g_o), 1)
    x_mine, x_recv = to_rows(g_x)
    x_rows = by_core(x_mine[:, :inner], x_recv[:, :inner], 1)
    t_rows = by_core(x_mine[:, inner + state2 :], x_recv[:, inner + state2 :], 1)
    bc_rows = (x_mine + x_recv)[:, inner : inner + state2]
    bc_sum = bc_rows
    for g in range(1, n):
        bc_sum = bc_sum + grid.send_x(bc_rows, g)
    g_w_zx = jnp.stack([z_rows, x_rows], axis=1)

    conv_rows = jnp.zeros((5, total), F32)
    conv_rows = lax.dynamic_update_slice(conv_rows, g_channels[:5, :inner], (0, channel_base))
    conv_rows = lax.dynamic_update_slice(
        conv_rows, g_channels[:5, inner : inner + state2], (0, all_inner)
    )
    gate_row = lax.dynamic_update_slice(jnp.zeros((all_inner,), F32), g_gate, (channel_base,))
    g_skip = g_channels[5, :inner].reshape(heads, HEAD_DIM).sum(axis=1)
    head_parts = jnp.stack([g_heads[0, :heads], g_heads[1, :heads], g_skip])
    head_parts = lax.dynamic_update_slice(
        jnp.zeros((3, d_skip.shape[0]), F32), head_parts, (0, head_base)
    )
    flat = jnp.concatenate(
        [
            from_slots(grid, g_norm_part, 0),
            conv_rows.reshape(-1),
            gate_row,
            head_parts.reshape(-1),
        ]
    )
    size = flat.shape[0]
    flat = jnp.pad(flat, (0, -size % 1024)).reshape(-1, LANES)
    flat = lax.psum(flat, ("dp", "fsdp")).reshape(-1)[:size]
    ends = [width, width + 5 * total, width + 5 * total + all_inner]
    g_norm, g_conv, g_gate, g_small = jnp.split(flat, ends)
    g_conv = g_conv.reshape(5, total)
    g_small = g_small.reshape(3, -1)
    return (
        output,
        input_grad,
        g_norm,
        g_w_zx,
        bc_sum,
        t_rows,
        o_rows.T,
        g_conv[:4],
        g_conv[4],
        g_small[0],
        g_small[1],
        g_small[2],
        g_gate,
    )


def solution(mesh):
    in_specs = (
        P(("dp", "fsdp"), None),
        P(("dp", "fsdp"), None),
        P(("dp", "fsdp")),
        P(),
        P(),
        P("dp", None, "fsdp"),
        P("dp", None),
        P("dp", "fsdp"),
        P("fsdp", "dp"),
        P(),
        P(),
        P(),
        P(),
        P(),
        P(),
    )
    out_specs = (
        P(("dp", "fsdp"), None),
        P(("dp", "fsdp"), None),
        P(),
        P("dp", None, "fsdp"),
        P("dp", None),
        P("dp", "fsdp"),
        P("fsdp", "dp"),
        P(),
        P(),
        P(),
        P(),
        P(),
        P(),
    )
    return jax.shard_map(
        per_device, mesh=mesh, in_specs=in_specs, out_specs=out_specs, check_vma=False
    )
```

```python
import functools

import jax
import jax.numpy as jnp
from jax import lax
from jax.experimental import pallas as pl
from jax.experimental.pallas import tpu as pltpu
from jax.sharding import PartitionSpec as P

HEADS = 64
HEAD_DIM = 64
STRETCH = 256
LANES = 128
F32 = jnp.float32
BF16 = jnp.bfloat16
NEG = -1e30
HIGH = lax.Precision.HIGHEST


def dot_nn(a, b):
    return lax.dot_general(a, b, (((1,), (0,)), ((), ())), preferred_element_type=F32)


def dot_nt(a, b):
    return lax.dot_general(a, b, (((1,), (1,)), ((), ())), preferred_element_type=F32)


def dot_tn(a, b):
    return lax.dot_general(a, b, (((0,), (0,)), ((), ())), preferred_element_type=F32)


class Grid:
    def __init__(self):
        self.dp = lax.axis_size("dp")
        self.n = lax.axis_size("fsdp")
        chips = self.dp // 2
        self.zs = 4 if chips % 4 == 0 else 1
        self.ys = chips // self.zs
        index = lax.axis_index("dp")
        self.core = index % 2
        self.chip = index // 2
        self.z = self.chip // self.ys
        self.y = self.chip % self.ys
        self.j = lax.axis_index("fsdp")
        self.slots = self.zs * self.ys

    def _dp(self, value, move):
        pairs = []
        for i in range(self.dp):
            z, y, c = i // (2 * self.ys), (i // 2) % self.ys, i % 2
            z, y, c = move(z, y, c)
            pairs.append((i, (z * self.ys + y) * 2 + c))
        return lax.ppermute(value, "dp", pairs)

    def swap_core(self, value):
        return self._dp(value, lambda z, y, c: (z, y, 1 - c))

    def send_z(self, value, s):
        return self._dp(value, lambda z, y, c: ((z + s) % self.zs, y, c))

    def send_y(self, value, f):
        return self._dp(value, lambda z, y, c: (z, (y + f) % self.ys, c))

    def send_x(self, value, g):
        pairs = [(i, (i + g) % self.n) for i in range(self.n)]
        return lax.ppermute(value, "fsdp", pairs)

    def slot_chip(self, k):
        f, s = k // self.zs, k % self.zs
        return ((self.z - s) % self.zs) * self.ys + (self.y - f) % self.ys

    def all_sum(self, value, axis, bits):
        for bit in bits:
            size = self.dp if axis == "dp" else self.n
            value = value + lax.ppermute(value, axis, [(i, i ^ bit) for i in range(size)])
        return value

    def dp_bits(self):
        return [1 << i for i in range(1, self.dp.bit_length() - 1)]

    def fsdp_bits(self):
        return [1 << i for i in range(self.n.bit_length() - 1)]


def gather_blocks(grid, block):
    rows = block.shape[0]
    out = jnp.zeros((grid.slots * rows,) + block.shape[1:], block.dtype)
    piece = block
    for s in range(grid.zs):
        moved = grid.send_z(piece, 1) if s + 1 < grid.zs else None
        for f in range(grid.ys):
            here = grid.send_y(piece, f) if f else piece
            out = lax.dynamic_update_slice_in_dim(
                out, here, grid.slot_chip(f * grid.zs + s) * rows, 0
            )
        piece = moved
    return out


def scatter_blocks(grid, value):
    rows = value.shape[0] // grid.slots
    total = None
    for s in range(grid.zs - 1, -1, -1):
        piece = lambda f: lax.dynamic_slice_in_dim(
            value, grid.slot_chip(f * grid.zs + s) * rows, rows, 0
        )
        part = piece(0).astype(F32)
        for f in range(1, grid.ys):
            part = part + grid.send_y(piece(f), -f).astype(F32)
        if total is not None:
            part = part + grid.send_z(total.astype(BF16), -1).astype(F32)
        total = part
    return total


def core_groups(grid):
    return [list(range(c, grid.dp, 2)) for c in (0, 1)]


def gather_all(grid, block):
    return lax.all_gather(block, "dp", axis=0, tiled=True, axis_index_groups=core_groups(grid))


def scatter_all(grid, value):
    return lax.psum_scatter(
        value, "dp", scatter_dimension=0, tiled=True, axis_index_groups=core_groups(grid)
    ).astype(F32)


def shift_down(value, by):
    if by == 0:
        return value
    rows = lax.broadcasted_iota(jnp.int32, value.shape, 0)
    return jnp.where(rows < by, 0.0, pltpu.roll(value, by, 0))


def shift_up(value, by):
    if by == 0:
        return value
    size = value.shape[0]
    rows = lax.broadcasted_iota(jnp.int32, value.shape, 0)
    return jnp.where(rows >= size - by, 0.0, pltpu.roll(value, size - by, 0))


def convolve(joined, taps, lanes):
    shifted = [shift_down(joined, 3 - k) for k in range(4)]
    total = taps[4:5, lanes]
    for k in range(4):
        total = total + taps[k : k + 1, lanes] * shifted[k]
    return shifted, total


def head_tables(dtr, heads):
    x = dtr + heads[0:1, :]
    dt = jnp.maximum(x, 0.0) + jnp.log1p(jnp.exp(-jnp.abs(x)))
    small = x < -30.0
    log_dt = jnp.where(small, x, jnp.log(dt))
    ratio = jnp.where(small, 1.0, jax.nn.sigmoid(x) / dt)
    rate = -dt * jnp.exp(heads[1:2, :])
    return log_dt, rate, ratio


def triangle(upper):
    rows = lax.broadcasted_iota(jnp.int32, (STRETCH, STRETCH), 0)
    cols = lax.broadcasted_iota(jnp.int32, (STRETCH, STRETCH), 1)
    return jnp.where(cols >= rows if upper else cols <= rows, 1.0, 0.0).astype(F32)


def dot_high(a, b):
    return jnp.dot(a, b, precision=HIGH, preferred_element_type=F32)


def pair_lanes(low, high, width=LANES):
    lane = lax.broadcasted_iota(jnp.int32, (low.shape[0], width), 1)
    return jnp.where(lane < HEAD_DIM, low, high)


def only(value, e):
    lane = lax.broadcasted_iota(jnp.int32, value.shape, 1)
    keep = (lane < HEAD_DIM) if e == 0 else (lane >= HEAD_DIM)
    return jnp.where(keep, value, jnp.zeros_like(value))


def fwd_kernel(waits, limit_ref, xb_ref, taps_ref, heads_ref, skip_ref, *refs):
    y_ref, s1_ref = refs[waits:]
    inner = y_ref.shape[1]
    limit = limit_ref[pl.program_id(0)]
    half = STRETCH // 2
    lo, hi = slice(0, STRETCH), slice(STRETCH, 2 * STRETCH)
    bc = slice(inner, inner + 2 * LANES)
    _, conv = convolve(xb_ref[:, bc], taps_ref, bc)
    act = jax.nn.silu(conv).astype(BF16)
    bm, cm = act[:, :LANES], act[:, LANES:]
    log_dt, rate, _ = head_tables(xb_ref[:, inner + 2 * LANES :], heads_ref)
    tri = triangle(False)
    cum = jnp.concatenate([dot_high(tri, rate[lo]), dot_high(tri, rate[hi])], 0)
    late = cum - log_dt
    late_t = late.T
    tail = jnp.exp(cum[STRETCH - 1 : STRETCH] - late[lo])
    ecum = jnp.exp(cum[hi])
    grams = [dot_nt(cm[b], bm[b]) for b in (lo, hi)]
    mask = lax.broadcasted_iota(jnp.int32, (half, half), 0) >= lax.broadcasted_iota(
        jnp.int32, (half, half), 1
    )
    for p in range(inner // LANES):
        lanes = slice(p * LANES, (p + 1) * LANES)
        _, conv = convolve(xb_ref[:, lanes], taps_ref, lanes)
        channel = lax.broadcasted_iota(jnp.int32, (1, LANES), 1) + p * LANES
        xs = (jax.nn.silu(conv) * (channel < limit).astype(F32)).astype(BF16)
        h = 2 * p
        weights = pair_lanes(tail[:, h : h + 1], tail[:, h + 1 : h + 2])
        weighted = (xs[lo].astype(F32) * weights).astype(BF16)
        state = dot_tn(weighted, bm[lo]).astype(BF16)
        s1_ref[lanes, :] = state
        for b, gram in zip((lo, hi), grams):
            tops, lows = [], []
            xe = [only(xs[b], e) for e in (0, 1)]
            base = b.start
            for e in (0, 1):
                col = cum[b, h + e : h + e + 1]
                row = late_t[h + e : h + e + 1, b]
                top = jnp.exp(jnp.where(mask, col[:half] - row[:, :half], NEG))
                low0 = jnp.exp(col[half:] - row[:, :half])
                low1 = jnp.exp(jnp.where(mask, col[half:] - row[:, half:], NEG))
                tops.append((gram[:half, :half] * top).astype(BF16))
                lows.append((gram[half:, :half] * low0).astype(BF16))
                lows.append((gram[half:, half:] * low1).astype(BF16))
            y0 = dot_nn(
                jnp.concatenate(tops, 1), jnp.concatenate([xe[0][:half], xe[1][:half]], 0)
            )
            y1 = dot_nn(jnp.concatenate(lows, 1), jnp.concatenate(xe, 0))
            if base:
                inter = dot_nt(cm[b], state)
                inter = inter * pair_lanes(ecum[:, h : h + 1], ecum[:, h + 1 : h + 2])
                y0, y1 = y0 + inter[:half], y1 + inter[half:]
            skip = skip_ref[0:1, lanes] * xs[b].astype(F32)
            y_ref[pl.ds(base, half), lanes] = y0 + skip[:half]
            y_ref[pl.ds(base + half, half), lanes] = y1 + skip[half:]


def lane_sum(value, e):
    return jnp.sum(only(value, e), axis=1, keepdims=True)


def bwd_kernel(first, extra, limit_ref, xb_ref, y_ref, dy_ref, s1_ref, taps_ref, *refs):
    heads_ref, skip_ref = refs[:2]
    dxb_ref, gch_ref, gh_ref, dg_ref, rs_ref = refs[2 + extra :]
    inner = y_ref.shape[1]
    q = pl.program_id(0)
    limit = limit_ref[q + first]
    half = STRETCH // 2
    lo, hi = slice(0, STRETCH), slice(STRETCH, 2 * STRETCH)
    bc = slice(inner, inner + 2 * LANES)

    @pl.when(q == 0)
    def _():
        gch_ref[...] = jnp.zeros_like(gch_ref)
        gh_ref[...] = jnp.zeros_like(gh_ref)

    dg_ref[...] = jnp.zeros_like(dg_ref)
    rs_ref[...] = jnp.zeros_like(rs_ref)
    shifted_bc, conv_bc = convolve(xb_ref[:, bc], taps_ref, bc)
    sig_bc = jax.nn.sigmoid(conv_bc)
    act = (conv_bc * sig_bc).astype(BF16)
    bm, cm = act[:, :LANES], act[:, LANES:]
    log_dt, rate, ratio = head_tables(xb_ref[:, inner + 2 * LANES :], heads_ref)
    tri = triangle(False)
    cum = jnp.concatenate([dot_high(tri, rate[lo]), dot_high(tri, rate[hi])], 0)
    late = cum - log_dt
    cum_t = cum.T
    tail = jnp.exp(cum[STRETCH - 1 : STRETCH] - late[lo])
    ecum = jnp.exp(cum[hi])
    grams = [dot_nt(bm[b], cm[b]) for b in (lo, hi)]
    mask = lax.broadcasted_iota(jnp.int32, (half, half), 1) >= lax.broadcasted_iota(
        jnp.int32, (half, half), 0
    )
    d_bm0 = jnp.zeros((STRETCH, LANES), F32)
    d_cm1 = jnp.zeros((STRETCH, LANES), F32)
    d_tail = jnp.zeros((1, LANES), F32)
    lane_of = lax.broadcasted_iota(jnp.int32, (1, LANES), 1)

    def conv_back(d_act, conv, sig, shifted, lanes):
        d_conv = d_act * (sig * (1.0 + conv * (1.0 - sig)))
        rows = [jnp.sum(d_conv * part, axis=0, keepdims=True) for part in shifted]
        rows.append(jnp.sum(d_conv, axis=0, keepdims=True))
        total = None
        for k in range(4):
            part = taps_ref[k : k + 1, lanes] * shift_up(d_conv, 3 - k)
            total = part if total is None else total + part
        dxb_ref[:, lanes] = total.astype(BF16)
        return rows

    for p in range(inner // LANES):
        lanes = slice(p * LANES, (p + 1) * LANES)
        h = 2 * p
        shifted, conv = convolve(xb_ref[:, lanes], taps_ref, lanes)
        sig = jax.nn.sigmoid(conv)
        channel = lane_of + p * LANES
        used = (channel < limit).astype(F32)
        xs = (conv * sig * used).astype(BF16)
        xf = xs.astype(F32)
        dy = dy_ref[:, lanes]
        dyf = dy.astype(F32)
        skip = skip_ref[0:1, lanes]
        d_prior = (dyf[hi] * pair_lanes(ecum[:, h : h + 1], ecum[:, h + 1 : h + 2])).astype(BF16)
        d_state = dot_tn(d_prior, cm[hi]).astype(BF16)
        weights = pair_lanes(tail[:, h : h + 1], tail[:, h + 1 : h + 2])
        weighted = (xf[lo] * weights).astype(BF16)
        d_from_state = dot_nt(bm[lo], d_state) * weights
        d_bm0 = d_bm0 + dot_nn(weighted, d_state)
        d_cm1 = d_cm1 + dot_nn(d_prior, s1_ref[lanes, :])
        columns = []
        for i, (b, gram) in enumerate(zip((lo, hi), grams)):
            tops, lows = [], []
            dye = [only(dy[b], e) for e in (0, 1)]
            for e in (0, 1):
                col = late[b, h + e : h + e + 1]
                row = cum_t[h + e : h + e + 1, b]
                top0 = jnp.exp(jnp.where(mask, row[:, :half] - col[:half], NEG))
                top1 = jnp.exp(row[:, half:] - col[:half])
                low = jnp.exp(jnp.where(mask, row[:, half:] - col[half:], NEG))
                xe = only(xs[b], e)
                d_top = dot_nt(xe[:half], dy[b])
                d_low = dot_nt(xe[half:], dy[b][half:])
                tops.append((gram[:half, :half] * top0).astype(BF16))
                tops.append((gram[:half, half:] * top1).astype(BF16))
                lows.append((gram[half:, half:] * low).astype(BF16))
                dg_ref[i, :half, :half] += d_top[:, :half] * top0
                dg_ref[i, :half, half:] += d_top[:, half:] * top1
                dg_ref[i, half:, half:] += d_low * low
            d0 = dot_nn(jnp.concatenate(tops, 1), jnp.concatenate(dye, 0))
            d1 = dot_nn(
                jnp.concatenate(lows, 1), jnp.concatenate([dye[0][half:], dye[1][half:]], 0)
            )
            columns += [d0, d1]
        d_x = jnp.concatenate(columns, 0)
        d_x = jnp.concatenate([d_x[lo] + d_from_state, d_x[hi]], 0)
        from_x = xf * d_x
        from_y = dyf * (y_ref[:, lanes] - skip * xf)
        state_sum = jnp.sum(xf[lo] * d_from_state, axis=0, keepdims=True)
        for e in (0, 1):
            here = lane_of == h + e
            rs_ref[0] = jnp.where(here, lane_sum(from_x, e), rs_ref[0])
            rs_ref[1] = jnp.where(here, lane_sum(from_y, e), rs_ref[1])
            d_tail = jnp.where(here, lane_sum(state_sum, e), d_tail)
        d_act = (d_x + skip * dyf) * used
        rows = conv_back(d_act, conv, sig, shifted, lanes)
        rows.append(jnp.sum(dyf * xf, axis=0, keepdims=True))
        for r, row in enumerate(rows):
            gch_ref[r : r + 1, lanes] += row

    d_bm, d_cm = [], []
    for i, b in enumerate((lo, hi)):
        d_gram = dg_ref[i].astype(BF16)
        d_bm.append(dot_nn(d_gram, cm[b]))
        d_cm.append(dot_tn(d_gram, bm[b]))
    d_bm[0] = d_bm[0] + d_bm0
    d_cm[1] = d_cm[1] + d_cm1
    d_act = jnp.concatenate([jnp.concatenate(d_bm, 0), jnp.concatenate(d_cm, 0)], 1)
    rows = conv_back(d_act, conv_bc, sig_bc, shifted_bc, bc)
    for r, row in enumerate(rows):
        gch_ref[r : r + 1, bc] += row

    from_x, from_y = rs_ref[0], rs_ref[1]
    d_cum = from_y - from_x
    row_of = lax.broadcasted_iota(jnp.int32, (STRETCH, 1), 0)
    first = d_cum[lo] + jnp.where(row_of == STRETCH - 1, d_tail, 0.0)
    tri_t = triangle(True)
    d_rate = jnp.concatenate([dot_high(tri_t, first), dot_high(tri_t, d_cum[hi])], 0)
    flow = rate * d_rate
    d_dt = (from_x + flow) * ratio
    dxb_ref[:, inner + 2 * LANES :] = d_dt.astype(BF16)
    gh_ref[0:1, :] += jnp.sum(d_dt, axis=0, keepdims=True)
    gh_ref[1:2, :] += jnp.sum(flow, axis=0, keepdims=True)


def run_fwd(limits, xb, taps, heads, skip, slot, waits=()):
    rows, cols = xb.shape
    inner = cols - 3 * LANES
    seqs = rows // slot
    whole = lambda shape: pl.BlockSpec(shape, lambda q, *_: (0,) * len(shape))
    per = lambda width: pl.BlockSpec((slot, width), lambda q, *_: (q, 0))
    return pl.pallas_call(
        functools.partial(fwd_kernel, len(waits)),
        grid_spec=pltpu.PrefetchScalarGridSpec(
            num_scalar_prefetch=1,
            grid=(seqs,),
            in_specs=[per(cols), whole(taps.shape), whole(heads.shape), whole(skip.shape)]
            + [pl.BlockSpec(memory_space=pl.ANY)] * len(waits),
            out_specs=[
                per(inner),
                pl.BlockSpec((inner, LANES), lambda q, *_: (q, 0)),
            ],
        ),
        out_shape=[
            jax.ShapeDtypeStruct((rows, inner), F32),
            jax.ShapeDtypeStruct((seqs * inner, LANES), BF16),
        ],
        name="scan_forward",
    )(limits, xb, taps, heads, skip, *waits)


def tie_kernel(*refs):
    pass


def tie(value, *waits):
    return pl.pallas_call(
        tie_kernel,
        in_specs=[pl.BlockSpec(memory_space=pl.ANY)] * (1 + len(waits)),
        out_specs=pl.BlockSpec(memory_space=pl.ANY),
        out_shape=jax.ShapeDtypeStruct(value.shape, value.dtype),
        input_output_aliases={0: 0},
        name="order",
    )(value, *waits)


def run_bwd(limits, xb, y, dy, s1, taps, heads, skip, slot, first, count, d_xb=None, waits=()):
    rows, cols = xb.shape
    inner = cols - 3 * LANES
    whole = lambda shape: pl.BlockSpec(shape, lambda q, *_: (0,) * len(shape))
    per = lambda width: pl.BlockSpec((slot, width), lambda q, *_: (q + first, 0))
    aliased = d_xb is not None
    kernel = functools.partial(bwd_kernel, first, aliased + len(waits))
    return pl.pallas_call(
        kernel,
        grid_spec=pltpu.PrefetchScalarGridSpec(
            num_scalar_prefetch=1,
            grid=(count,),
            in_specs=[
                per(cols),
                per(inner),
                per(inner),
                pl.BlockSpec((inner, LANES), lambda q, *_: (q + first, 0)),
                whole(taps.shape),
                whole(heads.shape),
                whole(skip.shape),
            ]
            + [pl.BlockSpec(memory_space=pl.ANY)] * (aliased + len(waits)),
            out_specs=[per(cols), whole((8, cols)), whole((8, LANES))],
            scratch_shapes=[
                pltpu.VMEM((2, STRETCH, STRETCH), F32),
                pltpu.VMEM((2, 2 * STRETCH, LANES), F32),
            ],
        ),
        out_shape=[
            jax.ShapeDtypeStruct((rows, cols), BF16),
            jax.ShapeDtypeStruct((8, cols), F32),
            jax.ShapeDtypeStruct((8, LANES), F32),
        ],
        input_output_aliases={8: 0} if aliased else {},
        name="scan_backward",
    )(limits, xb, y, dy, s1, taps, heads, skip, *([d_xb] if aliased else []), *waits)


def prepare_kernel(length_ref, u_ref, cot_ref, gain_ref, normed_ref, branch_ref):
    rows, _ = u_ref.shape
    u = u_ref[...].astype(F32)
    rstd = lax.rsqrt(jnp.mean(u * u, axis=-1, keepdims=True) + 1e-05)
    row = lax.broadcasted_iota(jnp.int32, (rows, 1), 0) + pl.program_id(0) * rows
    valid = row < length_ref[0]
    normed_ref[...] = (u * rstd * gain_ref[...]).astype(BF16)
    branch_ref[...] = jnp.where(valid, cot_ref[...].astype(F32), 0.0).astype(BF16)


def run_prepare(lengths, tokens, cotangent, gain):
    slot, width = tokens.shape
    step = slot // 4
    per = pl.BlockSpec((step, width), lambda i, *_: (i, 0))
    return pl.pallas_call(
        prepare_kernel,
        grid_spec=pltpu.PrefetchScalarGridSpec(
            num_scalar_prefetch=1,
            grid=(4,),
            in_specs=[per, per, pl.BlockSpec((1, width), lambda i, *_: (0, 0))],
            out_specs=[per, per],
        ),
        out_shape=[jax.ShapeDtypeStruct((slot, width), BF16)] * 2,
        name="prepare_rows",
    )(lengths, tokens, cotangent, gain)


def output_kernel(count, length_ref, u_ref, *refs):
    parts, out_ref = refs[:count], refs[count]
    rows, _ = u_ref.shape
    row = lax.broadcasted_iota(jnp.int32, (rows, 1), 0) + pl.program_id(0) * rows
    total = parts[0][...].astype(F32)
    for part in parts[1:]:
        total = total + part[...].astype(F32)
    total = jnp.where(row < length_ref[0], total, 0.0)
    out_ref[...] = (u_ref[...].astype(F32) + total).astype(BF16)


def grad_kernel(count, u_ref, cot_ref, gain_ref, *refs):
    parts, out_ref = refs[:count], refs[count]
    u = u_ref[...].astype(F32)
    rstd = lax.rsqrt(jnp.mean(u * u, axis=-1, keepdims=True) + 1e-05)
    total = parts[0][...].astype(F32)
    for part in parts[1:]:
        total = total + part[...].astype(F32)
    total = total * gain_ref[...]
    back = jnp.mean(total * u, axis=-1, keepdims=True)
    grad = total * rstd - u * (rstd * rstd * rstd * back)
    out_ref[...] = (cot_ref[...].astype(F32) + grad).astype(BF16)


def run_output(lengths, tokens, parts):
    slot, width = tokens.shape
    step = slot // 4
    per = pl.BlockSpec((step, width), lambda i, *_: (i, 0))
    return pl.pallas_call(
        functools.partial(output_kernel, len(parts)),
        grid_spec=pltpu.PrefetchScalarGridSpec(
            num_scalar_prefetch=1,
            grid=(4,),
            in_specs=[per] * (1 + len(parts)),
            out_specs=per,
        ),
        out_shape=jax.ShapeDtypeStruct((slot, width), BF16),
        name="layer_output",
    )(lengths, tokens, *parts)


def run_grad(tokens, cotangent, gain, parts):
    slot, width = tokens.shape
    step = slot // 8
    per = pl.BlockSpec((step, width), lambda i: (i, 0))
    return pl.pallas_call(
        functools.partial(grad_kernel, len(parts)),
        grid=(8,),
        in_specs=[per, per, pl.BlockSpec((1, width), lambda i: (0, 0))] + [per] * len(parts),
        out_specs=per,
        out_shape=jax.ShapeDtypeStruct((slot, width), BF16),
        name="input_gradient",
    )(tokens, cotangent, gain, *parts)


def per_device(
    tokens,
    cotangent,
    lengths,
    widths,
    norm_gain,
    w_zx,
    w_bc,
    w_dt,
    w_out,
    conv_w,
    conv_b,
    dt_bias,
    a_log,
    d_skip,
    gate_gain,
):
    grid = Grid()
    core, j, n = grid.core, grid.j, grid.n
    slot, width = tokens.shape
    assert lengths.shape[0] == 1 and slot == 2 * STRETCH
    rows_d = w_zx.shape[0]
    inner = w_zx.shape[2] // 2
    heads = w_dt.shape[1] // 2
    state2 = w_bc.shape[1]
    total = conv_w.shape[1]
    all_inner = total - state2
    part = j * 2 + core
    channel_base = part * inner
    head_base = part * heads
    cols = inner + 3 * LANES
    sent = inner + state2 + heads

    def halves(value, axis):
        size = value.shape[axis] // 2
        mine = lax.dynamic_slice_in_dim(value, core * size, size, axis)
        other = lax.dynamic_slice_in_dim(value, (1 - core) * size, size, axis)
        return mine, other

    def by_core(mine, other, axis):
        first = jnp.where(core == 0, mine, other)
        second = jnp.where(core == 0, other, mine)
        return jnp.concatenate([first, second], axis=axis)

    gain_row = norm_gain[None]
    normed_own, d_branch_own = run_prepare(lengths, tokens, cotangent, gain_row)

    x_mine, x_other = halves(w_zx[:, 1], 1)
    t_mine, t_other = halves(w_dt, 1)
    x_mine = jnp.concatenate([x_mine, w_bc, t_mine], axis=1)
    x_other = jnp.concatenate([x_other, w_bc, t_other], axis=1)
    block_x = by_core(x_mine, grid.swap_core(x_other), 0)
    z_mine, z_other = halves(w_zx[:, 0], 1)
    block_z = by_core(z_mine, grid.swap_core(z_other), 0)
    o_mine, o_other = halves(w_out.T, 1)
    block_o = by_core(o_mine, grid.swap_core(o_other), 0)
    w_x = gather_blocks(grid, block_x)
    w_z = gather_all(grid, block_z)
    w_o = gather_all(grid, block_o)
    w_x = jnp.pad(w_x, ((0, 0), (0, cols - sent)))

    order = [(g, e) for g in range(n - 1, -1, -1) for e in (1, 0)]
    index = lax.axis_index("dp")
    owners = [(index + e * (1 - 2 * core)) * n + (j - g) % n for g, e in order]

    def share(value):
        near = [value] + [grid.send_x(value, g) for g in range(1, n)]
        far = [grid.swap_core(piece) for piece in near]
        pieces = [far[g] if e else near[g] for g, e in order]
        return lax.optimization_barrier(jnp.concatenate(pieces, axis=0))

    def collect(parts):
        kept = []
        for i in range(0, len(parts), 2):
            g = order[i][0]
            there = grid.swap_core(parts[i])
            both = parts[i + 1].astype(F32) + there.astype(F32)
            kept.append(grid.send_x(both.astype(BF16), -g) if g else both)
        return kept

    normed = share(normed_own)
    d_branch = share(d_branch_own)
    seqs = len(owners)
    seq_width = jnp.stack([widths[o] for o in owners])
    used = seq_width * ((HEADS // 8) * HEAD_DIM)
    counts = jnp.repeat(used.astype(F32), slot)
    limits = jnp.clip(used - channel_base, 0, inner).astype(jnp.int32)

    taps = jnp.concatenate(
        [
            lax.dynamic_slice_in_dim(conv_w, channel_base, inner, 1),
            conv_w[:, all_inner:],
        ],
        axis=1,
    )
    bias = jnp.concatenate(
        [lax.dynamic_slice_in_dim(conv_b, channel_base, inner, 0), conv_b[all_inner:]]
    )
    taps = jnp.pad(jnp.concatenate([taps, bias[None]], 0), ((0, 3), (0, LANES)))
    own_heads = lambda v: lax.dynamic_slice_in_dim(v, head_base, heads, 0)
    head_rows = jnp.pad(
        jnp.stack([own_heads(dt_bias), own_heads(a_log)]), ((0, 6), (0, LANES - heads))
    )
    skip = jnp.broadcast_to(jnp.repeat(own_heads(d_skip), HEAD_DIM)[None], (8, inner))
    own_gain = lax.dynamic_slice_in_dim(gate_gain, channel_base, inner, 0)

    rows_of = lambda value, i: value[i * slot : (i + 1) * slot]
    xb = dot_nn(normed, w_x)
    scan = (taps, head_rows, skip, slot)
    y, s1 = run_fwd(limits, xb, *scan)
    z = dot_nn(normed, w_z)
    sig = jax.nn.sigmoid(z)
    gated = y * (z * sig)

    def group_sum(rows):
        rows = rows.reshape(n, 2, slot)
        rows = rows + grid.swap_core(rows)[:, ::-1]
        total = rows
        for g in range(1, n):
            total = total + jnp.roll(grid.send_x(rows, g), -g, axis=0)
        return total.reshape(seqs * slot)

    scale = lax.rsqrt(group_sum(jnp.sum(gated * gated, axis=1)) / counts + 1e-05)
    gnorm = (gated * scale[:, None] * own_gain).astype(BF16)

    g_o_part = dot_tn(d_branch, gnorm).astype(BF16)
    g_o = scatter_all(grid, g_o_part)
    d_gnorm = dot_nn(d_branch, w_o)
    weighted = d_gnorm * own_gain
    inner_sum = group_sum(jnp.sum(weighted * gated, axis=1))
    pull = scale * scale * scale / counts * inner_sum
    d_gated = weighted * scale[:, None] - gated * pull[:, None]
    g_gate = jnp.sum(d_gnorm * gated * scale[:, None], axis=0)
    silu = z * sig
    d_y = (d_gated * silu).astype(BF16)
    d_z = (d_gated * y * (sig * (1.0 + z * (1.0 - sig)))).astype(BF16)
    g_z_part = dot_tn(normed, d_z).astype(BF16)
    g_z = scatter_all(grid, g_z_part)

    def back(i):
        part = dot_nt(rows_of(d_z, i), w_z) + dot_nt(rows_of(d_xb, i), w_x)
        return jnp.sum(part * rows_of(normed, i).astype(F32), axis=0), part.astype(BF16)

    far = seqs - 2
    d_normed, branch, g_norm_part = [], [], 0.0
    d_xb, g_channels, g_heads = run_bwd(
        limits, xb, y, d_y, s1, *scan, 0, far, None, (g_o_part, g_z_part)
    )
    ahead = [back(i) for i in range(far)]
    for i in range(0, far, 2):
        both = ahead[i + 1][1].astype(F32) + grid.swap_core(ahead[i][1]).astype(F32)
        d_normed.append(both.astype(BF16))
    d_xb, more_channels, more_heads = run_bwd(
        limits, xb, y, d_y, s1, *scan, far, 2, d_xb, tuple(d_normed)
    )
    d_normed = [grid.send_x(d_normed[i], -order[2 * i][0]) for i in range(len(d_normed))]
    g_channels, g_heads = g_channels + more_channels, g_heads + more_heads
    g_x_part = dot_tn(normed, d_xb)[:, :sent].astype(BF16)
    g_x = scatter_blocks(grid, g_x_part)
    out_rows = [dot_nt(rows_of(gnorm, i), w_o).astype(BF16) for i in range(seqs)]
    branch = collect(out_rows)
    ahead += [back(i) for i in range(far, seqs)]
    d_normed.append(ahead[far + 1][1].astype(F32) + grid.swap_core(ahead[far][1]).astype(F32))
    g_norm_part = sum(part[0] for part in ahead)

    output = run_output(lengths, tokens, branch)
    input_grad = run_grad(tokens, cotangent, gain_row, d_normed)

    def to_rows(value):
        mine = lax.dynamic_slice_in_dim(value, core * rows_d, rows_d, 0)
        other = lax.dynamic_slice_in_dim(value, (1 - core) * rows_d, rows_d, 0)
        return mine, grid.swap_core(other)

    z_rows = by_core(*to_rows(g_z), 1)
    o_rows = by_core(*to_rows(g_o), 1)
    x_mine, x_recv = to_rows(g_x)
    x_rows = by_core(x_mine[:, :inner], x_recv[:, :inner], 1)
    t_rows = by_core(x_mine[:, inner + state2 :], x_recv[:, inner + state2 :], 1)
    bc_rows = (x_mine + x_recv)[:, inner : inner + state2]
    bc_sum = bc_rows
    for g in range(1, n):
        bc_sum = bc_sum + grid.send_x(bc_rows, g)
    g_w_zx = jnp.stack([z_rows, x_rows], axis=1)

    g_skip = g_channels[5, :inner].reshape(heads, HEAD_DIM).sum(axis=1)
    head_parts = jnp.stack([g_heads[0, :heads], g_heads[1, :heads], g_skip])
    mine = [
        g_channels[:5].reshape(-1),
        g_gate,
        g_norm_part / norm_gain,
        head_parts.reshape(-1),
    ]
    sizes = [piece.shape[0] for piece in mine]
    flat = jnp.concatenate(mine)
    flat = jnp.pad(flat, (0, -flat.shape[0] % 1024)).reshape(-1, LANES)
    flat = grid.all_sum(flat, "dp", grid.dp_bits()).reshape(-1)
    own_conv = flat[: sizes[0]].reshape(5, cols)
    own_gate = flat[sizes[0] : sizes[0] + sizes[1]]
    own_norm = flat[sizes[0] + sizes[1] : sum(sizes[:3])]
    own_heads_sum = flat[sum(sizes[:3]) : sum(sizes)].reshape(3, heads)
    conv_rows = jnp.zeros((5, total), F32)
    conv_rows = lax.dynamic_update_slice(conv_rows, own_conv[:, :inner], (0, channel_base))
    conv_rows = lax.dynamic_update_slice(
        conv_rows, own_conv[:, inner : inner + state2], (0, all_inner)
    )
    gate_row = lax.dynamic_update_slice(jnp.zeros((all_inner,), F32), own_gate, (channel_base,))
    head_all = lax.dynamic_update_slice(
        jnp.zeros((3, d_skip.shape[0]), F32), own_heads_sum, (0, head_base)
    )
    flat = jnp.concatenate([own_norm, conv_rows.reshape(-1), gate_row, head_all.reshape(-1)])
    size = flat.shape[0]
    flat = jnp.pad(flat, (0, -size % 1024)).reshape(-1, LANES)
    flat = grid.all_sum(flat, "dp", [1])
    flat = grid.all_sum(flat, "fsdp", grid.fsdp_bits()).reshape(-1)[:size]
    ends = [width, width + 5 * total, width + 5 * total + all_inner]
    g_norm, g_conv, g_gate, g_small = jnp.split(flat, ends)
    g_conv = g_conv.reshape(5, total)
    g_small = g_small.reshape(3, -1)
    return (
        output,
        input_grad,
        g_norm,
        g_w_zx,
        bc_sum,
        t_rows,
        o_rows.T,
        g_conv[:4],
        g_conv[4],
        g_small[0],
        g_small[1],
        g_small[2],
        g_gate,
    )


def solution(mesh):
    in_specs = (
        P(("dp", "fsdp"), None),
        P(("dp", "fsdp"), None),
        P(("dp", "fsdp")),
        P(),
        P(),
        P("dp", None, "fsdp"),
        P("dp", None),
        P("dp", "fsdp"),
        P("fsdp", "dp"),
        P(),
        P(),
        P(),
        P(),
        P(),
        P(),
    )
    out_specs = (
        P(("dp", "fsdp"), None),
        P(("dp", "fsdp"), None),
        P(),
        P("dp", None, "fsdp"),
        P("dp", None),
        P("dp", "fsdp"),
        P("fsdp", "dp"),
        P(),
        P(),
        P(),
        P(),
        P(),
        P(),
    )
    return jax.shard_map(
        per_device, mesh=mesh, in_specs=in_specs, out_specs=out_specs, check_vma=False
    )
```

```python
import functools

import jax
import jax.numpy as jnp
from jax import lax
from jax.experimental import pallas as pl
from jax.experimental.pallas import tpu as pltpu
from jax.sharding import PartitionSpec as P

HEADS = 64
HEAD_DIM = 64
STRETCH = 256
LANES = 128
F32 = jnp.float32
BF16 = jnp.bfloat16
NEG = -1e30
HIGH = lax.Precision.HIGHEST
MICRO = 10**9


def busy(flops, scale=1.0):
    return pl.CostEstimate(flops=int(flops * scale), transcendentals=0, bytes_accessed=0)


def dot_nn(a, b):
    return lax.dot_general(a, b, (((1,), (0,)), ((), ())), preferred_element_type=F32)


def dot_nt(a, b):
    return lax.dot_general(a, b, (((1,), (1,)), ((), ())), preferred_element_type=F32)


def dot_tn(a, b):
    return lax.dot_general(a, b, (((0,), (0,)), ((), ())), preferred_element_type=F32)


class Grid:
    def __init__(self):
        self.dp = lax.axis_size("dp")
        self.n = lax.axis_size("fsdp")
        chips = self.dp // 2
        self.zs = 4 if chips % 4 == 0 else 1
        self.ys = chips // self.zs
        index = lax.axis_index("dp")
        self.core = index % 2
        self.chip = index // 2
        self.z = self.chip // self.ys
        self.y = self.chip % self.ys
        self.j = lax.axis_index("fsdp")
        self.slots = self.zs * self.ys

    def _dp(self, value, move):
        pairs = []
        for i in range(self.dp):
            z, y, c = i // (2 * self.ys), (i // 2) % self.ys, i % 2
            z, y, c = move(z, y, c)
            pairs.append((i, (z * self.ys + y) * 2 + c))
        return lax.ppermute(value, "dp", pairs)

    def swap_core(self, value):
        return self._dp(value, lambda z, y, c: (z, y, 1 - c))

    def send_z(self, value, s):
        return self._dp(value, lambda z, y, c: ((z + s) % self.zs, y, c))

    def send_y(self, value, f):
        return self._dp(value, lambda z, y, c: (z, (y + f) % self.ys, c))

    def send_x(self, value, g):
        pairs = [(i, (i + g) % self.n) for i in range(self.n)]
        return lax.ppermute(value, "fsdp", pairs)

    def place(self, f, s):
        return ((self.z - s) % self.zs) * self.ys + (self.y - f) % self.ys

    def chip_sum(self, value):
        pieces = jnp.zeros((self.slots,) + value.shape, value.dtype)
        for s in range(self.zs):
            for f in range(self.ys):
                here = value
                if s or f:
                    here = self._dp(
                        value, lambda z, y, c: ((z + s) % self.zs, (y + f) % self.ys, c)
                    )
                pieces = lax.dynamic_update_slice_in_dim(pieces, here[None], self.place(f, s), 0)
        return jnp.sum(pieces, axis=0)

    def chip_sum(self, value):
        bit = 2
        while bit < self.dp:
            value = value + lax.ppermute(value, "dp", [(i, i ^ bit) for i in range(self.dp)])
            bit *= 2
        return value

    def group_parts(self, value):
        near = [value] + [self.send_x(value, g) for g in range(1, self.n)]
        pieces = jnp.zeros((self.n * 2,) + value.shape, value.dtype)
        for g, here in enumerate(near):
            place = ((self.j - g) % self.n) * 2
            pieces = lax.dynamic_update_slice_in_dim(pieces, here[None], place + self.core, 0)
            there = self.swap_core(here)
            pieces = lax.dynamic_update_slice_in_dim(pieces, there[None], place + 1 - self.core, 0)
        return pieces


def gather_ring(grid, block):
    rows = block.shape[0]
    out = jnp.zeros((grid.slots * rows,) + block.shape[1:], block.dtype)
    along, crossed = [block], ()
    for s in range(grid.zs):
        piece = along[s]
        waits = crossed
        if waits:
            piece = tie(piece, *waits)
            along[s] = piece
        if s + 1 < grid.zs:
            along.append(grid.send_z(piece, 1))
        crossed = tuple(grid.send_y(piece, f) for f in range(1, grid.ys))
        for f, here in enumerate((piece,) + crossed):
            out = lax.dynamic_update_slice_in_dim(out, here, grid.place(f, s) * rows, 0)
    return along, out


def add_kernel(place_ref, *refs):
    total = refs[0][...].astype(F32)
    for ref in refs[1:-1]:
        total = total + ref[...].astype(F32)
    refs[-1][...] = total.astype(refs[-1].dtype)


def add_rows(place, value, moved, dtype):
    rows, cols = value.shape[0], value.shape[1]
    size = moved[0][2]
    step = size // 2
    spec = lambda block: pl.BlockSpec((step, cols), lambda i, _: (2 * block + i, 0))
    return pl.pallas_call(
        add_kernel,
        grid_spec=pltpu.PrefetchScalarGridSpec(
            num_scalar_prefetch=1,
            grid=(2,),
            in_specs=[pl.BlockSpec((step, cols), lambda i, at: (2 * at[0] + i, 0))]
            + [spec(block) for _, block, _ in moved],
            out_specs=pl.BlockSpec((step, cols), lambda i, _: (i, 0)),
        ),
        out_shape=jax.ShapeDtypeStruct((size, cols), dtype),
        cost_estimate=busy(MICRO),
        name="add_rows",
    )(place, value, *[array for array, _, _ in moved])


class ScatterX:
    def __init__(self, grid, value):
        self.grid, self.value = grid, value
        self.rows = value.shape[0] // grid.slots
        steps = list(range(grid.zs - 1, -1, -1))
        cut = (grid.zs + 1) // 2
        self.come = {}
        for group in (steps[:cut], steps[cut:]):
            arrived = [
                grid.send_y(
                    jnp.concatenate(
                        [
                            lax.dynamic_slice_in_dim(
                                value, grid.place(f, s) * self.rows, self.rows, 0
                            )
                            for s in group
                        ],
                        axis=0,
                    ),
                    -f,
                )
                for f in range(1, grid.ys)
            ]
            for i, s in enumerate(group):
                self.come[s] = [(array, i, self.rows) for array in arrived]
        self.sums = []

    def send(self, s, *waits):
        place = self.grid.place(0, s).astype(jnp.int32).reshape(1)
        part = add_rows(place, self.value, self.come[s], BF16 if s else F32)
        if s:
            part = self.grid.send_z(tie(part, *waits) if waits else part, -s)
        self.sums.append(part)
        return part

    def total(self):
        total = self.sums[-1].astype(F32)
        for part in self.sums[:-1]:
            total = total + part.astype(F32)
        return total


def core_groups(grid):
    return [list(range(c, grid.dp, 2)) for c in (0, 1)]


def gather_all(grid, block):
    return lax.all_gather(block, "dp", axis=0, tiled=True, axis_index_groups=core_groups(grid))


def scatter_all(grid, value):
    return lax.psum_scatter(
        value, "dp", scatter_dimension=0, tiled=True, axis_index_groups=core_groups(grid)
    )


def shift_down(value, by):
    if by == 0:
        return value
    rows = lax.broadcasted_iota(jnp.int32, value.shape, 0)
    return jnp.where(rows < by, 0.0, pltpu.roll(value, by, 0))


def shift_up(value, by):
    if by == 0:
        return value
    size = value.shape[0]
    rows = lax.broadcasted_iota(jnp.int32, value.shape, 0)
    return jnp.where(rows >= size - by, 0.0, pltpu.roll(value, size - by, 0))


def convolve(joined, taps, lanes):
    shifted = [shift_down(joined, 3 - k) for k in range(4)]
    total = taps[4:5, lanes]
    for k in range(4):
        total = total + taps[k : k + 1, lanes] * shifted[k]
    return shifted, total


def head_tables(dtr, heads):
    x = dtr + heads[0:1, :]
    dt = jnp.maximum(x, 0.0) + jnp.log1p(jnp.exp(-jnp.abs(x)))
    small = x < -30.0
    log_dt = jnp.where(small, x, jnp.log(dt))
    ratio = jnp.where(small, 1.0, jax.nn.sigmoid(x) / dt)
    rate = -dt * jnp.exp(heads[1:2, :])
    return log_dt, rate, ratio


def triangle(upper):
    rows = lax.broadcasted_iota(jnp.int32, (STRETCH, STRETCH), 0)
    cols = lax.broadcasted_iota(jnp.int32, (STRETCH, STRETCH), 1)
    return jnp.where(cols >= rows if upper else cols <= rows, 1.0, 0.0).astype(F32)


def dot_high(a, b):
    return jnp.dot(a, b, precision=HIGH, preferred_element_type=F32)


def pair_lanes(low, high, width=LANES):
    lane = lax.broadcasted_iota(jnp.int32, (low.shape[0], width), 1)
    return jnp.where(lane < HEAD_DIM, low, high)


def only(value, e):
    lane = lax.broadcasted_iota(jnp.int32, value.shape, 1)
    keep = (lane < HEAD_DIM) if e == 0 else (lane >= HEAD_DIM)
    return jnp.where(keep, value, jnp.zeros_like(value))


def fwd_kernel(waits, limit_ref, xb_ref, taps_ref, heads_ref, skip_ref, *refs):
    y_ref, s1_ref = refs[waits:]
    inner = y_ref.shape[1]
    limit = limit_ref[pl.program_id(0)]
    half = STRETCH // 2
    lo, hi = slice(0, STRETCH), slice(STRETCH, 2 * STRETCH)
    bc = slice(inner, inner + 2 * LANES)
    _, conv = convolve(xb_ref[:, bc], taps_ref, bc)
    act = jax.nn.silu(conv).astype(BF16)
    bm, cm = act[:, :LANES], act[:, LANES:]
    log_dt, rate, _ = head_tables(xb_ref[:, inner + 2 * LANES :], heads_ref)
    tri = triangle(False)
    cum = jnp.concatenate([dot_high(tri, rate[lo]), dot_high(tri, rate[hi])], 0)
    late = cum - log_dt
    late_t = late.T
    tail = jnp.exp(cum[STRETCH - 1 : STRETCH] - late[lo])
    ecum = jnp.exp(cum[hi])
    grams = [dot_nt(cm[b], bm[b]) for b in (lo, hi)]
    mask = lax.broadcasted_iota(jnp.int32, (half, half), 0) >= lax.broadcasted_iota(
        jnp.int32, (half, half), 1
    )
    for p in range(inner // LANES):
        lanes = slice(p * LANES, (p + 1) * LANES)
        _, conv = convolve(xb_ref[:, lanes], taps_ref, lanes)
        channel = lax.broadcasted_iota(jnp.int32, (1, LANES), 1) + p * LANES
        xs = (jax.nn.silu(conv) * (channel < limit).astype(F32)).astype(BF16)
        h = 2 * p
        weights = pair_lanes(tail[:, h : h + 1], tail[:, h + 1 : h + 2])
        weighted = (xs[lo].astype(F32) * weights).astype(BF16)
        state = dot_tn(weighted, bm[lo]).astype(BF16)
        s1_ref[lanes, :] = state
        for b, gram in zip((lo, hi), grams):
            tops, lows = [], []
            xe = [only(xs[b], e) for e in (0, 1)]
            base = b.start
            for e in (0, 1):
                col = cum[b, h + e : h + e + 1]
                row = late_t[h + e : h + e + 1, b]
                top = jnp.exp(jnp.where(mask, col[:half] - row[:, :half], NEG))
                low0 = jnp.exp(col[half:] - row[:, :half])
                low1 = jnp.exp(jnp.where(mask, col[half:] - row[:, half:], NEG))
                tops.append((gram[:half, :half] * top).astype(BF16))
                lows.append((gram[half:, :half] * low0).astype(BF16))
                lows.append((gram[half:, half:] * low1).astype(BF16))
            y0 = dot_nn(
                jnp.concatenate(tops, 1), jnp.concatenate([xe[0][:half], xe[1][:half]], 0)
            )
            y1 = dot_nn(jnp.concatenate(lows, 1), jnp.concatenate(xe, 0))
            if base:
                inter = dot_nt(cm[b], state)
                inter = inter * pair_lanes(ecum[:, h : h + 1], ecum[:, h + 1 : h + 2])
                y0, y1 = y0 + inter[:half], y1 + inter[half:]
            skip = skip_ref[0:1, lanes] * xs[b].astype(F32)
            y_ref[pl.ds(base, half), lanes] = y0 + skip[:half]
            y_ref[pl.ds(base + half, half), lanes] = y1 + skip[half:]


def lane_sum(value, e):
    return jnp.sum(only(value, e), axis=1, keepdims=True)


def bwd_kernel(first, extra, limit_ref, xb_ref, y_ref, dy_ref, s1_ref, taps_ref, *refs):
    heads_ref, skip_ref = refs[:2]
    dxb_ref, gch_ref, gh_ref, dg_ref, rs_ref = refs[2 + extra :]
    inner = y_ref.shape[1]
    q = pl.program_id(0)
    limit = limit_ref[q + first]
    half = STRETCH // 2
    lo, hi = slice(0, STRETCH), slice(STRETCH, 2 * STRETCH)
    bc = slice(inner, inner + 2 * LANES)

    @pl.when(q == 0)
    def _():
        gch_ref[...] = jnp.zeros_like(gch_ref)
        gh_ref[...] = jnp.zeros_like(gh_ref)

    dg_ref[...] = jnp.zeros_like(dg_ref)
    rs_ref[...] = jnp.zeros_like(rs_ref)
    shifted_bc, conv_bc = convolve(xb_ref[:, bc], taps_ref, bc)
    sig_bc = jax.nn.sigmoid(conv_bc)
    act = (conv_bc * sig_bc).astype(BF16)
    bm, cm = act[:, :LANES], act[:, LANES:]
    log_dt, rate, ratio = head_tables(xb_ref[:, inner + 2 * LANES :], heads_ref)
    tri = triangle(False)
    cum = jnp.concatenate([dot_high(tri, rate[lo]), dot_high(tri, rate[hi])], 0)
    late = cum - log_dt
    cum_t = cum.T
    tail = jnp.exp(cum[STRETCH - 1 : STRETCH] - late[lo])
    ecum = jnp.exp(cum[hi])
    grams = [dot_nt(bm[b], cm[b]) for b in (lo, hi)]
    mask = lax.broadcasted_iota(jnp.int32, (half, half), 1) >= lax.broadcasted_iota(
        jnp.int32, (half, half), 0
    )
    d_bm0 = jnp.zeros((STRETCH, LANES), F32)
    d_cm1 = jnp.zeros((STRETCH, LANES), F32)
    d_tail = jnp.zeros((1, LANES), F32)
    lane_of = lax.broadcasted_iota(jnp.int32, (1, LANES), 1)

    def conv_back(d_act, conv, sig, shifted, lanes):
        d_conv = d_act * (sig * (1.0 + conv * (1.0 - sig)))
        rows = [jnp.sum(d_conv * part, axis=0, keepdims=True) for part in shifted]
        rows.append(jnp.sum(d_conv, axis=0, keepdims=True))
        total = None
        for k in range(4):
            part = taps_ref[k : k + 1, lanes] * shift_up(d_conv, 3 - k)
            total = part if total is None else total + part
        dxb_ref[:, lanes] = total.astype(BF16)
        return rows

    for p in range(inner // LANES):
        lanes = slice(p * LANES, (p + 1) * LANES)
        h = 2 * p
        shifted, conv = convolve(xb_ref[:, lanes], taps_ref, lanes)
        sig = jax.nn.sigmoid(conv)
        channel = lane_of + p * LANES
        used = (channel < limit).astype(F32)
        xs = (conv * sig * used).astype(BF16)
        xf = xs.astype(F32)
        dy = dy_ref[:, lanes]
        dyf = dy.astype(F32)
        skip = skip_ref[0:1, lanes]
        d_prior = (dyf[hi] * pair_lanes(ecum[:, h : h + 1], ecum[:, h + 1 : h + 2])).astype(BF16)
        d_state = dot_tn(d_prior, cm[hi]).astype(BF16)
        weights = pair_lanes(tail[:, h : h + 1], tail[:, h + 1 : h + 2])
        weighted = (xf[lo] * weights).astype(BF16)
        d_from_state = dot_nt(bm[lo], d_state) * weights
        d_bm0 = d_bm0 + dot_nn(weighted, d_state)
        d_cm1 = d_cm1 + dot_nn(d_prior, s1_ref[lanes, :])
        columns = []
        for i, (b, gram) in enumerate(zip((lo, hi), grams)):
            tops, lows = [], []
            dye = [only(dy[b], e) for e in (0, 1)]
            for e in (0, 1):
                col = late[b, h + e : h + e + 1]
                row = cum_t[h + e : h + e + 1, b]
                top0 = jnp.exp(jnp.where(mask, row[:, :half] - col[:half], NEG))
                top1 = jnp.exp(row[:, half:] - col[:half])
                low = jnp.exp(jnp.where(mask, row[:, half:] - col[half:], NEG))
                xe = only(xs[b], e)
                d_top = dot_nt(xe[:half], dy[b])
                d_low = dot_nt(xe[half:], dy[b][half:])
                tops.append((gram[:half, :half] * top0).astype(BF16))
                tops.append((gram[:half, half:] * top1).astype(BF16))
                lows.append((gram[half:, half:] * low).astype(BF16))
                dg_ref[i, :half, :half] += d_top[:, :half] * top0
                dg_ref[i, :half, half:] += d_top[:, half:] * top1
                dg_ref[i, half:, half:] += d_low * low
            d0 = dot_nn(jnp.concatenate(tops, 1), jnp.concatenate(dye, 0))
            d1 = dot_nn(
                jnp.concatenate(lows, 1), jnp.concatenate([dye[0][half:], dye[1][half:]], 0)
            )
            columns += [d0, d1]
        d_x = jnp.concatenate(columns, 0)
        d_x = jnp.concatenate([d_x[lo] + d_from_state, d_x[hi]], 0)
        from_x = xf * d_x
        from_y = dyf * (y_ref[:, lanes] - skip * xf)
        state_sum = jnp.sum(xf[lo] * d_from_state, axis=0, keepdims=True)
        for e in (0, 1):
            here = lane_of == h + e
            rs_ref[0] = jnp.where(here, lane_sum(from_x, e), rs_ref[0])
            rs_ref[1] = jnp.where(here, lane_sum(from_y, e), rs_ref[1])
            d_tail = jnp.where(here, lane_sum(state_sum, e), d_tail)
        d_act = (d_x + skip * dyf) * used
        rows = conv_back(d_act, conv, sig, shifted, lanes)
        rows.append(jnp.sum(dyf * xf, axis=0, keepdims=True))
        for r, row in enumerate(rows):
            gch_ref[r : r + 1, lanes] += row

    d_bm, d_cm = [], []
    for i, b in enumerate((lo, hi)):
        d_gram = dg_ref[i].astype(BF16)
        d_bm.append(dot_nn(d_gram, cm[b]))
        d_cm.append(dot_tn(d_gram, bm[b]))
    d_bm[0] = d_bm[0] + d_bm0
    d_cm[1] = d_cm[1] + d_cm1
    d_act = jnp.concatenate([jnp.concatenate(d_bm, 0), jnp.concatenate(d_cm, 0)], 1)
    rows = conv_back(d_act, conv_bc, sig_bc, shifted_bc, bc)
    for r, row in enumerate(rows):
        gch_ref[r : r + 1, bc] += row

    from_x, from_y = rs_ref[0], rs_ref[1]
    d_cum = from_y - from_x
    row_of = lax.broadcasted_iota(jnp.int32, (STRETCH, 1), 0)
    first = d_cum[lo] + jnp.where(row_of == STRETCH - 1, d_tail, 0.0)
    tri_t = triangle(True)
    d_rate = jnp.concatenate([dot_high(tri_t, first), dot_high(tri_t, d_cum[hi])], 0)
    flow = rate * d_rate
    d_dt = (from_x + flow) * ratio
    dxb_ref[:, inner + 2 * LANES :] = d_dt.astype(BF16)
    gh_ref[0:1, :] += jnp.sum(d_dt, axis=0, keepdims=True)
    gh_ref[1:2, :] += jnp.sum(flow, axis=0, keepdims=True)


def run_fwd(limits, xb, taps, heads, skip, slot, waits=()):
    rows, cols = xb.shape
    inner = cols - 3 * LANES
    seqs = rows // slot
    whole = lambda shape: pl.BlockSpec(shape, lambda q, *_: (0,) * len(shape))
    per = lambda width: pl.BlockSpec((slot, width), lambda q, *_: (q, 0))
    return pl.pallas_call(
        functools.partial(fwd_kernel, len(waits)),
        grid_spec=pltpu.PrefetchScalarGridSpec(
            num_scalar_prefetch=1,
            grid=(seqs,),
            in_specs=[per(cols), whole(taps.shape), whole(heads.shape), whole(skip.shape)]
            + [pl.BlockSpec(memory_space=pl.ANY)] * len(waits),
            out_specs=[
                per(inner),
                pl.BlockSpec((inner, LANES), lambda q, *_: (q, 0)),
            ],
        ),
        out_shape=[
            jax.ShapeDtypeStruct((rows, inner), F32),
            jax.ShapeDtypeStruct((seqs * inner, LANES), BF16),
        ],
        cost_estimate=busy(25 * MICRO),
        name="scan_forward",
    )(limits, xb, taps, heads, skip, *waits)


def tie_kernel(*refs):
    pass


def tie(value, *waits):
    return pl.pallas_call(
        tie_kernel,
        in_specs=[pl.BlockSpec(memory_space=pl.ANY)] * (1 + len(waits)),
        out_specs=pl.BlockSpec(memory_space=pl.ANY),
        out_shape=jax.ShapeDtypeStruct(value.shape, value.dtype),
        input_output_aliases={0: 0},
        name="order",
    )(value, *waits)


def run_bwd(limits, xb, y, dy, s1, taps, heads, skip, slot, first, count, d_xb=None, waits=()):
    rows, cols = xb.shape
    inner = cols - 3 * LANES
    whole = lambda shape: pl.BlockSpec(shape, lambda q, *_: (0,) * len(shape))
    per = lambda width: pl.BlockSpec((slot, width), lambda q, *_: (q + first, 0))
    aliased = d_xb is not None
    kernel = functools.partial(bwd_kernel, first, aliased + len(waits))
    return pl.pallas_call(
        kernel,
        grid_spec=pltpu.PrefetchScalarGridSpec(
            num_scalar_prefetch=1,
            grid=(count,),
            in_specs=[
                per(cols),
                per(inner),
                per(inner),
                pl.BlockSpec((inner, LANES), lambda q, *_: (q + first, 0)),
                whole(taps.shape),
                whole(heads.shape),
                whole(skip.shape),
            ]
            + [pl.BlockSpec(memory_space=pl.ANY)] * (aliased + len(waits)),
            out_specs=[per(cols), whole((8, cols)), whole((8, LANES))],
            scratch_shapes=[
                pltpu.VMEM((2, STRETCH, STRETCH), F32),
                pltpu.VMEM((2, 2 * STRETCH, LANES), F32),
            ],
        ),
        out_shape=[
            jax.ShapeDtypeStruct((rows, cols), BF16),
            jax.ShapeDtypeStruct((8, cols), F32),
            jax.ShapeDtypeStruct((8, LANES), F32),
        ],
        input_output_aliases={8: 0} if aliased else {},
        cost_estimate=busy(15 * count * MICRO),
        name="scan_backward",
    )(limits, xb, y, dy, s1, taps, heads, skip, *([d_xb] if aliased else []), *waits)


def prepare_kernel(length_ref, u_ref, cot_ref, gain_ref, *refs):
    normed_ref, branch_ref = refs[-2:]
    rows, _ = u_ref.shape
    u = u_ref[...].astype(F32)
    rstd = lax.rsqrt(jnp.mean(u * u, axis=-1, keepdims=True) + 1e-05)
    row = lax.broadcasted_iota(jnp.int32, (rows, 1), 0) + pl.program_id(0) * rows
    valid = row < length_ref[0]
    normed_ref[...] = (u * rstd * gain_ref[...]).astype(BF16)
    branch_ref[...] = jnp.where(valid, cot_ref[...].astype(F32), 0.0).astype(BF16)


def run_prepare(lengths, tokens, cotangent, gain, waits):
    slot, width = tokens.shape
    step = slot // 4
    per = pl.BlockSpec((step, width), lambda i, *_: (i, 0))
    return pl.pallas_call(
        prepare_kernel,
        grid_spec=pltpu.PrefetchScalarGridSpec(
            num_scalar_prefetch=1,
            grid=(4,),
            in_specs=[per, per, pl.BlockSpec((1, width), lambda i, *_: (0, 0))]
            + [pl.BlockSpec(memory_space=pl.ANY)] * len(waits),
            out_specs=[per, per],
        ),
        out_shape=[jax.ShapeDtypeStruct((slot, width), BF16)] * 2,
        cost_estimate=busy(5 * MICRO),
        name="prepare_rows",
    )(lengths, tokens, cotangent, gain, *waits)


def back_kernel(waits, dz_ref, dxb_ref, wz_ref, wx_ref, normed_ref, *refs):
    refs = refs[waits:]
    part = dot_nt(dz_ref[...], wz_ref[...]) + dot_nt(dxb_ref[...], wx_ref[...])
    slot = refs[0].shape[0]
    for i, ref in enumerate(refs[:-1]):
        ref[...] = part[i * slot : (i + 1) * slot].astype(BF16)
    product = part * normed_ref[...].astype(F32)
    refs[-1][...] = jnp.sum(product.reshape(-1, 8, product.shape[1]), axis=0)


def run_back(dz, dxb, wz, wx, normed, slot, first, waits=()):
    width, inner = wz.shape
    cols = wx.shape[1]
    step = 256
    rows = 2 * slot
    block = first // 2
    tall = lambda size: pl.BlockSpec((rows, size), lambda i: (block, 0))
    return pl.pallas_call(
        functools.partial(back_kernel, len(waits)),
        grid=(width // step,),
        in_specs=[
            tall(inner),
            tall(cols),
            pl.BlockSpec((step, inner), lambda i: (i, 0)),
            pl.BlockSpec((step, cols), lambda i: (i, 0)),
            pl.BlockSpec((rows, step), lambda i: (block, i)),
        ]
        + [pl.BlockSpec(memory_space=pl.ANY)] * len(waits),
        out_specs=[pl.BlockSpec((slot, step), lambda i: (0, i))] * 2
        + [pl.BlockSpec((8, step), lambda i: (0, i))],
        out_shape=[jax.ShapeDtypeStruct((slot, width), BF16)] * 2
        + [jax.ShapeDtypeStruct((8, width), F32)],
        cost_estimate=busy(0),
        name="normed_gradient",
    )(dz, dxb, wz, wx, normed, *waits)


def branch_kernel(waits, gnorm_ref, wo_ref, *refs):
    refs = refs[waits:]
    part = dot_nt(gnorm_ref[...], wo_ref[...])
    slot = refs[0].shape[0]
    for i, ref in enumerate(refs):
        ref[...] = part[i * slot : (i + 1) * slot].astype(BF16)


def run_branch(gnorm, wo, slot, first, waits=()):
    width, inner = wo.shape
    step = 256
    block = first // 2
    return pl.pallas_call(
        functools.partial(branch_kernel, len(waits)),
        grid=(width // step,),
        in_specs=[
            pl.BlockSpec((2 * slot, inner), lambda i: (block, 0)),
            pl.BlockSpec((step, inner), lambda i: (i, 0)),
        ]
        + [pl.BlockSpec(memory_space=pl.ANY)] * len(waits),
        out_specs=[pl.BlockSpec((slot, step), lambda i: (0, i))] * 2,
        out_shape=[jax.ShapeDtypeStruct((slot, width), BF16)] * 2,
        cost_estimate=busy(0),
        name="branch_rows",
    )(gnorm, wo, *waits)


def output_kernel(count, length_ref, u_ref, *refs):
    parts, out_ref = refs[:count], refs[count]
    rows, _ = u_ref.shape
    row = lax.broadcasted_iota(jnp.int32, (rows, 1), 0) + pl.program_id(0) * rows
    total = parts[0][...].astype(F32)
    for part in parts[1:]:
        total = total + part[...].astype(F32)
    total = jnp.where(row < length_ref[0], total, 0.0)
    out_ref[...] = (u_ref[...].astype(F32) + total).astype(BF16)


def grad_kernel(count, u_ref, cot_ref, gain_ref, *refs):
    parts, out_ref = refs[:count], refs[count]
    u = u_ref[...].astype(F32)
    rstd = lax.rsqrt(jnp.mean(u * u, axis=-1, keepdims=True) + 1e-05)
    total = parts[0][...].astype(F32)
    for part in parts[1:]:
        total = total + part[...].astype(F32)
    total = total * gain_ref[...]
    back = jnp.mean(total * u, axis=-1, keepdims=True)
    grad = total * rstd - u * (rstd * rstd * rstd * back)
    out_ref[...] = (cot_ref[...].astype(F32) + grad).astype(BF16)


def run_output(lengths, tokens, parts):
    slot, width = tokens.shape
    step = slot // 4
    per = pl.BlockSpec((step, width), lambda i, *_: (i, 0))
    return pl.pallas_call(
        functools.partial(output_kernel, len(parts)),
        grid_spec=pltpu.PrefetchScalarGridSpec(
            num_scalar_prefetch=1,
            grid=(4,),
            in_specs=[per] * (1 + len(parts)),
            out_specs=per,
        ),
        out_shape=jax.ShapeDtypeStruct((slot, width), BF16),
        cost_estimate=busy(5 * MICRO),
        name="layer_output",
    )(lengths, tokens, *parts)


def run_grad(tokens, cotangent, gain, parts):
    slot, width = tokens.shape
    step = slot // 8
    per = pl.BlockSpec((step, width), lambda i: (i, 0))
    return pl.pallas_call(
        functools.partial(grad_kernel, len(parts)),
        grid=(8,),
        in_specs=[per, per, pl.BlockSpec((1, width), lambda i: (0, 0))] + [per] * len(parts),
        out_specs=per,
        out_shape=jax.ShapeDtypeStruct((slot, width), BF16),
        cost_estimate=busy(8 * MICRO),
        name="input_gradient",
    )(tokens, cotangent, gain, *parts)


def per_device(
    tokens,
    cotangent,
    lengths,
    widths,
    norm_gain,
    w_zx,
    w_bc,
    w_dt,
    w_out,
    conv_w,
    conv_b,
    dt_bias,
    a_log,
    d_skip,
    gate_gain,
):
    grid = Grid()
    core, j, n = grid.core, grid.j, grid.n
    slot, width = tokens.shape
    assert lengths.shape[0] == 1 and slot == 2 * STRETCH
    rows_d = w_zx.shape[0]
    inner = w_zx.shape[2] // 2
    heads = w_dt.shape[1] // 2
    state2 = w_bc.shape[1]
    total = conv_w.shape[1]
    all_inner = total - state2
    part = j * 2 + core
    channel_base = part * inner
    head_base = part * heads
    cols = inner + 3 * LANES
    spare = cols - inner - state2 - heads

    def halves(value, axis):
        size = value.shape[axis] // 2
        mine = lax.dynamic_slice_in_dim(value, core * size, size, axis)
        other = lax.dynamic_slice_in_dim(value, (1 - core) * size, size, axis)
        return mine, other

    def by_core(mine, other, axis):
        first = jnp.where(core == 0, mine, other)
        second = jnp.where(core == 0, other, mine)
        return jnp.concatenate([first, second], axis=axis)

    def swapped(mine, other, *waits):
        return by_core(mine, grid.swap_core(tie(other, *waits) if waits else other), 0)

    fill = jnp.zeros((rows_d, spare), BF16)
    x_mine, x_other = halves(w_zx[:, 1], 1)
    t_mine, t_other = halves(w_dt, 1)
    x_mine = jnp.concatenate([x_mine, w_bc, t_mine, fill], axis=1)
    x_other = jnp.concatenate([x_other, w_bc, t_other, fill], axis=1)
    block_x = swapped(x_mine, x_other)
    gain_row = norm_gain[None]
    normed_own, d_branch_own = run_prepare(
        lengths, tokens, cotangent, gain_row, (x_other,)
    )
    z_mine, z_other = halves(w_zx[:, 0], 1)
    block_z = swapped(z_mine, z_other, normed_own)
    o_mine, o_other = halves(w_out.T, 1)
    block_o = swapped(o_mine, o_other, normed_own)
    arriving = [grid.send_x(normed_own, g) for g in range(1, n)]
    along, w_x = gather_ring(grid, block_x)
    arriving = [tie(value, along[-1]) for value in arriving]
    w_z = gather_all(grid, tie(block_z, along[1]))
    w_o = gather_all(grid, block_o)

    order = [(g, e) for g in range(n - 1, -1, -1) for e in (1, 0)]
    index = lax.axis_index("dp")
    owners = [(index + e * (1 - 2 * core)) * n + (j - g) % n for g, e in order]

    def share(value, arriving):
        near = [value] + arriving
        far = [grid.swap_core(piece) for piece in near]
        pieces = [far[g] if e else near[g] for g, e in order]
        return lax.optimization_barrier(jnp.concatenate(pieces, axis=0))

    normed = share(normed_own, arriving)
    d_branch = share(d_branch_own, [grid.send_x(d_branch_own, g) for g in range(1, n)])
    seqs = len(owners)
    seq_width = jnp.stack([widths[o] for o in owners])
    used = seq_width * ((HEADS // 8) * HEAD_DIM)
    counts = jnp.repeat(used.astype(F32), slot)
    limits = jnp.clip(used - channel_base, 0, inner).astype(jnp.int32)

    taps = jnp.concatenate(
        [
            lax.dynamic_slice_in_dim(conv_w, channel_base, inner, 1),
            conv_w[:, all_inner:],
        ],
        axis=1,
    )
    bias = jnp.concatenate(
        [lax.dynamic_slice_in_dim(conv_b, channel_base, inner, 0), conv_b[all_inner:]]
    )
    taps = jnp.pad(jnp.concatenate([taps, bias[None]], 0), ((0, 3), (0, LANES)))
    own_heads = lambda v: lax.dynamic_slice_in_dim(v, head_base, heads, 0)
    head_rows = jnp.pad(
        jnp.stack([own_heads(dt_bias), own_heads(a_log)]), ((0, 6), (0, LANES - heads))
    )
    skip = jnp.broadcast_to(jnp.repeat(own_heads(d_skip), HEAD_DIM)[None], (8, inner))
    own_gain = lax.dynamic_slice_in_dim(gate_gain, channel_base, inner, 0)

    rows_of = lambda value, i: value[i * slot : (i + 1) * slot]
    xb = dot_nn(normed, w_x)
    scan = (taps, head_rows, skip, slot)
    y, s1 = run_fwd(limits, xb, *scan)
    z = dot_nn(normed, w_z)
    sig = jax.nn.sigmoid(z)
    gated = y * (z * sig)

    def group_sum(rows):
        rows = rows.reshape(n, 2, slot)
        rows = rows + grid.swap_core(rows)[:, ::-1]
        total = rows
        for g in range(1, n):
            total = total + jnp.roll(grid.send_x(rows, g), -g, axis=0)
        return total.reshape(seqs * slot)

    scale = lax.rsqrt(group_sum(jnp.sum(gated * gated, axis=1)) / counts + 1e-05)
    gnorm = (gated * scale[:, None] * own_gain).astype(BF16)

    g_o_part = dot_tn(d_branch, gnorm).astype(BF16)
    g_o = scatter_all(grid, g_o_part)
    w_o = tie(w_o, g_o_part)
    d_gnorm = dot_nn(d_branch, w_o)
    weighted = d_gnorm * own_gain
    inner_part = jnp.sum(weighted * gated, axis=1)
    far = seqs - 2
    out_far = [run_branch(gnorm, w_o, slot, i, (inner_part,)) for i in range(0, far, 2)]
    inner_sum = group_sum(inner_part)
    if out_far:
        inner_sum = tie(inner_sum, *[rows for pair in out_far for rows in pair])
    pull = scale * scale * scale / counts * inner_sum
    d_gated = weighted * scale[:, None] - gated * pull[:, None]
    g_gate = jnp.sum(d_gnorm * gated * scale[:, None], axis=0)
    silu = z * sig
    d_y = (d_gated * silu).astype(BF16)
    d_z = (d_gated * y * (sig * (1.0 + z * (1.0 - sig)))).astype(BF16)
    g_z_part = dot_tn(normed, d_z).astype(BF16)
    g_z = scatter_all(grid, g_z_part)

    cross = lambda values: [
        grid.send_x(value, -order[2 * i][0]) for i, value in enumerate(values)
    ]
    d_normed, branch, g_norm_part = [], [], 0.0
    for out_there, out_here in out_far:
        out_there = grid.swap_core(out_there)
        branch.append((out_here.astype(F32) + out_there.astype(F32)).astype(BF16))
    d_xb, g_channels, g_heads = run_bwd(
        limits, xb, y, d_y, s1, *scan, 0, far, None, (g_o_part, g_z_part, *branch)
    )
    branch = cross(branch)
    for i in range(0, far, 2):
        there, here, more = run_back(d_z, d_xb, w_z, w_x, normed, slot, i)
        g_norm_part = g_norm_part + more
        there = grid.swap_core(tie(there, *branch))
        d_normed.append((here.astype(F32) + there.astype(F32)).astype(BF16))
    d_xb, more_channels, more_heads = run_bwd(
        limits, xb, y, d_y, s1, *scan, far, 2, d_xb, (*d_normed, g_o)
    )
    d_normed = cross(d_normed)
    g_channels, g_heads = g_channels + more_channels, g_heads + more_heads
    g_skip = g_channels[5, :inner].reshape(heads, HEAD_DIM).sum(axis=1)
    mine = jnp.concatenate(
        [
            g_channels[:5].reshape(-1),
            g_gate,
            jnp.pad(jnp.concatenate([g_heads[0, :heads], g_heads[1, :heads], g_skip]), (0, -3 * heads % LANES)),
        ]
    )
    g_x_part = dot_tn(normed, d_xb).astype(BF16)
    to_x = ScatterX(grid, g_x_part)
    there, here, more = run_back(
        d_z, d_xb, w_z, w_x, normed, slot, far, (g_x_part,)
    )
    d_normed += [here, grid.swap_core(there)]
    out_there, out_here = run_branch(gnorm, w_o, slot, far, (here,))
    out_there = grid.swap_core(tie(out_there, *d_normed[: far // 2]))

    def to_rows(value):
        rows = lax.dynamic_slice_in_dim(value, core * rows_d, rows_d, 0)
        other = lax.dynamic_slice_in_dim(value, (1 - core) * rows_d, rows_d, 0)
        return rows, grid.swap_core(other)

    o_rows = by_core(*to_rows(g_o.astype(F32)), 1).T
    z_rows = by_core(*to_rows(g_z.astype(F32)), 1)
    third = to_x.send(3, out_here, g_z)
    to_x.send(2, out_here)
    to_x.send(1)
    to_x.send(0)
    g_x = to_x.total()
    small = mine.shape[0]
    mine = jnp.concatenate([mine, jnp.sum(g_norm_part + more, axis=0)])
    mine = jnp.pad(mine, (0, -mine.shape[0] % 1024)).reshape(-1, LANES)
    mine = grid.chip_sum(tie(mine, third, o_rows, z_rows))
    branch += [out_here, out_there]

    output = run_output(lengths, tokens, branch)
    input_grad = run_grad(tokens, cotangent, gain_row, d_normed)

    x_mine, x_recv = to_rows(g_x)
    x_rows = by_core(x_mine[:, :inner], x_recv[:, :inner], 1)
    t_rows = by_core(x_mine[:, inner + state2 : cols - spare], x_recv[:, inner + state2 : cols - spare], 1)
    bc_rows = (x_mine + x_recv)[:, inner : inner + state2]
    bc_sum = bc_rows
    for g in range(1, n):
        bc_sum = bc_sum + grid.send_x(bc_rows, g)
    g_w_zx = jnp.stack([z_rows, x_rows], axis=1)

    mine = grid.group_parts(mine).reshape(2 * n, -1)
    conv = mine[:, : 5 * cols].reshape(2 * n, 5, cols)
    conv_x = jnp.swapaxes(conv[:, :, :inner], 0, 1).reshape(5, all_inner)
    conv_bc = jnp.sum(conv[:, :, inner : inner + state2], axis=0)
    g_conv = jnp.concatenate([conv_x, conv_bc], axis=1)
    g_gate = mine[:, 5 * cols : 5 * cols + inner].reshape(all_inner)
    g_small = mine[:, 5 * cols + inner : 5 * cols + inner + 3 * heads].reshape(2 * n, 3, heads)
    g_small = jnp.swapaxes(g_small, 0, 1).reshape(3, -1)
    g_norm = jnp.sum(mine[:, small : small + width], axis=0) / norm_gain
    return (
        output,
        input_grad,
        g_norm,
        g_w_zx,
        bc_sum,
        t_rows,
        o_rows,
        g_conv[:4],
        g_conv[4],
        g_small[0],
        g_small[1],
        g_small[2],
        g_gate,
    )


def solution(mesh):
    in_specs = (
        P(("dp", "fsdp"), None),
        P(("dp", "fsdp"), None),
        P(("dp", "fsdp")),
        P(),
        P(),
        P("dp", None, "fsdp"),
        P("dp", None),
        P("dp", "fsdp"),
        P("fsdp", "dp"),
        P(),
        P(),
        P(),
        P(),
        P(),
        P(),
    )
    out_specs = (
        P(("dp", "fsdp"), None),
        P(("dp", "fsdp"), None),
        P(),
        P("dp", None, "fsdp"),
        P("dp", None),
        P("dp", "fsdp"),
        P("fsdp", "dp"),
        P(),
        P(),
        P(),
        P(),
        P(),
        P(),
    )
    return jax.shard_map(
        per_device, mesh=mesh, in_specs=in_specs, out_specs=out_specs, check_vma=False
    )
```

```python
import functools

import jax
import jax.numpy as jnp
from jax import lax
from jax.experimental import pallas as pl
from jax.experimental.pallas import tpu as pltpu
from jax.sharding import PartitionSpec as P

HEADS = 64
HEAD_DIM = 64
STRETCH = 256
LANES = 128
F32 = jnp.float32
BF16 = jnp.bfloat16
NEG = -1e30
HIGH = lax.Precision.HIGHEST
MICRO = 10**9
LOG2E = 1.4426950408889634


def busy(flops, scale=1.0):
    return pl.CostEstimate(flops=int(flops * scale), transcendentals=0, bytes_accessed=0)


def dot_nn(a, b):
    return lax.dot_general(a, b, (((1,), (0,)), ((), ())), preferred_element_type=F32)


def dot_nt(a, b):
    return lax.dot_general(a, b, (((1,), (1,)), ((), ())), preferred_element_type=F32)


def dot_tn(a, b):
    return lax.dot_general(a, b, (((0,), (0,)), ((), ())), preferred_element_type=F32)


class Grid:
    def __init__(self):
        self.dp = lax.axis_size("dp")
        self.n = lax.axis_size("fsdp")
        chips = self.dp // 2
        self.zs = 4 if chips % 4 == 0 else 1
        self.ys = chips // self.zs
        index = lax.axis_index("dp")
        self.core = index % 2
        self.chip = index // 2
        self.z = self.chip // self.ys
        self.y = self.chip % self.ys
        self.j = lax.axis_index("fsdp")
        self.slots = self.zs * self.ys

    def _dp(self, value, move):
        pairs = []
        for i in range(self.dp):
            z, y, c = i // (2 * self.ys), (i // 2) % self.ys, i % 2
            z, y, c = move(z, y, c)
            pairs.append((i, (z * self.ys + y) * 2 + c))
        return lax.ppermute(value, "dp", pairs)

    def swap_core(self, value):
        return self._dp(value, lambda z, y, c: (z, y, 1 - c))

    def send_z(self, value, s):
        return self._dp(value, lambda z, y, c: ((z + s) % self.zs, y, c))

    def send_y(self, value, f):
        return self._dp(value, lambda z, y, c: (z, (y + f) % self.ys, c))

    def send_x(self, value, g):
        pairs = [(i, (i + g) % self.n) for i in range(self.n)]
        return lax.ppermute(value, "fsdp", pairs)

    def place(self, f, s):
        return ((self.z - s) % self.zs) * self.ys + (self.y - f) % self.ys

    def chip_sum(self, value):
        bit = 2
        while bit < self.dp:
            value = value + lax.ppermute(value, "dp", [(i, i ^ bit) for i in range(self.dp)])
            bit *= 2
        return value

    def group_parts(self, value):
        near = [value] + [self.send_x(value, g) for g in range(1, self.n)]
        pieces = jnp.zeros((self.n * 2,) + value.shape, value.dtype)
        for g, here in enumerate(near):
            place = ((self.j - g) % self.n) * 2
            pieces = lax.dynamic_update_slice_in_dim(pieces, here[None], place + self.core, 0)
            there = self.swap_core(here)
            pieces = lax.dynamic_update_slice_in_dim(pieces, there[None], place + 1 - self.core, 0)
        return pieces


def gather_ring(grid, block):
    rows = block.shape[0]
    out = jnp.zeros((grid.slots * rows,) + block.shape[1:], block.dtype)
    along, crossed = [block], ()
    for s in range(grid.zs):
        piece = along[s]
        waits = crossed
        if waits:
            piece = tie(piece, *waits)
            along[s] = piece
        if s + 1 < grid.zs:
            along.append(grid.send_z(piece, 1))
        crossed = tuple(grid.send_y(piece, f) for f in range(1, grid.ys))
        for f, here in enumerate((piece,) + crossed):
            out = lax.dynamic_update_slice_in_dim(out, here, grid.place(f, s) * rows, 0)
    return along, out


def add_kernel(place_ref, *refs):
    total = refs[0][...].astype(F32)
    for ref in refs[1:-1]:
        total = total + ref[...].astype(F32)
    refs[-1][...] = total.astype(refs[-1].dtype)


def add_rows(place, value, moved, dtype):
    rows, cols = value.shape[0], value.shape[1]
    size = moved[0][2]
    step = size // 2
    spec = lambda block: pl.BlockSpec((step, cols), lambda i, _: (2 * block + i, 0))
    return pl.pallas_call(
        add_kernel,
        grid_spec=pltpu.PrefetchScalarGridSpec(
            num_scalar_prefetch=1,
            grid=(2,),
            in_specs=[pl.BlockSpec((step, cols), lambda i, at: (2 * at[0] + i, 0))]
            + [spec(block) for _, block, _ in moved],
            out_specs=pl.BlockSpec((step, cols), lambda i, _: (i, 0)),
        ),
        out_shape=jax.ShapeDtypeStruct((size, cols), dtype),
        cost_estimate=busy(MICRO),
        name="add_rows",
    )(place, value, *[array for array, _, _ in moved])


class ScatterX:
    def __init__(self, grid, value):
        self.grid, self.value = grid, value
        self.rows = value.shape[0] // grid.slots
        steps = list(range(grid.zs - 1, -1, -1))
        cut = (grid.zs + 1) // 2
        self.come = {}
        for group in (steps[:cut], steps[cut:]):
            arrived = [
                grid.send_y(
                    jnp.concatenate(
                        [
                            lax.dynamic_slice_in_dim(
                                value, grid.place(f, s) * self.rows, self.rows, 0
                            )
                            for s in group
                        ],
                        axis=0,
                    ),
                    -f,
                )
                for f in range(1, grid.ys)
            ]
            for i, s in enumerate(group):
                self.come[s] = [(array, i, self.rows) for array in arrived]
        self.sums = []

    def send(self, s, *waits):
        place = self.grid.place(0, s).astype(jnp.int32).reshape(1)
        part = add_rows(place, self.value, self.come[s], BF16 if s else F32)
        if s:
            part = self.grid.send_z(tie(part, *waits) if waits else part, -s)
        self.sums.append(part)
        return part

    def total(self):
        total = self.sums[-1].astype(F32)
        for part in self.sums[:-1]:
            total = total + part.astype(F32)
        return total


def core_groups(grid):
    return [list(range(c, grid.dp, 2)) for c in (0, 1)]


def gather_all(grid, block):
    return lax.all_gather(block, "dp", axis=0, tiled=True, axis_index_groups=core_groups(grid))


def scatter_all(grid, value):
    return lax.psum_scatter(
        value, "dp", scatter_dimension=0, tiled=True, axis_index_groups=core_groups(grid)
    )


def shift_down(value, by):
    if by == 0:
        return value
    turned = pltpu.roll(value, by, 0)
    rows = lax.broadcasted_iota(jnp.int32, (8, value.shape[1]), 0)
    return jnp.concatenate([jnp.where(rows < by, 0.0, turned[:8]), turned[8:]], axis=0)


def shift_up(value, by):
    if by == 0:
        return value
    size = value.shape[0]
    turned = pltpu.roll(value, size - by, 0)
    rows = lax.broadcasted_iota(jnp.int32, (8, value.shape[1]), 0)
    last = jnp.where(rows >= 8 - by, 0.0, turned[size - 8 :])
    return jnp.concatenate([turned[: size - 8], last], axis=0)


def convolve(joined, taps, lanes):
    shifted = [shift_down(joined, 3 - k) for k in range(4)]
    total = taps[4:5, lanes]
    for k in range(4):
        total = total + taps[k : k + 1, lanes] * shifted[k]
    return shifted, total


def head_tables(dtr, heads):
    x = dtr + heads[0:1, :]
    dt = jnp.maximum(x, 0.0) + jnp.log1p(jnp.exp(-jnp.abs(x)))
    small = x < -30.0
    log_dt = jnp.where(small, x, jnp.log(dt))
    ratio = jnp.where(small, 1.0, jax.nn.sigmoid(x) / dt)
    rate = -dt * jnp.exp(heads[1:2, :])
    return log_dt, rate, ratio


def triangle(upper):
    rows = lax.broadcasted_iota(jnp.int32, (STRETCH, STRETCH), 0)
    cols = lax.broadcasted_iota(jnp.int32, (STRETCH, STRETCH), 1)
    return jnp.where(cols >= rows if upper else cols <= rows, 1.0, 0.0).astype(F32)


def dot_high(a, b):
    return jnp.dot(a, b, precision=HIGH, preferred_element_type=F32)


def pair_lanes(low, high, width=LANES):
    lane = lax.broadcasted_iota(jnp.int32, (low.shape[0], width), 1)
    return jnp.where(lane < HEAD_DIM, low, high)


def only(value, e):
    lane = lax.broadcasted_iota(jnp.int32, value.shape, 1)
    keep = (lane < HEAD_DIM) if e == 0 else (lane >= HEAD_DIM)
    return jnp.where(keep, value, jnp.zeros_like(value))


def fwd_kernel(waits, limit_ref, xb_ref, taps_ref, heads_ref, skip_ref, *refs):
    y_ref, s1_ref, xs_ref, slope_ref = refs[waits:]
    inner = y_ref.shape[1]
    limit = limit_ref[pl.program_id(0)]
    half = STRETCH // 2
    lo, hi = slice(0, STRETCH), slice(STRETCH, 2 * STRETCH)
    bc = slice(inner, inner + 2 * LANES)
    _, conv = convolve(xb_ref[:, bc], taps_ref, bc)
    act = jax.nn.silu(conv).astype(BF16)
    bm, cm = act[:, :LANES], act[:, LANES:]
    log_dt, rate, _ = head_tables(xb_ref[:, inner + 2 * LANES :], heads_ref)
    tri = triangle(False)
    cum = jnp.concatenate([dot_high(tri, rate[lo]), dot_high(tri, rate[hi])], 0)
    late = cum - log_dt
    cum2, late2 = cum * LOG2E, late * LOG2E
    late_t = late2.T
    tail = jnp.exp(cum[STRETCH - 1 : STRETCH] - late[lo])
    ecum = jnp.exp(cum[hi])
    grams = [dot_nt(cm[b], bm[b]) for b in (lo, hi)]
    mask = lax.broadcasted_iota(jnp.int32, (half, half), 0) >= lax.broadcasted_iota(
        jnp.int32, (half, half), 1
    )
    for p in range(inner // LANES):
        lanes = slice(p * LANES, (p + 1) * LANES)
        _, conv = convolve(xb_ref[:, lanes], taps_ref, lanes)
        channel = lax.broadcasted_iota(jnp.int32, (1, LANES), 1) + p * LANES
        used = (channel < limit).astype(F32)
        sig = jax.nn.sigmoid(conv)
        act = conv * sig
        xs = (act * used).astype(BF16)
        xs_ref[:, lanes] = xs
        slope_ref[:, lanes] = ((sig + act * (1.0 - sig)) * used).astype(BF16)
        h = 2 * p
        weights = pair_lanes(tail[:, h : h + 1], tail[:, h + 1 : h + 2])
        weighted = (xs[lo].astype(F32) * weights).astype(BF16)
        state = dot_tn(weighted, bm[lo]).astype(BF16)
        s1_ref[lanes, :] = state
        for b, gram in zip((lo, hi), grams):
            tops, lows = [], []
            xe = [only(xs[b], e) for e in (0, 1)]
            base = b.start
            for e in (0, 1):
                col = cum2[b, h + e : h + e + 1]
                row = late_t[h + e : h + e + 1, b]
                top = jnp.exp2(jnp.where(mask, col[:half] - row[:, :half], NEG))
                low0 = jnp.exp2(col[half:] - row[:, :half])
                low1 = jnp.exp2(jnp.where(mask, col[half:] - row[:, half:], NEG))
                tops.append((gram[:half, :half] * top).astype(BF16))
                lows.append((gram[half:, :half] * low0).astype(BF16))
                lows.append((gram[half:, half:] * low1).astype(BF16))
            y0 = dot_nn(
                jnp.concatenate(tops, 1), jnp.concatenate([xe[0][:half], xe[1][:half]], 0)
            )
            y1 = dot_nn(jnp.concatenate(lows, 1), jnp.concatenate(xe, 0))
            if base:
                inter = dot_nt(cm[b], state)
                inter = inter * pair_lanes(ecum[:, h : h + 1], ecum[:, h + 1 : h + 2])
                y0, y1 = y0 + inter[:half], y1 + inter[half:]
            skip = skip_ref[0:1, lanes] * xs[b].astype(F32)
            y_ref[pl.ds(base, half), lanes] = y0 + skip[:half]
            y_ref[pl.ds(base + half, half), lanes] = y1 + skip[half:]


def lane_sum(value, e):
    return jnp.sum(only(value, e), axis=1, keepdims=True)


def bwd_kernel(extra, xb_ref, y_ref, dy_ref, s1_ref, xs_ref, slope_ref, taps_ref, *refs):
    heads_ref, skip_ref = refs[:2]
    dxb_ref, gch_ref, gh_ref, dg_ref, rs_ref = refs[2 + extra :]
    inner = y_ref.shape[1]
    q = pl.program_id(0)
    half = STRETCH // 2
    lo, hi = slice(0, STRETCH), slice(STRETCH, 2 * STRETCH)
    bc = slice(inner, inner + 2 * LANES)

    @pl.when(q == 0)
    def _():
        gch_ref[...] = jnp.zeros_like(gch_ref)
        gh_ref[...] = jnp.zeros_like(gh_ref)

    dg_ref[...] = jnp.zeros_like(dg_ref)
    rs_ref[...] = jnp.zeros_like(rs_ref)
    _, conv_bc = convolve(xb_ref[:, bc], taps_ref, bc)
    sig_bc = jax.nn.sigmoid(conv_bc)
    act = (conv_bc * sig_bc).astype(BF16)
    bm, cm = act[:, :LANES], act[:, LANES:]
    log_dt, rate, ratio = head_tables(xb_ref[:, inner + 2 * LANES :], heads_ref)
    tri = triangle(False)
    cum = jnp.concatenate([dot_high(tri, rate[lo]), dot_high(tri, rate[hi])], 0)
    late = cum - log_dt
    late2 = late * LOG2E
    cum_t = (cum * LOG2E).T
    tail = jnp.exp(cum[STRETCH - 1 : STRETCH] - late[lo])
    ecum = jnp.exp(cum[hi])
    grams = [dot_nt(bm[b], cm[b]) for b in (lo, hi)]
    mask = lax.broadcasted_iota(jnp.int32, (half, half), 1) >= lax.broadcasted_iota(
        jnp.int32, (half, half), 0
    )
    d_bm0 = jnp.zeros((STRETCH, LANES), F32)
    d_cm1 = jnp.zeros((STRETCH, LANES), F32)
    d_tail = jnp.zeros((1, LANES), F32)
    lane_of = lax.broadcasted_iota(jnp.int32, (1, LANES), 1)

    def conv_back(d_conv, lanes):
        joined = xb_ref[:, lanes]
        rows, total = [], None
        for k in range(4):
            moved = shift_up(d_conv, 3 - k)
            rows.append(jnp.sum(moved * joined, axis=0, keepdims=True))
            part = taps_ref[k : k + 1, lanes] * moved
            total = part if total is None else total + part
        rows.append(jnp.sum(d_conv, axis=0, keepdims=True))
        dxb_ref[:, lanes] = total.astype(BF16)
        return rows

    for p in range(inner // LANES):
        lanes = slice(p * LANES, (p + 1) * LANES)
        h = 2 * p
        xs = xs_ref[:, lanes]
        xf = xs.astype(F32)
        dy = dy_ref[:, lanes]
        dyf = dy.astype(F32)
        skip = skip_ref[0:1, lanes]
        d_prior = (dyf[hi] * pair_lanes(ecum[:, h : h + 1], ecum[:, h + 1 : h + 2])).astype(BF16)
        d_state = dot_tn(d_prior, cm[hi]).astype(BF16)
        weights = pair_lanes(tail[:, h : h + 1], tail[:, h + 1 : h + 2])
        weighted = (xf[lo] * weights).astype(BF16)
        d_from_state = dot_nt(bm[lo], d_state) * weights
        d_bm0 = d_bm0 + dot_nn(weighted, d_state)
        d_cm1 = d_cm1 + dot_nn(d_prior, s1_ref[lanes, :])
        columns = []
        for i, (b, gram) in enumerate(zip((lo, hi), grams)):
            tops, lows = [], []
            dye = [only(dy[b], e) for e in (0, 1)]
            for e in (0, 1):
                col = late2[b, h + e : h + e + 1]
                row = cum_t[h + e : h + e + 1, b]
                top0 = jnp.exp2(jnp.where(mask, row[:, :half] - col[:half], NEG))
                top1 = jnp.exp2(row[:, half:] - col[:half])
                low = jnp.exp2(jnp.where(mask, row[:, half:] - col[half:], NEG))
                xe = only(xs[b], e)
                d_top = dot_nt(xe[:half], dy[b])
                d_low = dot_nt(xe[half:], dy[b][half:])
                tops.append((gram[:half, :half] * top0).astype(BF16))
                tops.append((gram[:half, half:] * top1).astype(BF16))
                lows.append((gram[half:, half:] * low).astype(BF16))
                dg_ref[i, :half, :half] += d_top[:, :half] * top0
                dg_ref[i, :half, half:] += d_top[:, half:] * top1
                dg_ref[i, half:, half:] += d_low * low
            d0 = dot_nn(jnp.concatenate(tops, 1), jnp.concatenate(dye, 0))
            d1 = dot_nn(
                jnp.concatenate(lows, 1), jnp.concatenate([dye[0][half:], dye[1][half:]], 0)
            )
            columns += [d0, d1]
        d_x = jnp.concatenate(columns, 0)
        d_x = jnp.concatenate([d_x[lo] + d_from_state, d_x[hi]], 0)
        from_x = xf * d_x
        from_y = dyf * (y_ref[:, lanes] - skip * xf)
        state_sum = jnp.sum(xf[lo] * d_from_state, axis=0, keepdims=True)
        for e in (0, 1):
            at = slice(h + e, h + e + 1)
            rs_ref[0, :, at] = lane_sum(from_x, e)
            rs_ref[1, :, at] = lane_sum(from_y, e)
            d_tail = jnp.where(lane_of == h + e, lane_sum(state_sum, e), d_tail)
        d_conv = (d_x + skip * dyf) * slope_ref[:, lanes].astype(F32)
        rows = conv_back(d_conv, lanes)
        rows.append(jnp.sum(dyf * xf, axis=0, keepdims=True))
        for r, row in enumerate(rows):
            gch_ref[r : r + 1, lanes] += row

    d_bm, d_cm = [], []
    for i, b in enumerate((lo, hi)):
        d_gram = dg_ref[i].astype(BF16)
        d_bm.append(dot_nn(d_gram, cm[b]))
        d_cm.append(dot_tn(d_gram, bm[b]))
    d_bm[0] = d_bm[0] + d_bm0
    d_cm[1] = d_cm[1] + d_cm1
    d_act = jnp.concatenate([jnp.concatenate(d_bm, 0), jnp.concatenate(d_cm, 0)], 1)
    rows = conv_back(d_act * (sig_bc * (1.0 + conv_bc * (1.0 - sig_bc))), bc)
    for r, row in enumerate(rows):
        gch_ref[r : r + 1, bc] += row

    from_x, from_y = rs_ref[0], rs_ref[1]
    d_cum = from_y - from_x
    row_of = lax.broadcasted_iota(jnp.int32, (STRETCH, 1), 0)
    first = d_cum[lo] + jnp.where(row_of == STRETCH - 1, d_tail, 0.0)
    tri_t = triangle(True)
    d_rate = jnp.concatenate([dot_high(tri_t, first), dot_high(tri_t, d_cum[hi])], 0)
    flow = rate * d_rate
    d_dt = (from_x + flow) * ratio
    dxb_ref[:, inner + 2 * LANES :] = d_dt.astype(BF16)
    gh_ref[0:1, :] += jnp.sum(d_dt, axis=0, keepdims=True)
    gh_ref[1:2, :] += jnp.sum(flow, axis=0, keepdims=True)


def run_fwd(limits, xb, taps, heads, skip, slot, waits=()):
    rows, cols = xb.shape
    inner = cols - 3 * LANES
    seqs = rows // slot
    whole = lambda shape: pl.BlockSpec(shape, lambda q, *_: (0,) * len(shape))
    per = lambda width: pl.BlockSpec((slot, width), lambda q, *_: (q, 0))
    return pl.pallas_call(
        functools.partial(fwd_kernel, len(waits)),
        grid_spec=pltpu.PrefetchScalarGridSpec(
            num_scalar_prefetch=1,
            grid=(seqs,),
            in_specs=[per(cols), whole(taps.shape), whole(heads.shape), whole(skip.shape)]
            + [pl.BlockSpec(memory_space=pl.ANY)] * len(waits),
            out_specs=[
                per(inner),
                pl.BlockSpec((inner, LANES), lambda q, *_: (q, 0)),
                per(inner),
                per(inner),
            ],
        ),
        out_shape=[
            jax.ShapeDtypeStruct((rows, inner), F32),
            jax.ShapeDtypeStruct((seqs * inner, LANES), BF16),
            jax.ShapeDtypeStruct((rows, inner), BF16),
            jax.ShapeDtypeStruct((rows, inner), BF16),
        ],
        cost_estimate=busy(25 * MICRO),
        name="scan_forward",
    )(limits, xb, taps, heads, skip, *waits)


def tie_kernel(*refs):
    pass


def tie(value, *waits):
    return pl.pallas_call(
        tie_kernel,
        in_specs=[pl.BlockSpec(memory_space=pl.ANY)] * (1 + len(waits)),
        out_specs=pl.BlockSpec(memory_space=pl.ANY),
        out_shape=jax.ShapeDtypeStruct(value.shape, value.dtype),
        input_output_aliases={0: 0},
        name="order",
    )(value, *waits)


def run_bwd(xb, y, dy, s1, xs, slope, taps, heads, skip, slot, first, count, d_xb=None, waits=()):
    rows, cols = xb.shape
    inner = cols - 3 * LANES
    whole = lambda shape: pl.BlockSpec(shape, lambda q: (0,) * len(shape))
    per = lambda width: pl.BlockSpec((slot, width), lambda q: (q + first, 0))
    aliased = d_xb is not None
    kernel = functools.partial(bwd_kernel, aliased + len(waits))
    return pl.pallas_call(
        kernel,
        grid_spec=pl.GridSpec(
            grid=(count,),
            in_specs=[
                per(cols),
                per(inner),
                per(inner),
                pl.BlockSpec((inner, LANES), lambda q: (q + first, 0)),
                per(inner),
                per(inner),
                whole(taps.shape),
                whole(heads.shape),
                whole(skip.shape),
            ]
            + [pl.BlockSpec(memory_space=pl.ANY)] * (aliased + len(waits)),
            out_specs=[per(cols), whole((8, cols)), whole((8, LANES))],
            scratch_shapes=[
                pltpu.VMEM((2, STRETCH, STRETCH), F32),
                pltpu.VMEM((2, 2 * STRETCH, LANES), F32),
            ],
        ),
        out_shape=[
            jax.ShapeDtypeStruct((rows, cols), BF16),
            jax.ShapeDtypeStruct((8, cols), F32),
            jax.ShapeDtypeStruct((8, LANES), F32),
        ],
        input_output_aliases={9: 0} if aliased else {},
        cost_estimate=busy(4 * count * MICRO),
        name="scan_backward",
    )(xb, y, dy, s1, xs, slope, taps, heads, skip, *([d_xb] if aliased else []), *waits)


def prepare_kernel(length_ref, u_ref, cot_ref, gain_ref, *refs):
    normed_ref, branch_ref = refs[-2:]
    rows, _ = u_ref.shape
    u = u_ref[...].astype(F32)
    rstd = lax.rsqrt(jnp.mean(u * u, axis=-1, keepdims=True) + 1e-05)
    row = lax.broadcasted_iota(jnp.int32, (rows, 1), 0) + pl.program_id(0) * rows
    valid = row < length_ref[0]
    normed_ref[...] = (u * rstd * gain_ref[...]).astype(BF16)
    branch_ref[...] = jnp.where(valid, cot_ref[...].astype(F32), 0.0).astype(BF16)


def run_prepare(lengths, tokens, cotangent, gain, waits):
    slot, width = tokens.shape
    step = slot // 4
    per = pl.BlockSpec((step, width), lambda i, *_: (i, 0))
    return pl.pallas_call(
        prepare_kernel,
        grid_spec=pltpu.PrefetchScalarGridSpec(
            num_scalar_prefetch=1,
            grid=(4,),
            in_specs=[per, per, pl.BlockSpec((1, width), lambda i, *_: (0, 0))]
            + [pl.BlockSpec(memory_space=pl.ANY)] * len(waits),
            out_specs=[per, per],
        ),
        out_shape=[jax.ShapeDtypeStruct((slot, width), BF16)] * 2,
        cost_estimate=busy(5 * MICRO),
        name="prepare_rows",
    )(lengths, tokens, cotangent, gain, *waits)


def back_kernel(waits, dz_ref, dxb_ref, wz_ref, wx_ref, normed_ref, *refs):
    refs = refs[waits:]
    part = dot_nt(dz_ref[...], wz_ref[...]) + dot_nt(dxb_ref[...], wx_ref[...])
    slot = refs[0].shape[0]
    for i, ref in enumerate(refs[:-1]):
        ref[...] = part[i * slot : (i + 1) * slot].astype(BF16)
    product = part * normed_ref[...].astype(F32)
    refs[-1][...] = jnp.sum(product.reshape(-1, 8, product.shape[1]), axis=0)


def run_back(dz, dxb, wz, wx, normed, slot, first, waits=()):
    width, inner = wz.shape
    cols = wx.shape[1]
    step = 256
    rows = 2 * slot
    block = first // 2
    tall = lambda size: pl.BlockSpec((rows, size), lambda i: (block, 0))
    return pl.pallas_call(
        functools.partial(back_kernel, len(waits)),
        grid=(width // step,),
        in_specs=[
            tall(inner),
            tall(cols),
            pl.BlockSpec((step, inner), lambda i: (i, 0)),
            pl.BlockSpec((step, cols), lambda i: (i, 0)),
            pl.BlockSpec((rows, step), lambda i: (block, i)),
        ]
        + [pl.BlockSpec(memory_space=pl.ANY)] * len(waits),
        out_specs=[pl.BlockSpec((slot, step), lambda i: (0, i))] * 2
        + [pl.BlockSpec((8, step), lambda i: (0, i))],
        out_shape=[jax.ShapeDtypeStruct((slot, width), BF16)] * 2
        + [jax.ShapeDtypeStruct((8, width), F32)],
        cost_estimate=busy(0),
        name="normed_gradient",
    )(dz, dxb, wz, wx, normed, *waits)


def branch_kernel(waits, gnorm_ref, wo_ref, *refs):
    refs = refs[waits:]
    part = dot_nt(gnorm_ref[...], wo_ref[...])
    slot = refs[0].shape[0]
    for i, ref in enumerate(refs):
        ref[...] = part[i * slot : (i + 1) * slot].astype(BF16)


def run_branch(gnorm, wo, slot, first, waits=()):
    width, inner = wo.shape
    step = 256
    block = first // 2
    return pl.pallas_call(
        functools.partial(branch_kernel, len(waits)),
        grid=(width // step,),
        in_specs=[
            pl.BlockSpec((2 * slot, inner), lambda i: (block, 0)),
            pl.BlockSpec((step, inner), lambda i: (i, 0)),
        ]
        + [pl.BlockSpec(memory_space=pl.ANY)] * len(waits),
        out_specs=[pl.BlockSpec((slot, step), lambda i: (0, i))] * 2,
        out_shape=[jax.ShapeDtypeStruct((slot, width), BF16)] * 2,
        cost_estimate=busy(0),
        name="branch_rows",
    )(gnorm, wo, *waits)


def output_kernel(count, length_ref, u_ref, *refs):
    parts, out_ref = refs[:count], refs[count]
    rows, _ = u_ref.shape
    row = lax.broadcasted_iota(jnp.int32, (rows, 1), 0) + pl.program_id(0) * rows
    total = parts[0][...].astype(F32)
    for part in parts[1:]:
        total = total + part[...].astype(F32)
    total = jnp.where(row < length_ref[0], total, 0.0)
    out_ref[...] = (u_ref[...].astype(F32) + total).astype(BF16)


def grad_kernel(count, u_ref, cot_ref, gain_ref, *refs):
    parts, out_ref = refs[:count], refs[count]
    u = u_ref[...].astype(F32)
    rstd = lax.rsqrt(jnp.mean(u * u, axis=-1, keepdims=True) + 1e-05)
    total = parts[0][...].astype(F32)
    for part in parts[1:]:
        total = total + part[...].astype(F32)
    total = total * gain_ref[...]
    back = jnp.mean(total * u, axis=-1, keepdims=True)
    grad = total * rstd - u * (rstd * rstd * rstd * back)
    out_ref[...] = (cot_ref[...].astype(F32) + grad).astype(BF16)


def run_output(lengths, tokens, parts):
    slot, width = tokens.shape
    step = slot // 4
    per = pl.BlockSpec((step, width), lambda i, *_: (i, 0))
    return pl.pallas_call(
        functools.partial(output_kernel, len(parts)),
        grid_spec=pltpu.PrefetchScalarGridSpec(
            num_scalar_prefetch=1,
            grid=(4,),
            in_specs=[per] * (1 + len(parts)),
            out_specs=per,
        ),
        out_shape=jax.ShapeDtypeStruct((slot, width), BF16),
        cost_estimate=busy(5 * MICRO),
        name="layer_output",
    )(lengths, tokens, *parts)


def run_grad(tokens, cotangent, gain, parts):
    slot, width = tokens.shape
    step = slot // 8
    per = pl.BlockSpec((step, width), lambda i: (i, 0))
    return pl.pallas_call(
        functools.partial(grad_kernel, len(parts)),
        grid=(8,),
        in_specs=[per, per, pl.BlockSpec((1, width), lambda i: (0, 0))] + [per] * len(parts),
        out_specs=per,
        out_shape=jax.ShapeDtypeStruct((slot, width), BF16),
        cost_estimate=busy(8 * MICRO),
        name="input_gradient",
    )(tokens, cotangent, gain, *parts)


def per_device(
    tokens,
    cotangent,
    lengths,
    widths,
    norm_gain,
    w_zx,
    w_bc,
    w_dt,
    w_out,
    conv_w,
    conv_b,
    dt_bias,
    a_log,
    d_skip,
    gate_gain,
):
    grid = Grid()
    core, j, n = grid.core, grid.j, grid.n
    slot, width = tokens.shape
    assert lengths.shape[0] == 1 and slot == 2 * STRETCH
    rows_d = w_zx.shape[0]
    inner = w_zx.shape[2] // 2
    heads = w_dt.shape[1] // 2
    state2 = w_bc.shape[1]
    total = conv_w.shape[1]
    all_inner = total - state2
    part = j * 2 + core
    channel_base = part * inner
    head_base = part * heads
    cols = inner + 3 * LANES
    spare = cols - inner - state2 - heads

    def halves(value, axis):
        size = value.shape[axis] // 2
        mine = lax.dynamic_slice_in_dim(value, core * size, size, axis)
        other = lax.dynamic_slice_in_dim(value, (1 - core) * size, size, axis)
        return mine, other

    def by_core(mine, other, axis):
        first = jnp.where(core == 0, mine, other)
        second = jnp.where(core == 0, other, mine)
        return jnp.concatenate([first, second], axis=axis)

    def swapped(mine, other, *waits):
        return by_core(mine, grid.swap_core(tie(other, *waits) if waits else other), 0)

    fill = jnp.zeros((rows_d, spare), BF16)
    x_mine, x_other = halves(w_zx[:, 1], 1)
    t_mine, t_other = halves(w_dt, 1)
    x_mine = jnp.concatenate([x_mine, w_bc, t_mine, fill], axis=1)
    x_other = jnp.concatenate([x_other, w_bc, t_other, fill], axis=1)
    block_x = swapped(x_mine, x_other)
    gain_row = norm_gain[None]
    normed_own, d_branch_own = run_prepare(
        lengths, tokens, cotangent, gain_row, (x_other,)
    )
    z_mine, z_other = halves(w_zx[:, 0], 1)
    block_z = swapped(z_mine, z_other, normed_own)
    o_mine, o_other = halves(w_out.T, 1)
    block_o = swapped(o_mine, o_other, normed_own)
    arriving = [grid.send_x(normed_own, g) for g in range(1, n)]
    along, w_x = gather_ring(grid, block_x)
    arriving = [tie(value, along[-1]) for value in arriving]
    w_z = gather_all(grid, tie(block_z, along[1]))
    w_o = gather_all(grid, block_o)

    order = [(g, e) for g in range(n - 1, -1, -1) for e in (1, 0)]
    index = lax.axis_index("dp")
    owners = [(index + e * (1 - 2 * core)) * n + (j - g) % n for g, e in order]

    def share(value, arriving):
        near = [value] + arriving
        far = [grid.swap_core(piece) for piece in near]
        pieces = [far[g] if e else near[g] for g, e in order]
        return lax.optimization_barrier(jnp.concatenate(pieces, axis=0))

    normed = share(normed_own, arriving)
    crossing = [grid.send_x(d_branch_own, g) for g in range(1, n)]
    seqs = len(owners)
    seq_width = jnp.stack([widths[o] for o in owners])
    used = seq_width * ((HEADS // 8) * HEAD_DIM)
    counts = jnp.repeat(used.astype(F32), slot)
    limits = jnp.clip(used - channel_base, 0, inner).astype(jnp.int32)

    taps = jnp.concatenate(
        [
            lax.dynamic_slice_in_dim(conv_w, channel_base, inner, 1),
            conv_w[:, all_inner:],
        ],
        axis=1,
    )
    bias = jnp.concatenate(
        [lax.dynamic_slice_in_dim(conv_b, channel_base, inner, 0), conv_b[all_inner:]]
    )
    taps = jnp.pad(jnp.concatenate([taps, bias[None]], 0), ((0, 3), (0, LANES)))
    own_heads = lambda v: lax.dynamic_slice_in_dim(v, head_base, heads, 0)
    head_rows = jnp.pad(
        jnp.stack([own_heads(dt_bias), own_heads(a_log)]), ((0, 6), (0, LANES - heads))
    )
    skip = jnp.broadcast_to(jnp.repeat(own_heads(d_skip), HEAD_DIM)[None], (8, inner))
    own_gain = lax.dynamic_slice_in_dim(gate_gain, channel_base, inner, 0)

    rows_of = lambda value, i: value[i * slot : (i + 1) * slot]
    xb = dot_nn(normed, w_x)
    scan = (taps, head_rows, skip, slot)
    d_branch = share(d_branch_own, [tie(value, xb) for value in crossing])
    y, s1, xs, slope = run_fwd(limits, xb, *scan)
    z = dot_nn(normed, w_z)
    sig = jax.nn.sigmoid(z)
    held = lambda value: lax.optimization_barrier(value.astype(BF16)).astype(F32)
    gated = y * (z * sig)

    def group_sum(rows):
        rows = rows.reshape(n, 2, slot)
        rows = rows + grid.swap_core(rows)[:, ::-1]
        total = rows
        for g in range(1, n):
            total = total + jnp.roll(grid.send_x(rows, g), -g, axis=0)
        return total.reshape(seqs * slot)

    scale = lax.rsqrt(group_sum(jnp.sum(gated * gated, axis=1)) / counts + 1e-05)
    gnorm = (gated * scale[:, None] * own_gain).astype(BF16)

    g_o_part = dot_tn(d_branch, gnorm).astype(BF16)
    g_o = scatter_all(grid, g_o_part)
    w_o = tie(w_o, g_o_part)
    d_gnorm = dot_nn(d_branch, w_o)
    weighted = d_gnorm * own_gain
    inner_part = jnp.sum(weighted * gated, axis=1)
    far = seqs - 2
    out_far = [run_branch(gnorm, w_o, slot, i, (inner_part,)) for i in range(0, far, 2)]
    inner_sum = group_sum(inner_part)
    if out_far:
        inner_sum = tie(inner_sum, *[rows for pair in out_far for rows in pair])
    pull = scale * scale * scale / counts * inner_sum
    d_gated = held(weighted) * scale[:, None] - gated * pull[:, None]
    z = held(z)
    sig = jax.nn.sigmoid(z)
    g_gate = jnp.sum(d_gnorm * gated * scale[:, None], axis=0)
    silu = z * sig
    d_y = (d_gated * silu).astype(BF16)
    d_z = (d_gated * y * (sig * (1.0 + z * (1.0 - sig)))).astype(BF16)
    g_z_part = dot_tn(normed, d_z).astype(BF16)
    g_z = scatter_all(grid, g_z_part)

    cross = lambda values: [
        grid.send_x(value, -order[2 * i][0]) for i, value in enumerate(values)
    ]
    d_normed, branch, g_norm_part = [], [], 0.0
    for out_there, out_here in out_far:
        out_there = grid.swap_core(out_there)
        branch.append((out_here.astype(F32) + out_there.astype(F32)).astype(BF16))
    d_xb, g_channels, g_heads = run_bwd(
        xb, y, d_y, s1, xs, slope, *scan, 0, far, None, (g_o_part, g_z_part, *branch)
    )
    branch = cross(branch)
    for i in range(0, far, 2):
        there, here, more = run_back(d_z, d_xb, w_z, w_x, normed, slot, i)
        g_norm_part = g_norm_part + more
        there = grid.swap_core(tie(there, *branch))
        d_normed.append((here.astype(F32) + there.astype(F32)).astype(BF16))
    d_xb, more_channels, more_heads = run_bwd(
        xb, y, d_y, s1, xs, slope, *scan, far, 2, d_xb, (*d_normed, g_o)
    )
    d_normed = cross(d_normed)
    g_channels, g_heads = g_channels + more_channels, g_heads + more_heads
    g_skip = g_channels[5, :inner].reshape(heads, HEAD_DIM).sum(axis=1)
    mine = jnp.concatenate(
        [
            g_channels[:5].reshape(-1),
            g_gate,
            jnp.pad(jnp.concatenate([g_heads[0, :heads], g_heads[1, :heads], g_skip]), (0, -3 * heads % LANES)),
        ]
    )
    g_x_part = dot_tn(normed, d_xb).astype(BF16)
    to_x = ScatterX(grid, g_x_part)
    there, here, more = run_back(
        d_z, d_xb, w_z, w_x, normed, slot, far, (g_x_part,)
    )
    d_normed += [here, grid.swap_core(there)]
    out_there, out_here = run_branch(gnorm, w_o, slot, far, (here,))
    out_there = grid.swap_core(tie(out_there, *d_normed[: far // 2]))

    def to_rows(value):
        rows = lax.dynamic_slice_in_dim(value, core * rows_d, rows_d, 0)
        other = lax.dynamic_slice_in_dim(value, (1 - core) * rows_d, rows_d, 0)
        return rows, grid.swap_core(other)

    o_rows = by_core(*to_rows(g_o.astype(F32)), 1).T
    z_rows = by_core(*to_rows(g_z.astype(F32)), 1)
    third = to_x.send(3, out_here, g_z)
    to_x.send(2, out_here)
    to_x.send(1)
    to_x.send(0)
    g_x = to_x.total()
    small = mine.shape[0]
    mine = jnp.concatenate([mine, jnp.sum(g_norm_part + more, axis=0)])
    mine = jnp.pad(mine, (0, -mine.shape[0] % 1024)).reshape(-1, LANES)
    mine = grid.chip_sum(tie(mine, third, o_rows, z_rows))
    branch += [out_here, out_there]

    output = run_output(lengths, tokens, branch)
    input_grad = run_grad(tokens, cotangent, gain_row, d_normed)

    x_mine, x_recv = to_rows(g_x)
    x_rows = by_core(x_mine[:, :inner], x_recv[:, :inner], 1)
    t_rows = by_core(x_mine[:, inner + state2 : cols - spare], x_recv[:, inner + state2 : cols - spare], 1)
    bc_rows = (x_mine + x_recv)[:, inner : inner + state2]
    bc_sum = bc_rows
    for g in range(1, n):
        bc_sum = bc_sum + grid.send_x(bc_rows, g)
    g_w_zx = jnp.stack([z_rows, x_rows], axis=1)

    mine = grid.group_parts(mine).reshape(2 * n, -1)
    conv = mine[:, : 5 * cols].reshape(2 * n, 5, cols)
    conv_x = jnp.swapaxes(conv[:, :, :inner], 0, 1).reshape(5, all_inner)
    conv_bc = jnp.sum(conv[:, :, inner : inner + state2], axis=0)
    g_conv = jnp.concatenate([conv_x, conv_bc], axis=1)
    g_gate = mine[:, 5 * cols : 5 * cols + inner].reshape(all_inner)
    g_small = mine[:, 5 * cols + inner : 5 * cols + inner + 3 * heads].reshape(2 * n, 3, heads)
    g_small = jnp.swapaxes(g_small, 0, 1).reshape(3, -1)
    g_norm = jnp.sum(mine[:, small : small + width], axis=0) / norm_gain
    return (
        output,
        input_grad,
        g_norm,
        g_w_zx,
        bc_sum,
        t_rows,
        o_rows,
        g_conv[:4],
        g_conv[4],
        g_small[0],
        g_small[1],
        g_small[2],
        g_gate,
    )


def solution(mesh):
    in_specs = (
        P(("dp", "fsdp"), None),
        P(("dp", "fsdp"), None),
        P(("dp", "fsdp")),
        P(),
        P(),
        P("dp", None, "fsdp"),
        P("dp", None),
        P("dp", "fsdp"),
        P("fsdp", "dp"),
        P(),
        P(),
        P(),
        P(),
        P(),
        P(),
    )
    out_specs = (
        P(("dp", "fsdp"), None),
        P(("dp", "fsdp"), None),
        P(),
        P("dp", None, "fsdp"),
        P("dp", None),
        P("dp", "fsdp"),
        P("fsdp", "dp"),
        P(),
        P(),
        P(),
        P(),
        P(),
        P(),
    )
    return jax.shard_map(
        per_device, mesh=mesh, in_specs=in_specs, out_specs=out_specs, check_vma=False
    )
```

```python
import functools

import jax
import jax.numpy as jnp
from jax import lax
from jax.experimental import pallas as pl
from jax.experimental.pallas import tpu as pltpu
from jax.sharding import PartitionSpec as P

HEADS = 64
HEAD_DIM = 64
STRETCH = 256
LANES = 128
F32 = jnp.float32
BF16 = jnp.bfloat16
NEG = -1e30
HIGH = lax.Precision.HIGHEST
MICRO = 10**9
LOG2E = 1.4426950408889634


def busy(flops, scale=1.0):
    return pl.CostEstimate(flops=int(flops * scale), transcendentals=0, bytes_accessed=0)


def dot_nn(a, b):
    return lax.dot_general(a, b, (((1,), (0,)), ((), ())), preferred_element_type=F32)


def dot_nt(a, b):
    return lax.dot_general(a, b, (((1,), (1,)), ((), ())), preferred_element_type=F32)


def dot_tn(a, b):
    return lax.dot_general(a, b, (((0,), (0,)), ((), ())), preferred_element_type=F32)


class Grid:
    def __init__(self):
        self.dp = lax.axis_size("dp")
        self.n = lax.axis_size("fsdp")
        chips = self.dp // 2
        self.zs = 4 if chips % 4 == 0 else 1
        self.ys = chips // self.zs
        index = lax.axis_index("dp")
        self.core = index % 2
        self.chip = index // 2
        self.z = self.chip // self.ys
        self.y = self.chip % self.ys
        self.j = lax.axis_index("fsdp")
        self.slots = self.zs * self.ys

    def _dp(self, value, move):
        pairs = []
        for i in range(self.dp):
            z, y, c = i // (2 * self.ys), (i // 2) % self.ys, i % 2
            z, y, c = move(z, y, c)
            pairs.append((i, (z * self.ys + y) * 2 + c))
        return lax.ppermute(value, "dp", pairs)

    def swap_core(self, value):
        return self._dp(value, lambda z, y, c: (z, y, 1 - c))

    def send_z(self, value, s):
        return self._dp(value, lambda z, y, c: ((z + s) % self.zs, y, c))

    def send_y(self, value, f):
        return self._dp(value, lambda z, y, c: (z, (y + f) % self.ys, c))

    def send_x(self, value, g):
        pairs = [(i, (i + g) % self.n) for i in range(self.n)]
        return lax.ppermute(value, "fsdp", pairs)

    def place(self, f, s):
        return ((self.z - s) % self.zs) * self.ys + (self.y - f) % self.ys

    def chip_sum(self, value):
        bit = 2
        while bit < self.dp:
            value = value + lax.ppermute(value, "dp", [(i, i ^ bit) for i in range(self.dp)])
            bit *= 2
        return value

    def group_parts(self, value):
        near = [value] + [self.send_x(value, g) for g in range(1, self.n)]
        pieces = jnp.zeros((self.n * 2,) + value.shape, value.dtype)
        for g, here in enumerate(near):
            place = ((self.j - g) % self.n) * 2
            pieces = lax.dynamic_update_slice_in_dim(pieces, here[None], place + self.core, 0)
            there = self.swap_core(here)
            pieces = lax.dynamic_update_slice_in_dim(pieces, there[None], place + 1 - self.core, 0)
        return pieces


def gather_ring(grid, block):
    rows = block.shape[0]
    out = jnp.zeros((grid.slots * rows,) + block.shape[1:], block.dtype)
    along, crossed = [block], ()
    for s in range(grid.zs):
        piece = along[s]
        waits = crossed
        if waits:
            piece = tie(piece, *waits)
            along[s] = piece
        if s + 1 < grid.zs:
            along.append(grid.send_z(piece, 1))
        crossed = tuple(grid.send_y(piece, f) for f in range(1, grid.ys))
        for f, here in enumerate((piece,) + crossed):
            out = lax.dynamic_update_slice_in_dim(out, here, grid.place(f, s) * rows, 0)
    return along, out


def add_kernel(place_ref, *refs):
    total = refs[0][...].astype(F32)
    for ref in refs[1:-1]:
        total = total + ref[...].astype(F32)
    refs[-1][...] = total.astype(refs[-1].dtype)


def add_rows(place, value, moved, dtype):
    rows, cols = value.shape[0], value.shape[1]
    size = moved[0][2]
    step = size // 2
    spec = lambda block: pl.BlockSpec((step, cols), lambda i, _: (2 * block + i, 0))
    return pl.pallas_call(
        add_kernel,
        grid_spec=pltpu.PrefetchScalarGridSpec(
            num_scalar_prefetch=1,
            grid=(2,),
            in_specs=[pl.BlockSpec((step, cols), lambda i, at: (2 * at[0] + i, 0))]
            + [spec(block) for _, block, _ in moved],
            out_specs=pl.BlockSpec((step, cols), lambda i, _: (i, 0)),
        ),
        out_shape=jax.ShapeDtypeStruct((size, cols), dtype),
        cost_estimate=busy(MICRO),
        name="add_rows",
    )(place, value, *[array for array, _, _ in moved])


class ScatterX:
    def __init__(self, grid, value):
        self.grid, self.value = grid, value
        self.rows = value.shape[0] // grid.slots
        steps = list(range(grid.zs - 1, -1, -1))
        cut = (grid.zs + 1) // 2
        self.come = {}
        for group in (steps[:cut], steps[cut:]):
            arrived = [
                grid.send_y(
                    jnp.concatenate(
                        [
                            lax.dynamic_slice_in_dim(
                                value, grid.place(f, s) * self.rows, self.rows, 0
                            )
                            for s in group
                        ],
                        axis=0,
                    ),
                    -f,
                )
                for f in range(1, grid.ys)
            ]
            for i, s in enumerate(group):
                self.come[s] = [(array, i, self.rows) for array in arrived]
        self.sums = []

    def send(self, s, *waits):
        place = self.grid.place(0, s).astype(jnp.int32).reshape(1)
        part = add_rows(place, self.value, self.come[s], BF16 if s else F32)
        if s:
            part = self.grid.send_z(tie(part, *waits) if waits else part, -s)
        self.sums.append(part)
        return part

    def total(self):
        total = self.sums[-1].astype(F32)
        for part in self.sums[:-1]:
            total = total + part.astype(F32)
        return total


def core_groups(grid):
    return [list(range(c, grid.dp, 2)) for c in (0, 1)]


def gather_all(grid, block):
    return lax.all_gather(block, "dp", axis=0, tiled=True, axis_index_groups=core_groups(grid))


def scatter_all(grid, value):
    return lax.psum_scatter(
        value, "dp", scatter_dimension=0, tiled=True, axis_index_groups=core_groups(grid)
    )


def shift_down(value, by):
    if by == 0:
        return value
    turned = pltpu.roll(value, by, 0)
    rows = lax.broadcasted_iota(jnp.int32, (8, value.shape[1]), 0)
    return jnp.concatenate([jnp.where(rows < by, 0.0, turned[:8]), turned[8:]], axis=0)


def shift_up(value, by):
    if by == 0:
        return value
    size = value.shape[0]
    turned = pltpu.roll(value, size - by, 0)
    rows = lax.broadcasted_iota(jnp.int32, (8, value.shape[1]), 0)
    last = jnp.where(rows >= 8 - by, 0.0, turned[size - 8 :])
    return jnp.concatenate([turned[: size - 8], last], axis=0)


def convolve(joined, taps, lanes):
    shifted = [shift_down(joined, 3 - k) for k in range(4)]
    total = taps[4:5, lanes]
    for k in range(4):
        total = total + taps[k : k + 1, lanes] * shifted[k]
    return shifted, total


def head_tables(dtr, heads):
    x = dtr + heads[0:1, :]
    dt = jnp.maximum(x, 0.0) + jnp.log1p(jnp.exp(-jnp.abs(x)))
    small = x < -30.0
    log_dt = jnp.where(small, x, jnp.log(dt))
    ratio = jnp.where(small, 1.0, jax.nn.sigmoid(x) / dt)
    rate = -dt * jnp.exp(heads[1:2, :])
    return log_dt, rate, ratio


def triangle(upper):
    rows = lax.broadcasted_iota(jnp.int32, (STRETCH, STRETCH), 0)
    cols = lax.broadcasted_iota(jnp.int32, (STRETCH, STRETCH), 1)
    return jnp.where(cols >= rows if upper else cols <= rows, 1.0, 0.0).astype(F32)


def dot_high(a, b):
    return jnp.dot(a, b, precision=HIGH, preferred_element_type=F32)


def pair_lanes(low, high, width=LANES):
    lane = lax.broadcasted_iota(jnp.int32, (low.shape[0], width), 1)
    return jnp.where(lane < HEAD_DIM, low, high)


def only(value, e):
    lane = lax.broadcasted_iota(jnp.int32, value.shape, 1)
    keep = (lane < HEAD_DIM) if e == 0 else (lane >= HEAD_DIM)
    return jnp.where(keep, value, jnp.zeros_like(value))


def fwd_kernel(waits, limit_ref, xb_ref, taps_ref, heads_ref, skip_ref, *refs):
    y_ref, s1_ref, xs_ref, slope_ref = refs[waits:]
    inner = y_ref.shape[1]
    limit = limit_ref[pl.program_id(0)]
    half = STRETCH // 2
    lo, hi = slice(0, STRETCH), slice(STRETCH, 2 * STRETCH)
    bc = slice(inner, inner + 2 * LANES)
    _, conv = convolve(xb_ref[:, bc], taps_ref, bc)
    act = jax.nn.silu(conv).astype(BF16)
    bm, cm = act[:, :LANES], act[:, LANES:]
    log_dt, rate, _ = head_tables(xb_ref[:, inner + 2 * LANES :], heads_ref)
    tri = triangle(False)
    cum = jnp.concatenate([dot_high(tri, rate[lo]), dot_high(tri, rate[hi])], 0)
    late = cum - log_dt
    cum2, late2 = cum * LOG2E, late * LOG2E
    late_t = late2.T
    tail = jnp.exp(cum[STRETCH - 1 : STRETCH] - late[lo])
    ecum = jnp.exp(cum[hi])
    grams = [dot_nt(cm[b], bm[b]) for b in (lo, hi)]
    mask = lax.broadcasted_iota(jnp.int32, (half, half), 0) >= lax.broadcasted_iota(
        jnp.int32, (half, half), 1
    )
    for p in range(inner // LANES):
        lanes = slice(p * LANES, (p + 1) * LANES)
        _, conv = convolve(xb_ref[:, lanes], taps_ref, lanes)
        channel = lax.broadcasted_iota(jnp.int32, (1, LANES), 1) + p * LANES
        used = (channel < limit).astype(F32)
        sig = jax.nn.sigmoid(conv)
        act = conv * sig
        xs = (act * used).astype(BF16)
        xs_ref[:, lanes] = xs
        slope_ref[:, lanes] = ((sig + act * (1.0 - sig)) * used).astype(BF16)
        h = 2 * p
        weights = pair_lanes(tail[:, h : h + 1], tail[:, h + 1 : h + 2])
        weighted = (xs[lo].astype(F32) * weights).astype(BF16)
        state = dot_tn(weighted, bm[lo]).astype(BF16)
        s1_ref[lanes, :] = state
        for b, gram in zip((lo, hi), grams):
            tops, lows = [], []
            xe = [only(xs[b], e) for e in (0, 1)]
            base = b.start
            for e in (0, 1):
                col = cum2[b, h + e : h + e + 1]
                row = late_t[h + e : h + e + 1, b]
                top = jnp.exp2(jnp.where(mask, col[:half] - row[:, :half], NEG))
                low0 = jnp.exp2(col[half:] - row[:, :half])
                low1 = jnp.exp2(jnp.where(mask, col[half:] - row[:, half:], NEG))
                tops.append((gram[:half, :half] * top).astype(BF16))
                lows.append((gram[half:, :half] * low0).astype(BF16))
                lows.append((gram[half:, half:] * low1).astype(BF16))
            y0 = dot_nn(
                jnp.concatenate(tops, 1), jnp.concatenate([xe[0][:half], xe[1][:half]], 0)
            )
            y1 = dot_nn(jnp.concatenate(lows, 1), jnp.concatenate(xe, 0))
            if base:
                inter = dot_nt(cm[b], state)
                inter = inter * pair_lanes(ecum[:, h : h + 1], ecum[:, h + 1 : h + 2])
                y0, y1 = y0 + inter[:half], y1 + inter[half:]
            skip = skip_ref[0:1, lanes] * xs[b].astype(F32)
            y_ref[pl.ds(base, half), lanes] = y0 + skip[:half]
            y_ref[pl.ds(base + half, half), lanes] = y1 + skip[half:]


def lane_sum(value, e):
    return jnp.sum(only(value, e), axis=1, keepdims=True)


def bwd_kernel(extra, xb_ref, y_ref, dy_ref, s1_ref, xs_ref, slope_ref, taps_ref, *refs):
    heads_ref, skip_ref = refs[:2]
    dxb_ref, gch_ref, gh_ref, dg_ref, rs_ref = refs[2 + extra :]
    inner = y_ref.shape[1]
    q = pl.program_id(0)
    half = STRETCH // 2
    lo, hi = slice(0, STRETCH), slice(STRETCH, 2 * STRETCH)
    bc = slice(inner, inner + 2 * LANES)

    @pl.when(q == 0)
    def _():
        gch_ref[...] = jnp.zeros_like(gch_ref)
        gh_ref[...] = jnp.zeros_like(gh_ref)

    dg_ref[...] = jnp.zeros_like(dg_ref)
    rs_ref[...] = jnp.zeros_like(rs_ref)
    _, conv_bc = convolve(xb_ref[:, bc], taps_ref, bc)
    sig_bc = jax.nn.sigmoid(conv_bc)
    act = (conv_bc * sig_bc).astype(BF16)
    bm, cm = act[:, :LANES], act[:, LANES:]
    log_dt, rate, ratio = head_tables(xb_ref[:, inner + 2 * LANES :], heads_ref)
    tri = triangle(False)
    cum = jnp.concatenate([dot_high(tri, rate[lo]), dot_high(tri, rate[hi])], 0)
    late = cum - log_dt
    late2 = late * LOG2E
    cum_t = (cum * LOG2E).T
    tail = jnp.exp(cum[STRETCH - 1 : STRETCH] - late[lo])
    ecum = jnp.exp(cum[hi])
    grams = [dot_nt(bm[b], cm[b]) for b in (lo, hi)]
    mask = lax.broadcasted_iota(jnp.int32, (half, half), 1) >= lax.broadcasted_iota(
        jnp.int32, (half, half), 0
    )
    d_bm0 = jnp.zeros((STRETCH, LANES), F32)
    d_cm1 = jnp.zeros((STRETCH, LANES), F32)
    d_tail = jnp.zeros((1, LANES), F32)
    lane_of = lax.broadcasted_iota(jnp.int32, (1, LANES), 1)

    def conv_back(d_conv, lanes):
        joined = xb_ref[:, lanes]
        rows, total = [], None
        for k in range(4):
            moved = shift_up(d_conv, 3 - k)
            rows.append(jnp.sum(moved * joined, axis=0, keepdims=True))
            part = taps_ref[k : k + 1, lanes] * moved
            total = part if total is None else total + part
        rows.append(jnp.sum(d_conv, axis=0, keepdims=True))
        dxb_ref[:, lanes] = total.astype(BF16)
        return rows

    for p in range(inner // LANES):
        lanes = slice(p * LANES, (p + 1) * LANES)
        h = 2 * p
        xs = xs_ref[:, lanes]
        xf = xs.astype(F32)
        dy = dy_ref[:, lanes]
        dyf = dy.astype(F32)
        skip = skip_ref[0:1, lanes]
        d_prior = (dyf[hi] * pair_lanes(ecum[:, h : h + 1], ecum[:, h + 1 : h + 2])).astype(BF16)
        d_state = dot_tn(d_prior, cm[hi]).astype(BF16)
        weights = pair_lanes(tail[:, h : h + 1], tail[:, h + 1 : h + 2])
        weighted = (xf[lo] * weights).astype(BF16)
        d_from_state = dot_nt(bm[lo], d_state) * weights
        d_bm0 = d_bm0 + dot_nn(weighted, d_state)
        d_cm1 = d_cm1 + dot_nn(d_prior, s1_ref[lanes, :])
        columns = []
        for i, (b, gram) in enumerate(zip((lo, hi), grams)):
            tops, lows = [], []
            dye = [only(dy[b], e) for e in (0, 1)]
            for e in (0, 1):
                col = late2[b, h + e : h + e + 1]
                row = cum_t[h + e : h + e + 1, b]
                top0 = jnp.exp2(jnp.where(mask, row[:, :half] - col[:half], NEG))
                top1 = jnp.exp2(row[:, half:] - col[:half])
                low = jnp.exp2(jnp.where(mask, row[:, half:] - col[half:], NEG))
                xe = only(xs[b], e)
                d_top = dot_nt(xe[:half], dy[b])
                d_low = dot_nt(xe[half:], dy[b][half:])
                tops.append((gram[:half, :half] * top0).astype(BF16))
                tops.append((gram[:half, half:] * top1).astype(BF16))
                lows.append((gram[half:, half:] * low).astype(BF16))
                dg_ref[i, :half, :half] += d_top[:, :half] * top0
                dg_ref[i, :half, half:] += d_top[:, half:] * top1
                dg_ref[i, half:, half:] += d_low * low
            d0 = dot_nn(jnp.concatenate(tops, 1), jnp.concatenate(dye, 0))
            d1 = dot_nn(
                jnp.concatenate(lows, 1), jnp.concatenate([dye[0][half:], dye[1][half:]], 0)
            )
            columns += [d0, d1]
        d_x = jnp.concatenate(columns, 0)
        d_x = jnp.concatenate([d_x[lo] + d_from_state, d_x[hi]], 0)
        from_x = xf * d_x
        from_y = dyf * (y_ref[:, lanes] - skip * xf)
        state_sum = jnp.sum(xf[lo] * d_from_state, axis=0, keepdims=True)
        for e in (0, 1):
            at = slice(h + e, h + e + 1)
            rs_ref[0, :, at] = lane_sum(from_x, e)
            rs_ref[1, :, at] = lane_sum(from_y, e)
            d_tail = jnp.where(lane_of == h + e, lane_sum(state_sum, e), d_tail)
        d_conv = (d_x + skip * dyf) * slope_ref[:, lanes].astype(F32)
        rows = conv_back(d_conv, lanes)
        rows.append(jnp.sum(dyf * xf, axis=0, keepdims=True))
        for r, row in enumerate(rows):
            gch_ref[r : r + 1, lanes] += row

    d_bm, d_cm = [], []
    for i, b in enumerate((lo, hi)):
        d_gram = dg_ref[i].astype(BF16)
        d_bm.append(dot_nn(d_gram, cm[b]))
        d_cm.append(dot_tn(d_gram, bm[b]))
    d_bm[0] = d_bm[0] + d_bm0
    d_cm[1] = d_cm[1] + d_cm1
    d_act = jnp.concatenate([jnp.concatenate(d_bm, 0), jnp.concatenate(d_cm, 0)], 1)
    rows = conv_back(d_act * (sig_bc * (1.0 + conv_bc * (1.0 - sig_bc))), bc)
    for r, row in enumerate(rows):
        gch_ref[r : r + 1, bc] += row

    from_x, from_y = rs_ref[0], rs_ref[1]
    d_cum = from_y - from_x
    row_of = lax.broadcasted_iota(jnp.int32, (STRETCH, 1), 0)
    first = d_cum[lo] + jnp.where(row_of == STRETCH - 1, d_tail, 0.0)
    tri_t = triangle(True)
    d_rate = jnp.concatenate([dot_high(tri_t, first), dot_high(tri_t, d_cum[hi])], 0)
    flow = rate * d_rate
    d_dt = (from_x + flow) * ratio
    dxb_ref[:, inner + 2 * LANES :] = d_dt.astype(BF16)
    gh_ref[0:1, :] += jnp.sum(d_dt, axis=0, keepdims=True)
    gh_ref[1:2, :] += jnp.sum(flow, axis=0, keepdims=True)


def run_fwd(limits, xb, taps, heads, skip, slot, waits=()):
    rows, cols = xb.shape
    inner = cols - 3 * LANES
    seqs = rows // slot
    whole = lambda shape: pl.BlockSpec(shape, lambda q, *_: (0,) * len(shape))
    per = lambda width: pl.BlockSpec((slot, width), lambda q, *_: (q, 0))
    return pl.pallas_call(
        functools.partial(fwd_kernel, len(waits)),
        grid_spec=pltpu.PrefetchScalarGridSpec(
            num_scalar_prefetch=1,
            grid=(seqs,),
            in_specs=[per(cols), whole(taps.shape), whole(heads.shape), whole(skip.shape)]
            + [pl.BlockSpec(memory_space=pl.ANY)] * len(waits),
            out_specs=[
                per(inner),
                pl.BlockSpec((inner, LANES), lambda q, *_: (q, 0)),
                per(inner),
                per(inner),
            ],
        ),
        out_shape=[
            jax.ShapeDtypeStruct((rows, inner), F32),
            jax.ShapeDtypeStruct((seqs * inner, LANES), BF16),
            jax.ShapeDtypeStruct((rows, inner), BF16),
            jax.ShapeDtypeStruct((rows, inner), BF16),
        ],
        cost_estimate=busy(25 * MICRO),
        name="scan_forward",
    )(limits, xb, taps, heads, skip, *waits)


def tie_kernel(*refs):
    pass


def tie(value, *waits):
    return pl.pallas_call(
        tie_kernel,
        in_specs=[pl.BlockSpec(memory_space=pl.ANY)] * (1 + len(waits)),
        out_specs=pl.BlockSpec(memory_space=pl.ANY),
        out_shape=jax.ShapeDtypeStruct(value.shape, value.dtype),
        input_output_aliases={0: 0},
        name="order",
    )(value, *waits)


def run_bwd(xb, y, dy, s1, xs, slope, taps, heads, skip, slot, first, count, d_xb=None, waits=()):
    rows, cols = xb.shape
    inner = cols - 3 * LANES
    whole = lambda shape: pl.BlockSpec(shape, lambda q: (0,) * len(shape))
    per = lambda width: pl.BlockSpec((slot, width), lambda q: (q + first, 0))
    aliased = d_xb is not None
    kernel = functools.partial(bwd_kernel, aliased + len(waits))
    return pl.pallas_call(
        kernel,
        grid_spec=pl.GridSpec(
            grid=(count,),
            in_specs=[
                per(cols),
                per(inner),
                per(inner),
                pl.BlockSpec((inner, LANES), lambda q: (q + first, 0)),
                per(inner),
                per(inner),
                whole(taps.shape),
                whole(heads.shape),
                whole(skip.shape),
            ]
            + [pl.BlockSpec(memory_space=pl.ANY)] * (aliased + len(waits)),
            out_specs=[per(cols), whole((8, cols)), whole((8, LANES))],
            scratch_shapes=[
                pltpu.VMEM((2, STRETCH, STRETCH), F32),
                pltpu.VMEM((2, 2 * STRETCH, LANES), F32),
            ],
        ),
        out_shape=[
            jax.ShapeDtypeStruct((rows, cols), BF16),
            jax.ShapeDtypeStruct((8, cols), F32),
            jax.ShapeDtypeStruct((8, LANES), F32),
        ],
        input_output_aliases={9: 0} if aliased else {},
        cost_estimate=busy(4 * count * MICRO),
        name="scan_backward",
    )(xb, y, dy, s1, xs, slope, taps, heads, skip, *([d_xb] if aliased else []), *waits)


def prepare_kernel(length_ref, u_ref, cot_ref, gain_ref, *refs):
    normed_ref, branch_ref = refs[-2:]
    rows, _ = u_ref.shape
    u = u_ref[...].astype(F32)
    rstd = lax.rsqrt(jnp.mean(u * u, axis=-1, keepdims=True) + 1e-05)
    row = lax.broadcasted_iota(jnp.int32, (rows, 1), 0) + pl.program_id(0) * rows
    valid = row < length_ref[0]
    normed_ref[...] = (u * rstd * gain_ref[...]).astype(BF16)
    branch_ref[...] = jnp.where(valid, cot_ref[...].astype(F32), 0.0).astype(BF16)


def run_prepare(lengths, tokens, cotangent, gain, waits):
    slot, width = tokens.shape
    step = slot // 4
    per = pl.BlockSpec((step, width), lambda i, *_: (i, 0))
    return pl.pallas_call(
        prepare_kernel,
        grid_spec=pltpu.PrefetchScalarGridSpec(
            num_scalar_prefetch=1,
            grid=(4,),
            in_specs=[per, per, pl.BlockSpec((1, width), lambda i, *_: (0, 0))]
            + [pl.BlockSpec(memory_space=pl.ANY)] * len(waits),
            out_specs=[per, per],
        ),
        out_shape=[jax.ShapeDtypeStruct((slot, width), BF16)] * 2,
        cost_estimate=busy(5 * MICRO),
        name="prepare_rows",
    )(lengths, tokens, cotangent, gain, *waits)


def back_kernel(waits, dz_ref, dxb_ref, wz_ref, wx_ref, normed_ref, *refs):
    refs = refs[waits:]
    part = dot_nt(dz_ref[...], wz_ref[...]) + dot_nt(dxb_ref[...], wx_ref[...])
    slot = refs[0].shape[0]
    for i, ref in enumerate(refs[:-1]):
        ref[...] = part[i * slot : (i + 1) * slot].astype(BF16)
    product = part * normed_ref[...].astype(F32)
    refs[-1][...] = jnp.sum(product.reshape(-1, 8, product.shape[1]), axis=0)


def run_back(dz, dxb, wz, wx, normed, slot, first, waits=()):
    width, inner = wz.shape
    cols = wx.shape[1]
    step = 256
    rows = 2 * slot
    block = first // 2
    tall = lambda size: pl.BlockSpec((rows, size), lambda i: (block, 0))
    return pl.pallas_call(
        functools.partial(back_kernel, len(waits)),
        grid=(width // step,),
        in_specs=[
            tall(inner),
            tall(cols),
            pl.BlockSpec((step, inner), lambda i: (i, 0)),
            pl.BlockSpec((step, cols), lambda i: (i, 0)),
            pl.BlockSpec((rows, step), lambda i: (block, i)),
        ]
        + [pl.BlockSpec(memory_space=pl.ANY)] * len(waits),
        out_specs=[pl.BlockSpec((slot, step), lambda i: (0, i))] * 2
        + [pl.BlockSpec((8, step), lambda i: (0, i))],
        out_shape=[jax.ShapeDtypeStruct((slot, width), BF16)] * 2
        + [jax.ShapeDtypeStruct((8, width), F32)],
        cost_estimate=busy(0),
        name="normed_gradient",
    )(dz, dxb, wz, wx, normed, *waits)


def branch_kernel(waits, gnorm_ref, wo_ref, *refs):
    refs = refs[waits:]
    part = dot_nt(gnorm_ref[...], wo_ref[...])
    slot = refs[0].shape[0]
    for i, ref in enumerate(refs):
        ref[...] = part[i * slot : (i + 1) * slot].astype(BF16)


def run_branch(gnorm, wo, slot, first, waits=()):
    width, inner = wo.shape
    step = 256
    block = first // 2
    return pl.pallas_call(
        functools.partial(branch_kernel, len(waits)),
        grid=(width // step,),
        in_specs=[
            pl.BlockSpec((2 * slot, inner), lambda i: (block, 0)),
            pl.BlockSpec((step, inner), lambda i: (i, 0)),
        ]
        + [pl.BlockSpec(memory_space=pl.ANY)] * len(waits),
        out_specs=[pl.BlockSpec((slot, step), lambda i: (0, i))] * 2,
        out_shape=[jax.ShapeDtypeStruct((slot, width), BF16)] * 2,
        cost_estimate=busy(0),
        name="branch_rows",
    )(gnorm, wo, *waits)


def output_kernel(count, length_ref, u_ref, *refs):
    parts, out_ref = refs[:count], refs[count]
    rows, _ = u_ref.shape
    row = lax.broadcasted_iota(jnp.int32, (rows, 1), 0) + pl.program_id(0) * rows
    total = parts[0][...].astype(F32)
    for part in parts[1:]:
        total = total + part[...].astype(F32)
    total = jnp.where(row < length_ref[0], total, 0.0)
    out_ref[...] = (u_ref[...].astype(F32) + total).astype(BF16)


def grad_kernel(count, u_ref, cot_ref, gain_ref, *refs):
    parts, out_ref = refs[:count], refs[count]
    u = u_ref[...].astype(F32)
    rstd = lax.rsqrt(jnp.mean(u * u, axis=-1, keepdims=True) + 1e-05)
    total = parts[0][...].astype(F32)
    for part in parts[1:]:
        total = total + part[...].astype(F32)
    total = total * gain_ref[...]
    back = jnp.mean(total * u, axis=-1, keepdims=True)
    grad = total * rstd - u * (rstd * rstd * rstd * back)
    out_ref[...] = (cot_ref[...].astype(F32) + grad).astype(BF16)


def run_output(lengths, tokens, parts):
    slot, width = tokens.shape
    step = slot // 4
    per = pl.BlockSpec((step, width), lambda i, *_: (i, 0))
    return pl.pallas_call(
        functools.partial(output_kernel, len(parts)),
        grid_spec=pltpu.PrefetchScalarGridSpec(
            num_scalar_prefetch=1,
            grid=(4,),
            in_specs=[per] * (1 + len(parts)),
            out_specs=per,
        ),
        out_shape=jax.ShapeDtypeStruct((slot, width), BF16),
        cost_estimate=busy(5 * MICRO),
        name="layer_output",
    )(lengths, tokens, *parts)


def run_grad(tokens, cotangent, gain, parts):
    slot, width = tokens.shape
    step = slot // 8
    per = pl.BlockSpec((step, width), lambda i: (i, 0))
    return pl.pallas_call(
        functools.partial(grad_kernel, len(parts)),
        grid=(8,),
        in_specs=[per, per, pl.BlockSpec((1, width), lambda i: (0, 0))] + [per] * len(parts),
        out_specs=per,
        out_shape=jax.ShapeDtypeStruct((slot, width), BF16),
        cost_estimate=busy(8 * MICRO),
        name="input_gradient",
    )(tokens, cotangent, gain, *parts)


def per_device(
    tokens,
    cotangent,
    lengths,
    widths,
    norm_gain,
    w_zx,
    w_bc,
    w_dt,
    w_out,
    conv_w,
    conv_b,
    dt_bias,
    a_log,
    d_skip,
    gate_gain,
):
    grid = Grid()
    core, j, n = grid.core, grid.j, grid.n
    slot, width = tokens.shape
    assert lengths.shape[0] == 1 and slot == 2 * STRETCH
    rows_d = w_zx.shape[0]
    inner = w_zx.shape[2] // 2
    heads = w_dt.shape[1] // 2
    state2 = w_bc.shape[1]
    total = conv_w.shape[1]
    all_inner = total - state2
    part = j * 2 + core
    channel_base = part * inner
    head_base = part * heads
    cols = inner + 3 * LANES
    spare = cols - inner - state2 - heads

    def halves(value, axis):
        size = value.shape[axis] // 2
        mine = lax.dynamic_slice_in_dim(value, core * size, size, axis)
        other = lax.dynamic_slice_in_dim(value, (1 - core) * size, size, axis)
        return mine, other

    def by_core(mine, other, axis):
        first = jnp.where(core == 0, mine, other)
        second = jnp.where(core == 0, other, mine)
        return jnp.concatenate([first, second], axis=axis)

    def swapped(mine, other, *waits):
        return by_core(mine, grid.swap_core(tie(other, *waits) if waits else other), 0)

    fill = jnp.zeros((rows_d, spare), BF16)
    x_mine, x_other = halves(w_zx[:, 1], 1)
    t_mine, t_other = halves(w_dt, 1)
    x_mine = jnp.concatenate([x_mine, w_bc, t_mine, fill], axis=1)
    x_other = jnp.concatenate([x_other, w_bc, t_other, fill], axis=1)
    block_x = swapped(x_mine, x_other)
    gain_row = norm_gain[None]
    normed_own, d_branch_own = run_prepare(
        lengths, tokens, cotangent, gain_row, (x_other,)
    )
    z_mine, z_other = halves(w_zx[:, 0], 1)
    block_z = swapped(z_mine, z_other, normed_own)
    o_mine, o_other = halves(w_out.T, 1)
    block_o = swapped(o_mine, o_other, normed_own)
    arriving = [grid.send_x(normed_own, g) for g in range(1, n)]
    along, w_x = gather_ring(grid, block_x)
    arriving = [tie(value, along[-1]) for value in arriving]
    w_z = gather_all(grid, tie(block_z, along[1]))
    w_o = gather_all(grid, block_o)

    order = [(g, e) for g in range(n - 1, -1, -1) for e in (1, 0)]
    index = lax.axis_index("dp")
    owners = [(index + e * (1 - 2 * core)) * n + (j - g) % n for g, e in order]

    def share(value, arriving):
        near = [value] + arriving
        far = [grid.swap_core(piece) for piece in near]
        pieces = [far[g] if e else near[g] for g, e in order]
        return lax.optimization_barrier(jnp.concatenate(pieces, axis=0))

    normed = share(normed_own, arriving)
    crossing = [grid.send_x(d_branch_own, g) for g in range(1, n)]
    seqs = len(owners)
    seq_width = jnp.stack([widths[o] for o in owners])
    used = seq_width * ((HEADS // 8) * HEAD_DIM)
    counts = jnp.repeat(used.astype(F32), slot)
    limits = jnp.clip(used - channel_base, 0, inner).astype(jnp.int32)

    taps = jnp.concatenate(
        [
            lax.dynamic_slice_in_dim(conv_w, channel_base, inner, 1),
            conv_w[:, all_inner:],
        ],
        axis=1,
    )
    bias = jnp.concatenate(
        [lax.dynamic_slice_in_dim(conv_b, channel_base, inner, 0), conv_b[all_inner:]]
    )
    taps = jnp.pad(jnp.concatenate([taps, bias[None]], 0), ((0, 3), (0, LANES)))
    own_heads = lambda v: lax.dynamic_slice_in_dim(v, head_base, heads, 0)
    head_rows = jnp.pad(
        jnp.stack([own_heads(dt_bias), own_heads(a_log)]), ((0, 6), (0, LANES - heads))
    )
    skip = jnp.broadcast_to(jnp.repeat(own_heads(d_skip), HEAD_DIM)[None], (8, inner))
    own_gain = lax.dynamic_slice_in_dim(gate_gain, channel_base, inner, 0)

    rows_of = lambda value, i: value[i * slot : (i + 1) * slot]
    xb = dot_nn(normed, w_x)
    scan = (taps, head_rows, skip, slot)
    d_branch = share(d_branch_own, [tie(value, xb) for value in crossing])
    y, s1, xs, slope = run_fwd(limits, xb, *scan)
    z = dot_nn(normed, w_z)
    sig = jax.nn.sigmoid(z)
    held = lambda value: lax.optimization_barrier(value.astype(BF16)).astype(F32)
    gated = y * (z * sig)

    def group_sum(rows):
        rows = rows.reshape(n, 2, slot)
        rows = rows + grid.swap_core(rows)[:, ::-1]
        total = rows
        for g in range(1, n):
            total = total + jnp.roll(grid.send_x(rows, g), -g, axis=0)
        return total.reshape(seqs * slot)

    scale = lax.rsqrt(group_sum(jnp.sum(gated * gated, axis=1)) / counts + 1e-05)
    gnorm = (gated * scale[:, None] * own_gain).astype(BF16)

    g_o_part = dot_tn(d_branch, gnorm).astype(BF16)
    g_o = scatter_all(grid, g_o_part)
    w_o = tie(w_o, g_o_part)
    d_gnorm = dot_nn(d_branch, w_o)
    weighted = d_gnorm * own_gain
    inner_part = jnp.sum(weighted * gated, axis=1)
    far = seqs - 2
    out_far = [run_branch(gnorm, w_o, slot, i, (inner_part,)) for i in range(0, far, 2)]
    inner_sum = group_sum(inner_part)
    if out_far:
        inner_sum = tie(inner_sum, *[rows for pair in out_far for rows in pair])
    pull = scale * scale * scale / counts * inner_sum
    d_gated = held(weighted) * scale[:, None] - gated * pull[:, None]
    z = held(z)
    sig = jax.nn.sigmoid(z)
    g_gate = jnp.sum(d_gnorm * gated * scale[:, None], axis=0)
    silu = z * sig
    d_y = (d_gated * silu).astype(BF16)
    d_z = (d_gated * y * (sig * (1.0 + z * (1.0 - sig)))).astype(BF16)
    g_z_part = dot_tn(normed, d_z).astype(BF16)
    g_z = scatter_all(grid, g_z_part)

    cross = lambda values: [
        grid.send_x(value, -order[2 * i][0]) for i, value in enumerate(values)
    ]
    d_normed, branch, done, g_norm_part = [], [], [], 0.0
    for out_there, out_here in out_far:
        out_there = grid.swap_core(out_there)
        branch.append((out_here.astype(F32) + out_there.astype(F32)).astype(BF16))
    d_xb, g_channels, g_heads = run_bwd(
        xb, y, d_y, s1, xs, slope, *scan, 0, far, None, (g_o_part, g_z_part, *branch)
    )
    branch = cross(branch)
    for i in range(0, far, 2):
        there, here, more = run_back(d_z, d_xb, w_z, w_x, normed, slot, i)
        g_norm_part = g_norm_part + more
        there = grid.swap_core(tie(there, *branch))
        done.append((here, there))
    d_xb, more_channels, more_heads = run_bwd(
        xb, y, d_y, s1, xs, slope, *scan, far, 2, d_xb, (*[here for here, _ in done], g_o)
    )
    for here, there in done:
        there = tie(there, g_channels + more_channels)
        d_normed.append((here.astype(F32) + there.astype(F32)).astype(BF16))
    d_normed = cross(d_normed)
    g_channels, g_heads = g_channels + more_channels, g_heads + more_heads
    g_skip = g_channels[5, :inner].reshape(heads, HEAD_DIM).sum(axis=1)
    mine = jnp.concatenate(
        [
            g_channels[:5].reshape(-1),
            g_gate,
            jnp.pad(jnp.concatenate([g_heads[0, :heads], g_heads[1, :heads], g_skip]), (0, -3 * heads % LANES)),
        ]
    )
    g_x_part = dot_tn(normed, d_xb).astype(BF16)
    to_x = ScatterX(grid, g_x_part)
    there, here, more = run_back(
        d_z, d_xb, w_z, w_x, normed, slot, far, (g_x_part,)
    )
    d_normed += [here, grid.swap_core(there)]
    out_there, out_here = run_branch(gnorm, w_o, slot, far, (here,))
    out_there = grid.swap_core(tie(out_there, *d_normed[: far // 2]))

    def to_rows(value):
        rows = lax.dynamic_slice_in_dim(value, core * rows_d, rows_d, 0)
        other = lax.dynamic_slice_in_dim(value, (1 - core) * rows_d, rows_d, 0)
        return rows, grid.swap_core(other)

    o_rows = by_core(*to_rows(g_o.astype(F32)), 1).T
    z_rows = by_core(*to_rows(g_z.astype(F32)), 1)
    third = to_x.send(3, out_here, g_z)
    to_x.send(2, out_here)
    to_x.send(1)
    to_x.send(0)
    g_x = to_x.total()
    small = mine.shape[0]
    mine = jnp.concatenate([mine, jnp.sum(g_norm_part + more, axis=0)])
    mine = jnp.pad(mine, (0, -mine.shape[0] % 1024)).reshape(-1, LANES)
    mine = grid.chip_sum(tie(mine, third, o_rows, z_rows))
    branch += [out_here, out_there]

    output = run_output(lengths, tokens, branch)
    input_grad = run_grad(tokens, cotangent, gain_row, d_normed)

    x_mine, x_recv = to_rows(g_x)
    x_rows = by_core(x_mine[:, :inner], x_recv[:, :inner], 1)
    t_rows = by_core(x_mine[:, inner + state2 : cols - spare], x_recv[:, inner + state2 : cols - spare], 1)
    bc_rows = (x_mine + x_recv)[:, inner : inner + state2]
    bc_sum = bc_rows
    for g in range(1, n):
        bc_sum = bc_sum + grid.send_x(bc_rows, g)
    g_w_zx = jnp.stack([z_rows, x_rows], axis=1)

    mine = grid.group_parts(mine).reshape(2 * n, -1)
    conv = mine[:, : 5 * cols].reshape(2 * n, 5, cols)
    conv_x = jnp.swapaxes(conv[:, :, :inner], 0, 1).reshape(5, all_inner)
    conv_bc = jnp.sum(conv[:, :, inner : inner + state2], axis=0)
    g_conv = jnp.concatenate([conv_x, conv_bc], axis=1)
    g_gate = mine[:, 5 * cols : 5 * cols + inner].reshape(all_inner)
    g_small = mine[:, 5 * cols + inner : 5 * cols + inner + 3 * heads].reshape(2 * n, 3, heads)
    g_small = jnp.swapaxes(g_small, 0, 1).reshape(3, -1)
    g_norm = jnp.sum(mine[:, small : small + width], axis=0) / norm_gain
    return (
        output,
        input_grad,
        g_norm,
        g_w_zx,
        bc_sum,
        t_rows,
        o_rows,
        g_conv[:4],
        g_conv[4],
        g_small[0],
        g_small[1],
        g_small[2],
        g_gate,
    )


def solution(mesh):
    in_specs = (
        P(("dp", "fsdp"), None),
        P(("dp", "fsdp"), None),
        P(("dp", "fsdp")),
        P(),
        P(),
        P("dp", None, "fsdp"),
        P("dp", None),
        P("dp", "fsdp"),
        P("fsdp", "dp"),
        P(),
        P(),
        P(),
        P(),
        P(),
        P(),
    )
    out_specs = (
        P(("dp", "fsdp"), None),
        P(("dp", "fsdp"), None),
        P(),
        P("dp", None, "fsdp"),
        P("dp", None),
        P("dp", "fsdp"),
        P("fsdp", "dp"),
        P(),
        P(),
        P(),
        P(),
        P(),
        P(),
    )
    return jax.shard_map(
        per_device, mesh=mesh, in_specs=in_specs, out_specs=out_specs, check_vma=False
    )
```
